32 devices in a mesh: dp: 16 (over z, x, core), rep: 2 (over y).
Axes of the slice: x: 2, y: 2, z: 4, core: 2. Of those that a mesh axis runs over, the one named last changes fastest.
Arguments:
- block_input: bfloat16 [32, 512, 512], P(('dp', 'rep')), may hold values from -6 to 6
- segment_ids: int32 [32, 512], P(('dp', 'rep')), may hold values from 0 to 3, never falling along the last dimension, each value on 1 to 256 neighbouring positions
- cotangent: bfloat16 [32, 512, 512], P(('dp', 'rep')), may hold values from -6 to 6
- master_weights: float32 [3151872], P(('dp', 'rep')), may hold values from -2 to 2
- momentum: float32 [3151872], P(('dp', 'rep')), may hold values from -4096 to 4096
- weight_average: float32 [3151872], P(('dp', 'rep')), may hold values from -2 to 2
Outputs:
- block_output: float32 [32, 512, 512], P(('dp', 'rep'))
- input_grad: float32 [32, 512, 512], P(('dp', 'rep'))
- weight_grad: float32 [3151872], P(('dp', 'rep'))
- vector_grad: float32 [4096], P(('dp', 'rep'))
- new_momentum: float32 [3151872], P(('dp', 'rep'))
- new_average: float32 [3151872], P(('dp', 'rep'))
- new_weights: float32 [3151872], P(('dp', 'rep'))
The draws below stay inside these ranges and needn't reach their ends.
Inputs may be any that keep to these rules, and one draw needn't show every extreme that they name: `segment_ids`: segment numbers never fall along a row, and every number occurs in each row.
All inputs are finite; a program needn't handle non-finite values.
Results may differ from the reference program's by a relative error of at most 0.025.
The reference program's roundings to bfloat16 on the way count: a program that leaves them out, or rounds other values in their place, can miss the bound.
Values may be sent and summed in bfloat16 or wider, within the bound.
No kernel may reach another device: no remote copies, remote signals or barrier semaphores. Data moves between devices by JAX's collectives and lax.ppermute only.
A program may use at most 128 MiB of HBM per device.

```python
import math
import jax
import jax.numpy as jnp
import numpy as np
from jax import lax

D = 512
FF = 2048
HEADS = 8
SEQ = 512
REC = 2
SEGS = 4
ROWS = 32
TOKENS = 16384
PARAMS = 3151872


def layout_draw(key):
    total = 4 * D * D + 2 * D * FF + FF + 8 * D
    index = jnp.arange(total, dtype=jnp.int32)
    noise = jnp.clip(jax.random.normal(key, (total,), jnp.float32), -4.0, 4.0)
    attn_end = 4 * D * D
    in_end = attn_end + D * FF
    out_end = in_end + FF * D
    bias_end = out_end + FF
    column = index % (4 * D)
    attn_scale = jnp.where(column < 2 * D, 1.5, jnp.where(column < 3 * D, 1.0, 4.0)) / math.sqrt(D)
    scale_all = jnp.where(index < attn_end, attn_scale, jnp.where(index < in_end, 1.0 / math.sqrt(D), jnp.where(index < out_end, math.sqrt(2.0 / FF), 0.3)))
    vector_row = (index - bias_end) // D
    is_gain = (index >= bias_end) & ((vector_row == 4) | (vector_row == 6))
    return jnp.where(is_gain, 1.0 + 0.25 * noise, scale_all * noise).astype(jnp.float32)


def draw_master_weights(key, part):
    return layout_draw(jax.random.fold_in(key, 11))


def draw_weight_average(key, part):
    return layout_draw(jax.random.fold_in(key, 23))


def block_scale(rng, extent, cuts, least, largest):
    def one(position, blocks):
        draws = jax.random.uniform(jax.random.fold_in(jax.random.fold_in(rng, 6), position), (blocks,), jnp.float32, least / len(cuts), largest / len(cuts))
        return jnp.repeat(jnp.exp(draws), extent[position] // blocks).reshape((-1,) + (1,) * (len(extent) - position - 1))

    level = one(*cuts[0])
    for cut in cuts[1:]:
        level = level * one(*cut)
    return level


def profile(count, total, most, skew):
    weights = [(1 << 20) // math.isqrt(standing ** skew) + 1 for standing in range(2, count + 1)]
    rest, counts = total - most - (count - 1), [1] * (count - 1)
    while rest > 0:
        free = [i for i in range(count - 1) if counts[i] < most]
        whole, remaining = sum([weights[i] for i in free]), rest
        for i in free:
            more = min(most - counts[i], max(1, remaining * weights[i] // whole), rest)
            counts[i] = counts[i] + more
            rest = rest - more
    return np.array([most] + counts)


def ragged(rng, count, total, limit, lean):
    if count == 2:
        one = jax.random.randint(rng, (), max(1, total - limit), min(limit, total - 1) + 1)
        return jnp.stack([one, total - one])
    lengths = jnp.asarray(profile(count, total, limit, lean), jnp.int32)
    couples = (count - 1) // 2
    giver, sink = lengths[1:1 + 2 * couples:2], lengths[2:2 + 2 * couples:2]
    room = jnp.minimum(giver - 1, limit - sink)
    passed = jax.random.randint(jax.random.fold_in(rng, 1), (couples,), 0, 1 << 20) % (room + 1)
    lengths = lengths.at[1:1 + 2 * couples:2].set(giver - passed).at[2:2 + 2 * couples:2].set(sink + passed)
    return lengths[jax.random.permutation(jax.random.fold_in(rng, 2), count)]


def gaussian(rng, dims, scale, most, pieces=(), held_as=jnp.bfloat16):
    entries = scale * jax.random.normal(rng, dims, jnp.float32)
    if pieces:
        entries = entries * block_scale(rng, dims, pieces, -0.22, 0.18)
    return jnp.clip(entries, -most, most).astype(held_as)


def setup_inputs(seed: int = 0) -> dict:
    splits = jax.random.split(jax.random.key(seed), 7)
    return {
        "block_input": gaussian(splits[0], (ROWS, SEQ, D), 1.0, 6.0, ((0, 32),)),
        "segment_ids": jax.vmap(lambda own: jnp.searchsorted(jnp.cumsum(ragged(own, SEGS, SEQ, SEQ // 2, 2)), jnp.arange(SEQ), side="right"))(jax.random.split(splits[1], ROWS)).reshape((ROWS, SEQ)).astype(jnp.int32),
        "cotangent": gaussian(splits[2], (ROWS, SEQ, D), 1.0, 6.0, ((0, 32),)),
        "master_weights": draw_master_weights(jax.random.fold_in(splits[6], 71), 0),
        "momentum": gaussian(splits[4], (PARAMS,), (6 * TOKENS ** 0.5), 4096.0, ((0, 32),), jnp.float32),
        "weight_average": draw_weight_average(jax.random.fold_in(splits[6], 71), 0),
    }


@jax.custom_vjp
def low(v):
    return lax.optimization_barrier(v.astype(jnp.bfloat16)).astype(jnp.float32)

@jax.custom_vjp
def low_back(v):
    return v

def low_keep(v):
    return (low(v), None)

def low_pass(kept, grad):
    return (grad,)

def back_keep(v):
    return (v, None)

def back_low(kept, grad):
    return (low(grad),)
low.defvjp(low_keep, low_pass)
low_back.defvjp(back_keep, back_low)
norm_eps = 1e-05
mom_decay = 0.9
avg_keep = 0.8
rate_base = 0.006

def matmul(left, right):
    return jnp.matmul(left, right, precision=lax.Precision.HIGHEST)

def unpack(flat_vec):
    offset = 4 * D * D
    attn_weight = flat_vec[:offset].reshape(D, 4 * D)
    w_in = flat_vec[offset:offset + D * FF].reshape(D, FF)
    offset = offset + D * FF
    w_out = flat_vec[offset:offset + FF * D].reshape(FF, D)
    offset = offset + FF * D
    bias_in = flat_vec[offset:offset + FF]
    offset = offset + FF
    vectors = flat_vec[offset:offset + 8 * D].reshape(8, D)
    return (attn_weight, w_in, w_out, bias_in, vectors)

def layer_norm(resid, gain, shift):
    center = resid - lax.optimization_barrier(jnp.mean(resid, axis=-1, keepdims=True))
    variance = lax.optimization_barrier(jnp.mean(center * center, axis=-1, keepdims=True))
    return center * lax.rsqrt(variance + norm_eps) * gain + shift

def layer(inputs, segments, weights):
    attn_weight, w_in, w_out, bias_in, vectors = weights
    batch, length, width = inputs.shape
    head_dim = width // HEADS
    projected = matmul(low(inputs), attn_weight[:, :3 * width])
    queries = low_back(low(projected[..., :width] + vectors[0]))
    keys = low_back(low(projected[..., width:2 * width]))
    values = low_back(low(projected[..., 2 * width:] + vectors[1]))

    def split_heads(tensor):
        return tensor.reshape(batch, length, HEADS, head_dim)
    scores = jnp.einsum('bqhd,bkhd->bhqk', split_heads(queries), split_heads(keys), precision=lax.Precision.HIGHEST) * (1.0 / math.sqrt(head_dim))
    scores = low_back(scores)
    allowed = (segments[:, :, None] == segments[:, None, :])[:, None]
    probs = low(jax.nn.softmax(jnp.where(allowed, scores, -1e+30), axis=-1))
    context = jnp.einsum('bhqk,bkhd->bqhd', probs, split_heads(values), precision=lax.Precision.HIGHEST).reshape(batch, length, width)
    context = low_back(low(context))
    attended = low_back(matmul(context, attn_weight[:, 3 * width:]) + vectors[2])
    first = layer_norm(inputs + attended, vectors[4], vectors[5])
    pre_act = low_back(matmul(low(first), w_in) + bias_in)
    hidden = low_back(low(jax.nn.gelu(pre_act, approximate=True)))
    branch = low_back(matmul(hidden, w_out) + vectors[3])
    return layer_norm(first + branch, vectors[6], vectors[7])

def forward(inputs, flat_weight, segment_ids):
    weights = unpack(low(flat_weight))
    group = math.gcd(ROWS, max(1, 4096 // SEQ))
    seg_groups = segment_ids.reshape(ROWS // group, group, SEQ)

    def one_group(pair):
        block, seg_block = pair
        return layer(block, seg_block, weights)
    checked = jax.checkpoint(one_group)
    state = inputs
    for layer_index in range(REC):
        grouped = state.reshape(ROWS // group, group, SEQ, D)
        state = lax.map(checked, (grouped, seg_groups)).reshape(ROWS, SEQ, D)
    return state

def reference(block_input, segment_ids, cotangent, master_weights, momentum, weight_average):
    inputs = block_input.astype(jnp.float32)

    def run(first_in, flat_weight):
        return forward(first_in, flat_weight, segment_ids)
    block_output, pullback = jax.vjp(run, inputs, master_weights)
    input_grad, weight_grad = pullback(cotangent.astype(jnp.float32))
    vector_grad = weight_grad[PARAMS - 8 * D:]
    rate = rate_base / math.sqrt(TOKENS)
    new_momentum = mom_decay * momentum + weight_grad
    new_weights = master_weights - rate * (weight_grad + mom_decay * new_momentum)
    new_average = avg_keep * weight_average + (1.0 - avg_keep) * new_weights
    return (block_output, input_grad, weight_grad, vector_grad, new_momentum, new_average, new_weights)
```

```python
import functools
import math

import jax
import jax.numpy as jnp
from jax import lax
from jax.experimental import pallas as pl
from jax.experimental.pallas import tpu as pltpu
from jax.sharding import PartitionSpec as P

FF = 2048
HEADS = 8
REC = 2
TILE = 16
LANES = 128

norm_eps = 1e-05
mom_decay = 0.9
avg_keep = 0.8
rate_base = 0.006

BF = jnp.bfloat16
F32 = jnp.float32


def dot(a, b):
    return lax.dot_general(a, b, (((1,), (0,)), ((), ())), preferred_element_type=F32)


def dot_t(a, b):
    return lax.dot_general(a, b, (((1,), (1,)), ((), ())), preferred_element_type=F32)


def t_dot(a, b):
    return lax.dot_general(a, b, (((0,), (0,)), ((), ())), preferred_element_type=F32)


def one_hot_swap(outer, inner):
    size = outer * inner
    row = lax.broadcasted_iota(jnp.int32, (size, size), 0)
    col = lax.broadcasted_iota(jnp.int32, (size, size), 1)
    shift = inner.bit_length() - 1
    want = (row & (inner - 1)) * outer + (row >> shift)
    return jnp.where(col == want, 1.0, 0.0).astype(F32).astype(BF)


def unpack_weights(flat, wa, wi, wo, b1, vec, width):
    per = 4 * width // LANES
    swap = one_hot_swap(per, 256 // per)
    groups = width * per // 512

    def wide(dst, base):
        def body(g, carry):
            first = flat[pl.ds(pl.multiple_of(base + g * 512, 256), 256), :]
            second = flat[pl.ds(pl.multiple_of(base + g * 512 + 256, 256), 256), :]
            out = dot(swap, jnp.concatenate([first, second], axis=1)).astype(BF)
            n = 256 // per
            for c in range(per):
                piece = out[c * n : (c + 1) * n]
                dst[pl.ds(pl.multiple_of(g * 2 * n, n), n), c * LANES : (c + 1) * LANES] = piece[:, :LANES]
                dst[pl.ds(pl.multiple_of(g * 2 * n + n, n), n), c * LANES : (c + 1) * LANES] = piece[:, LANES:]
            return carry

        lax.fori_loop(0, groups, body, 0, unroll=2)

    wide(wa, 0)
    wide(wi, width * per)
    per_out = width // LANES
    swap_out = one_hot_swap(per_out, 256 // per_out)
    base = 2 * width * per

    def narrow(g, carry):
        first = flat[pl.ds(pl.multiple_of(base + g * 512, 256), 256), :]
        second = flat[pl.ds(pl.multiple_of(base + g * 512 + 256, 256), 256), :]
        out = dot(swap_out, jnp.concatenate([first, second], axis=1)).astype(BF)
        n = 256 // per_out
        for c in range(per_out):
            piece = out[c * n : (c + 1) * n]
            wo[pl.ds(pl.multiple_of(g * 2 * n, n), n), c * LANES : (c + 1) * LANES] = piece[:, :LANES]
            wo[pl.ds(pl.multiple_of(g * 2 * n + n, n), n), c * LANES : (c + 1) * LANES] = piece[:, LANES:]
        return carry

    lax.fori_loop(0, FF * per_out // 512, narrow, 0, unroll=2)
    base = base + FF * per_out
    tail = flat[base : base + FF // LANES + 8 * per_out, :].astype(F32)
    for c in range(FF // LANES):
        b1[0:1, c * LANES : (c + 1) * LANES] = tail[c : c + 1]
    for r in range(8):
        for c in range(per_out):
            k = FF // LANES + r * per_out + c
            vec[r : r + 1, c * LANES : (c + 1) * LANES] = tail[k : k + 1]


def norm_stats(resid):
    center = resid - jnp.mean(resid, axis=-1, keepdims=True)
    variance = jnp.mean(center * center, axis=-1, keepdims=True)
    inv = lax.rsqrt(variance + norm_eps)
    return center * inv, inv


def norm_grad(upstream, normed, inv, gain):
    scaled = upstream * gain
    m0 = jnp.mean(scaled, axis=-1, keepdims=True)
    m1 = jnp.mean(scaled * normed, axis=-1, keepdims=True)
    return inv * (scaled - m0 - normed * m1)


def colsum(v):
    return jnp.sum(v, axis=0, keepdims=True)


def lane_mask(which, dtype):
    lane = lax.broadcasted_iota(jnp.int32, (1, LANES), 1)
    keep = (lane < 64) if which == 0 else (lane >= 64)
    return jnp.where(keep, 1.0, 0.0).astype(F32).astype(dtype)


C0 = math.sqrt(2.0 / math.pi)


def gelu_pair(u):
    u2 = u * u
    inner = u * (C0 + (C0 * 0.044715) * u2)
    half = 0.5 + 0.5 * jnp.tanh(inner)
    g = u * half
    slope = half + 2.0 * g * (1.0 - half) * (C0 + (3.0 * C0 * 0.044715) * u2)
    return g, slope


def window_starts(shards, tiles):
    return [i * tiles // shards for i in range(shards + 1)]


def own_index():
    return lax.axis_index("dp") * lax.axis_size("rep") + lax.axis_index("rep")


def load_windows(w_refs, pieces, flat, edge, sem, shards):
    tiles = flat.shape[0] // TILE
    rows = [ref.shape[-2] for ref in w_refs]
    half = rows[0]
    base = tiles // shards * TILE
    me = own_index()
    copies = []
    for ref, (part, entries) in zip(w_refs, pieces):
        for pos, rel in entries:
            src = ref
            for k in pos:
                src = src.at[k]
            owner = jnp.bitwise_xor(me, rel)
            start = pl.multiple_of((owner * tiles // shards) * TILE, TILE)
            if part == 0:
                moves = [(src, flat.at[pl.ds(start, half)])]
            else:
                moves = [
                    (src.at[pl.ds(0, base - half)], flat.at[pl.ds(pl.multiple_of(start + half, TILE), base - half)]),
                    (src.at[pl.ds(base - half, 2 * TILE)], edge.at[owner]),
                ]
            for a, b in moves:
                copies.append(pltpu.make_async_copy(a, b, sem.at[len(copies)]))
                copies[-1].start()
    for copy in copies:
        copy.wait()
    starts = window_starts(shards, tiles)
    for i in range(shards):
        nxt = starts[i + 1]
        low = edge[i, 0:TILE, :]
        if nxt - starts[i] == base // TILE:
            if i + 1 < shards:
                flat[nxt * TILE : (nxt + 1) * TILE, :] = flat[nxt * TILE : (nxt + 1) * TILE, :] + low
        else:
            flat[(nxt - 1) * TILE : nxt * TILE, :] = low
            if i + 1 < shards:
                flat[nxt * TILE : (nxt + 1) * TILE, :] = flat[nxt * TILE : (nxt + 1) * TILE, :] + edge[i, TILE : 2 * TILE, :]


def store_windows(g_refs, flat, edge, sem, shards, vec_rows):
    tiles = flat.shape[0] // TILE
    half = g_refs[0].shape[-2]
    whole = 2 * half
    starts = window_starts(shards, tiles)
    last = lax.broadcasted_iota(jnp.int32, (TILE, LANES), 0) == TILE - 1
    for i in range(shards):
        low = starts[i] * TILE + whole - TILE
        if low + TILE <= flat.shape[0]:
            tile = flat[low : low + TILE, :].astype(F32)
        else:
            tile = jnp.zeros((TILE, LANES), F32)
        edge[i, 0:TILE, :] = jnp.where(last, vec_rows[i : i + 1], tile).astype(BF)
    me = own_index()
    copies = []
    for part in range(2):
        for rc in range(2):
            ref = g_refs[2 * rc + part]
            for r0 in range(2):
                for r1 in range(2):
                    rx, ry = (r0, r1) if part == 0 else (r1, r0)
                    for rz in range(4):
                        owner = jnp.bitwise_xor(me, rz * 8 + rx * 4 + rc * 2 + ry)
                        start = pl.multiple_of((owner * tiles // shards) * TILE, TILE)
                        dst = ref.at[r0].at[r1].at[rz]
                        if part == 0:
                            moves = [(flat.at[pl.ds(start, half)], dst)]
                        else:
                            moves = [
                                (flat.at[pl.ds(pl.multiple_of(start + half, TILE), half - TILE)], dst.at[pl.ds(0, half - TILE)]),
                                (edge.at[owner].at[pl.ds(0, TILE)], dst.at[pl.ds(half - TILE, TILE)]),
                            ]
                        for a, b in moves:
                            copies.append(pltpu.make_async_copy(a, b, sem.at[len(copies)]))
                            copies[-1].start()
    for copy in copies:
        copy.wait()


def pack_kernel(x_ref, a_ref, b_ref):
    me = own_index()
    v = x_ref[...]
    rows = v.shape[0]
    lane = lax.broadcasted_iota(jnp.int32, v.shape, 1)
    turned = pltpu.roll(v, 64, 1)
    moved = jnp.where(lane >= 64, turned, pltpu.roll(turned, 1, 0))
    odd = (me & 1) == 1
    v = jnp.where(odd, moved, v)
    shift = ((me * 192) & 2047) >> 7
    v = pltpu.roll(v, shift, 0).astype(BF)
    a_ref[...] = v[: rows // 2]
    b_ref[...] = v[rows // 2 :]


def finish_kernel(*refs):
    parts = []
    for h in range(2):
        total = None
        for ref in refs[4 * h : 4 * h + 4]:
            v = ref[...].astype(F32)
            total = v if total is None else total + v
        parts.append(total)
    out_ref, vec_ref = refs[8:]
    v = jnp.concatenate(parts, axis=0)
    rows = v.shape[0]
    vec_ref[...] = v[rows - 8 :]
    me = own_index()
    shift = ((me * 192) & 2047) >> 7
    v = pltpu.roll(v, rows - shift, 0)
    lane = lax.broadcasted_iota(jnp.int32, v.shape, 1)
    turned = pltpu.roll(v, 64, 1)
    moved = jnp.where(lane < 64, turned, pltpu.roll(turned, rows - 1, 0))
    odd = (me & 1) == 1
    out_ref[...] = jnp.where(odd, moved, v)


ROWB = 256
CHUNK = 512


def core_kernel(*refs, width, length, shards, pieces):
    n_in = 1 if pieces is None else len(pieces)
    (x_ref, cot_ref, segr_ref, segc_ref) = refs[:4]
    w_refs = refs[4 : 4 + n_in]
    refs = refs[4 + n_in :]
    (y_ref, dx_ref) = refs[:2]
    n_out = 1 if pieces is None else 4
    g_refs = refs[2 : 2 + n_out]
    (flat, wa, wi, wo, b1, vec, xb, qkv, ab0, ctx, xh1, iv1, xh2, iv2, h1b, slope, hb, du, df, da, dqkv, dc, xs, dr1, edge,
     gb1, gvec, sem) = refs[2 + n_out :]
    D = width
    T = length
    nb = T // ROWB
    pairs = D // LANES

    if pieces is None:
        cp = pltpu.make_async_copy(w_refs[0], flat, sem.at[0])
        cp.start()
        cp.wait()
    else:
        load_windows(w_refs, pieces, flat, edge, sem, shards)
    unpack_weights(flat, wa, wi, wo, b1, vec, D)

    scale = 0.125

    def bq(v):
        return v.astype(F32).astype(BF)

    def ab_store(r, h, qb, val):
        if r == 0:
            ab0[h, pl.ds(qb * ROWB, ROWB), :] = val
        else:
            for c in range(T // LANES):
                flat[pl.ds((h * (T // LANES) + c) * T + qb * ROWB, ROWB), :] = val[:, c * LANES : (c + 1) * LANES]

    def ab_load(r, h, qb):
        if r == 0:
            return ab0[h, pl.ds(qb * ROWB, ROWB), :]
        return jnp.concatenate(
            [flat[pl.ds((h * (T // LANES) + c) * T + qb * ROWB, ROWB), :] for c in range(T // LANES)], axis=1
        )

    def forward(r):
        src = x_ref if r == 0 else xs

        def proj(tb, carry):
            rows = pl.ds(pl.multiple_of(tb * ROWB, ROWB), ROWB)
            x16 = src[rows, :].astype(BF)
            xb[r, rows, :] = x16
            for j in range(3):
                p = dot(x16, wa[:, j * D : (j + 1) * D])
                if j == 0:
                    p = p + vec[0:1, :]
                if j == 2:
                    p = p + vec[1:2, :]
                p = p.astype(BF)
                for c in range(pairs):
                    qkv[r, j * pairs + c, rows, :] = p[:, c * LANES : (c + 1) * LANES]
            return carry

        lax.fori_loop(0, nb, proj, 0)

        def attend(p, carry):
            k2 = qkv[r, pairs + p]
            v2 = qkv[r, 2 * pairs + p]
            for qb in range(nb):
                out = None
                q2 = qkv[r, p, pl.ds(qb * ROWB, ROWB), :]
                allowed = segc_ref[pl.ds(qb * ROWB, ROWB), :] == segr_ref[...]
                for e in range(2):
                    m = lane_mask(e, BF)
                    s = dot_t(q2 * (m * scale).astype(BF), k2)
                    s = jnp.where(allowed, s, -1e30)
                    peak = jnp.max(s, axis=-1, keepdims=True)
                    ex = jnp.exp(s - peak)
                    tot = jnp.sum(ex, axis=-1, keepdims=True)
                    prob = (ex * (1.0 / tot)).astype(BF)
                    ab_store(r, 2 * p + e, qb, prob)
                    part = dot(prob, v2 * m)
                    out = part if out is None else out + part
                ctx[r, p, pl.ds(qb * ROWB, ROWB), :] = out.astype(BF)
            return carry

        lax.fori_loop(0, pairs, attend, 0)

        def mlp(tb, carry):
            rows = pl.ds(pl.multiple_of(tb * ROWB, ROWB), ROWB)
            c16 = jnp.concatenate([ctx[r, c, rows, :] for c in range(pairs)], axis=1)
            a = dot(c16, wa[:, 3 * D : 4 * D]) + vec[2:3, :]
            hat, inv = norm_stats(src[rows, :].astype(F32) + a)
            xh1[r, rows, :] = hat
            iv1[r, rows, :] = jnp.broadcast_to(inv, (ROWB, LANES))
            h1 = hat * vec[4:5, :] + vec[5:6, :]
            h16 = h1.astype(BF)
            h1b[r, rows, :] = h16
            f = h1 + vec[3:4, :]
            for c in range(FF // CHUNK):
                cols = slice(c * CHUNK, (c + 1) * CHUNK)
                u = dot(h16, wi[:, cols]) + b1[:, cols]
                g, sl = gelu_pair(u)
                g16 = g.astype(BF)
                hb[r, rows, cols] = g16
                slope[r, rows, cols] = sl
                f = f + dot(g16, wo[cols, :])
            hat, inv = norm_stats(f)
            xh2[r, rows, :] = hat
            iv2[r, rows, :] = jnp.broadcast_to(inv, (ROWB, LANES))
            y = hat * vec[6:7, :] + vec[7:8, :]
            if r == REC - 1:
                y_ref[rows, :] = y
            else:
                xs[rows, :] = y
            return carry

        lax.fori_loop(0, nb, mlp, 0)

    def acc(ref, row, val):
        ref[row : row + 1, :] = ref[row : row + 1, :] + val

    def backward(r):
        src = cot_ref if r == REC - 1 else dx_ref

        def mlp(tb, carry):
            rows = pl.ds(pl.multiple_of(tb * ROWB, ROWB), ROWB)
            dy = src[rows, :].astype(F32)
            hat = xh2[r, rows, :]
            acc(gvec, 6, colsum(dy * hat))
            acc(gvec, 7, colsum(dy))
            dr2 = norm_grad(dy, hat, iv2[r, rows, 0:1], vec[6:7, :])
            d16 = dr2.astype(BF)
            df[r, rows, :] = d16
            acc(gvec, 3, colsum(d16.astype(F32)))
            dh = dr2
            for c in range(FF // CHUNK):
                cols = slice(c * CHUNK, (c + 1) * CHUNK)
                t = dot_t(d16, wo[cols, :]).astype(BF).astype(F32)
                g16 = (t * slope[r, rows, cols]).astype(BF)
                du[r, rows, cols] = g16
                gb1[0:1, cols] = gb1[0:1, cols] + colsum(g16.astype(F32))
                dh = dh + dot_t(g16, wi[:, cols])
            hat = xh1[r, rows, :]
            acc(gvec, 4, colsum(dh * hat))
            acc(gvec, 5, colsum(dh))
            d1 = norm_grad(dh, hat, iv1[r, rows, 0:1], vec[4:5, :])
            dr1[rows, :] = d1
            a16 = d1.astype(BF)
            da[r, rows, :] = a16
            acc(gvec, 2, colsum(a16.astype(F32)))
            c16 = dot_t(a16, wa[:, 3 * D : 4 * D]).astype(BF)
            for c in range(pairs):
                dc[c, rows, :] = c16[:, c * LANES : (c + 1) * LANES]
            return carry

        lax.fori_loop(0, nb, mlp, 0)

        def attend(p, carry):
            k2 = qkv[r, pairs + p]
            v2 = qkv[r, 2 * pairs + p]
            dk = jnp.zeros((T, LANES), F32)
            dv = jnp.zeros((T, LANES), F32)
            for qb in range(nb):
                rows = pl.ds(qb * ROWB, ROWB)
                q2 = qkv[r, p, rows, :]
                dc2 = dc[p, rows, :]
                dq = None
                for e in range(2):
                    m = lane_mask(e, BF)
                    p16 = ab_load(r, 2 * p + e, qb)
                    pf = p16.astype(F32)
                    dcm = dc2 * m
                    t = dot_t(dcm, v2) * pf
                    s16 = (t - pf * jnp.sum(t, axis=-1, keepdims=True)).astype(BF)
                    part = dot(s16, k2 * m)
                    dq = part if dq is None else dq + part
                    dk = dk + t_dot(s16, q2 * m)
                    dv = dv + t_dot(p16, dcm)
                dqkv[r, p, rows, :] = (dq * scale).astype(BF)
            dqkv[r, pairs + p, :, :] = (dk * scale).astype(BF)
            dqkv[r, 2 * pairs + p, :, :] = dv.astype(BF)
            return carry

        lax.fori_loop(0, pairs, attend, 0)
        for c in range(pairs):
            cols = slice(c * LANES, (c + 1) * LANES)
            gvec[0:1, cols] = gvec[0:1, cols] + colsum(dqkv[r, c].astype(F32))
            gvec[1:2, cols] = gvec[1:2, cols] + colsum(dqkv[r, 2 * pairs + c].astype(F32))

        def back(tb, carry):
            rows = pl.ds(pl.multiple_of(tb * ROWB, ROWB), ROWB)
            d3 = jnp.concatenate([dqkv[r, c, rows, :] for c in range(3 * pairs)], axis=1)
            dx_ref[rows, :] = dr1[rows, :] + dot_t(d3, wa[:, : 3 * D])
            return carry

        lax.fori_loop(0, nb, back, 0)

    gb1[...] = jnp.zeros_like(gb1)
    gvec[...] = jnp.zeros_like(gvec)
    for r in range(REC):
        forward(r)
    for r in reversed(range(REC)):
        backward(r)

    per = 4 * D // LANES
    n = 256 // per
    swap = one_hot_swap(n, per)

    def wide_rows(base, d0, vals):
        for k in range(256 // n):
            pieces = []
            for c in range(per):
                v = vals[c * LANES // 512]
                o = c * LANES % 512
                pieces.append(v[k * n : (k + 1) * n, o : o + LANES])
            out = dot(swap, jnp.concatenate(pieces, axis=0)).astype(BF)
            flat[pl.ds(base + d0 * per + k * 256, 256), :] = out

    for d0 in range(0, D, 256):
        xt = [jnp.transpose(xb[r, :, d0 : d0 + 256]) for r in range(REC)]
        vals = []
        for j in range(3):
            g = None
            for r in range(REC):
                d3 = jnp.concatenate([dqkv[r, j * pairs + c] for c in range(pairs)], axis=1)
                part = dot(xt[r], d3)
                g = part if g is None else g + part
            vals.append(g.astype(BF))
        g = None
        for r in range(REC):
            cc = jnp.concatenate([ctx[r, d0 // LANES + c] for c in range(256 // LANES)], axis=1)
            part = t_dot(cc, da[r])
            g = part if g is None else g + part
        vals.append(g.astype(BF))
        wide_rows(0, d0, vals)
    for d0 in range(0, D, 256):
        ht = [jnp.transpose(h1b[r, :, d0 : d0 + 256]) for r in range(REC)]
        vals = []
        for j in range(FF // 512):
            g = None
            for r in range(REC):
                part = dot(ht[r], du[r, :, j * 512 : (j + 1) * 512])
                g = part if g is None else g + part
            vals.append(g.astype(BF))
        wide_rows(D * per, d0, vals)
    per_out = D // LANES
    n_out = 256 // per_out
    swap_out = one_hot_swap(n_out, per_out)
    base = 2 * D * per

    def out_rows(fb, carry):
        cols = pl.ds(pl.multiple_of(fb * 256, 256), 256)
        g = None
        for r in range(REC):
            part = t_dot(hb[r, :, cols], df[r])
            g = part if g is None else g + part
        g = g.astype(BF)
        for k in range(256 // n_out):
            pieces = [g[k * n_out : (k + 1) * n_out, c * LANES : (c + 1) * LANES] for c in range(per_out)]
            out = dot(swap_out, jnp.concatenate(pieces, axis=0)).astype(BF)
            flat[pl.ds(pl.multiple_of(base + fb * (256 * per_out) + k * 256, 256), 256), :] = out
        return carry

    lax.fori_loop(0, FF // 256, out_rows, 0)
    base = base + FF * per_out
    rows = [gb1[0:1, c * LANES : (c + 1) * LANES] for c in range(FF // LANES)]
    for r in range(8):
        rows = rows + [gvec[r : r + 1, c * LANES : (c + 1) * LANES] for c in range(per_out)]
    tail = jnp.concatenate(rows, axis=0)
    flat[base : base + len(rows), :] = tail.astype(BF)
    if pieces is None:
        cp = pltpu.make_async_copy(flat, g_refs[0], sem.at[0])
        cp.start()
        cp.wait()
    else:
        store_windows(g_refs, flat, edge, sem, shards, tail[FF // LANES :])


def core(x, cot, seg, flats, pieces, shards, rows):
    T, D = x.shape
    vm = pltpu.VMEM
    pairs = D // LANES
    scratch = [
        vm((rows, LANES), BF),
        vm((D, 4 * D), BF), vm((D, FF), BF), vm((FF, D), BF), vm((1, FF), F32), vm((8, D), F32),
        vm((REC, T, D), BF), vm((REC, 3 * pairs, T, LANES), BF), vm((HEADS, T, T), BF), vm((REC, pairs, T, LANES), BF),
        vm((REC, T, D), F32), vm((REC, T, LANES), F32), vm((REC, T, D), F32), vm((REC, T, LANES), F32),
        vm((REC, T, D), BF), vm((REC, T, FF), F32), vm((REC, T, FF), BF), vm((REC, T, FF), BF),
        vm((REC, T, D), BF), vm((REC, T, D), BF), vm((REC, 3 * pairs, T, LANES), BF), vm((pairs, T, LANES), BF),
        vm((T, D), F32), vm((T, D), F32), vm((shards if pieces else 1, 2 * TILE, LANES), BF),
        vm((1, FF), F32), vm((8, D), F32),
        pltpu.SemaphoreType.DMA((96,)),
    ]
    if pieces is None:
        g_shapes = [jax.ShapeDtypeStruct((rows, LANES), BF)]
    else:
        half = flats[0].shape[-2]
        g_shapes = [jax.ShapeDtypeStruct((2, 2, 4, half, LANES), BF)] * 4
    in_vmem = pl.BlockSpec(memory_space=pltpu.VMEM)
    anywhere = pl.BlockSpec(memory_space=pl.ANY)
    return pl.pallas_call(
        functools.partial(core_kernel, width=D, length=T, shards=shards, pieces=pieces),
        out_shape=tuple([jax.ShapeDtypeStruct((T, D), F32)] * 2 + g_shapes),
        in_specs=[in_vmem] * 4 + [anywhere] * len(flats),
        out_specs=tuple([in_vmem] * 2 + [anywhere] * len(g_shapes)),
        scratch_shapes=scratch,
        compiler_params=pltpu.CompilerParams(vmem_limit_bytes=60 * 1024 * 1024),
        name="layer_core",
    )(x, cot, seg.reshape(1, T), seg.reshape(T, 1), *flats)


AXES = ("dp", "rep")


def exchange(v, rel):
    count = lax.axis_size("dp") * lax.axis_size("rep")
    return lax.ppermute(v, AXES, [(j, j ^ rel) for j in range(count)])


RZ, RX, RC, RY = 8, 4, 2, 1


def gather_windows(a, b):
    out, pieces = [], []
    for part, own in enumerate((a, b)):
        first, second = (RX, RY) if part == 0 else (RY, RX)
        stack = jnp.stack([own] + [exchange(own, k * RZ) for k in (1, 2, 3)])
        near = exchange(stack, first)
        far = exchange(jnp.stack([stack, near]), second)
        for rc in (0, RC):
            for v, dims in ((stack, (0,)), (near, (first,)), (far, (second,))):
                out.append(v if rc == 0 else exchange(v, rc))
                if v is far:
                    ent = [((n, k), k * RZ + second + n * first + rc) for n in range(2) for k in range(4)]
                else:
                    ent = [((k,), k * RZ + dims[0] + rc) for k in range(4)]
                pieces.append((part, ent))
    order = sorted(range(len(out)), key=lambda i: pieces[i][0])
    return [out[i] for i in order], [pieces[i] for i in order]


def sum_windows(keeps, sends):
    res = []
    for part in range(2):
        first, second = (RX, RY) if part == 0 else (RY, RX)
        got = exchange(sends[part], RC)
        keep = keeps[part]
        got1 = exchange(keep[1] + got[1], first)
        mine = keep[0] + got[0]
        got2 = exchange(mine[1] + got1[1], second)
        mine = mine[0] + got1[0]
        v = mine + got2
        res.append([v[0]] + [exchange(v[k], k * RZ) for k in (1, 2, 3)])
    return res


def shards_fn(block_input, segment_ids, cotangent, master_weights, momentum, weight_average):
    width = block_input.shape[2]
    length = block_input.shape[1]
    count = lax.axis_size("dp") * lax.axis_size("rep")
    share = master_weights.shape[0]
    rows = share * count // LANES
    tiles = rows // TILE
    vec_len = 8 * width // count
    args = (block_input[0], cotangent[0], segment_ids[0])
    in_vmem = pl.BlockSpec(memory_space=pltpu.VMEM)
    if count == 32:
        window = (tiles // count + 2) * TILE
        padded = jnp.pad(master_weights, (0, window * LANES - share)).reshape(window, LANES)
        half = jax.ShapeDtypeStruct((window // 2, LANES), BF)
        a, b = pl.pallas_call(
            pack_kernel, out_shape=(half, half), in_specs=[in_vmem], out_specs=(in_vmem, in_vmem), name="pack_shard"
        )(padded)
        flats, pieces = gather_windows(a, b)
        block_output, input_grad, ka, kb, sa, sb = core(*args, flats, pieces, count, rows)
        parts = sum_windows((ka, kb), (sa, sb))
        grad, tail = pl.pallas_call(
            finish_kernel,
            out_shape=(jax.ShapeDtypeStruct((window, LANES), F32), jax.ShapeDtypeStruct((8, LANES), F32)),
            in_specs=[in_vmem] * 8,
            out_specs=(in_vmem, in_vmem),
            name="finish_shard",
        )(*parts[0], *parts[1])
        weight_grad = grad.reshape(-1)[:share]
        vector_grad = tail[7]
    else:
        flat = lax.all_gather(master_weights.astype(BF), AXES, axis=0, tiled=True).reshape(rows, LANES)
        block_output, input_grad, grad = core(*args, [flat], None, count, rows)
        grad = grad.reshape(-1).astype(F32)
        weight_grad = lax.psum_scatter(grad, AXES, scatter_dimension=0, tiled=True)
        vector_grad = lax.psum_scatter(grad[grad.shape[0] - 8 * width :], AXES, scatter_dimension=0, tiled=True)
    token_count = block_input.shape[0] * length * count
    rate = rate_base / math.sqrt(token_count)
    new_momentum = mom_decay * momentum + weight_grad
    new_weights = master_weights - rate * (weight_grad + mom_decay * new_momentum)
    new_average = avg_keep * weight_average + (1.0 - avg_keep) * new_weights
    return (
        block_output[None],
        input_grad[None],
        weight_grad,
        vector_grad,
        new_momentum,
        new_average,
        new_weights,
    )


def solution(mesh):
    three = P(AXES, None, None)
    two = P(AXES, None)
    one = P(AXES)
    return jax.shard_map(
        shards_fn,
        mesh=mesh,
        in_specs=(three, two, three, one, one, one),
        out_specs=(three, three, one, one, one, one, one),
        check_vma=False,
    )
```

```python
import functools
import math

import jax
import jax.numpy as jnp
from jax import lax
from jax.experimental import pallas as pl
from jax.experimental.pallas import tpu as pltpu
from jax.sharding import PartitionSpec as P

FF = 2048
HEADS = 8
REC = 2
TILE = 16
LANES = 128

norm_eps = 1e-05
mom_decay = 0.9
avg_keep = 0.8
rate_base = 0.006

BF = jnp.bfloat16
F32 = jnp.float32


def dot(a, b):
    return lax.dot_general(a, b, (((1,), (0,)), ((), ())), preferred_element_type=F32)


def dot_t(a, b):
    return lax.dot_general(a, b, (((1,), (1,)), ((), ())), preferred_element_type=F32)


def t_dot(a, b):
    return lax.dot_general(a, b, (((0,), (0,)), ((), ())), preferred_element_type=F32)


def one_hot_swap(outer, inner):
    size = outer * inner
    row = lax.broadcasted_iota(jnp.int32, (size, size), 0)
    col = lax.broadcasted_iota(jnp.int32, (size, size), 1)
    shift = inner.bit_length() - 1
    want = (row & (inner - 1)) * outer + (row >> shift)
    return jnp.where(col == want, 1.0, 0.0).astype(F32).astype(BF)


def matrix_blocks(wa, wi, wo, width):
    per = 4 * width // LANES
    base = 0
    for ref, per in ((wa, per), (wi, FF // LANES), (wo, width // LANES)):
        yield ref, per, base
        base = base + ref.shape[0] * per


def unpack_weights(flat, wa, wi, wo, b1, vec, width):
    for ref, per, base in matrix_blocks(wa, wi, wo, width):
        n = 256 // per
        swap = one_hot_swap(per, n)

        def body(g, carry, ref=ref, per=per, base=base, n=n, swap=swap):
            first = flat[pl.ds(pl.multiple_of(base + g * 512, 512), 256), :]
            second = flat[pl.ds(pl.multiple_of(base + g * 512, 512) + 256, 256), :]
            out = dot(swap, jnp.concatenate([first, second], axis=1)).astype(BF)
            row = pl.multiple_of(g * 2 * n, 2 * n)
            for c in range(per):
                piece = out[c * n : (c + 1) * n]
                cols = slice(c * LANES, (c + 1) * LANES)
                ref[pl.ds(row, 2 * n), cols] = jnp.concatenate([piece[:, :LANES], piece[:, LANES:]], axis=0)
            return carry

        lax.fori_loop(0, ref.shape[0] * per // 512, body, 0, unroll=8)
    per_out = width // LANES
    tail = flat[flat.shape[0] - FF // LANES - 8 * per_out : flat.shape[0], :].astype(F32)
    for c in range(FF // LANES):
        b1[0:1, c * LANES : (c + 1) * LANES] = tail[c : c + 1]
    for r in range(8):
        for c in range(per_out):
            k = FF // LANES + r * per_out + c
            vec[r : r + 1, c * LANES : (c + 1) * LANES] = tail[k : k + 1]


def pack_weights(flat, wa, wi, wo, width):
    for ref, per, base in matrix_blocks(wa, wi, wo, width):
        n = 256 // per
        swap = one_hot_swap(n, per)

        def body(g, carry, ref=ref, per=per, base=base, n=n, swap=swap):
            row = pl.multiple_of(g * 2 * n, 2 * n)
            pieces = []
            for c in range(per):
                v = ref[pl.ds(row, 2 * n), c * LANES : (c + 1) * LANES]
                pieces.append(jnp.concatenate([v[:n], v[n:]], axis=1))
            out = dot(swap, jnp.concatenate(pieces, axis=0)).astype(BF)
            first = pl.multiple_of(base + g * 512, 512)
            flat[pl.ds(first, 256), :] = out[:, :LANES]
            flat[pl.ds(first + 256, 256), :] = out[:, LANES:]
            return carry

        lax.fori_loop(0, ref.shape[0] * per // 512, body, 0, unroll=8)


def norm_stats(resid):
    center = resid - jnp.mean(resid, axis=-1, keepdims=True)
    variance = jnp.mean(center * center, axis=-1, keepdims=True)
    inv = lax.rsqrt(variance + norm_eps)
    return center * inv, inv


def norm_grad(upstream, normed, inv, gain):
    scaled = upstream * gain
    m0 = jnp.mean(scaled, axis=-1, keepdims=True)
    m1 = jnp.mean(scaled * normed, axis=-1, keepdims=True)
    return inv * (scaled - m0 - normed * m1)


def colsum(v):
    return jnp.sum(v, axis=0, keepdims=True)


def lane_mask(which, dtype):
    lane = lax.broadcasted_iota(jnp.int32, (1, LANES), 1)
    keep = (lane < 64) if which == 0 else (lane >= 64)
    return jnp.where(keep, 1.0, 0.0).astype(F32).astype(dtype)


C0 = math.sqrt(2.0 / math.pi)


def gelu_pair(u):
    u2 = u * u
    inner = u * (C0 + (C0 * 0.044715) * u2)
    half = 0.5 + 0.5 * jnp.tanh(inner)
    g = u * half
    slope = half + 2.0 * g * (1.0 - half) * (C0 + (3.0 * C0 * 0.044715) * u2)
    return g, slope


def window_starts(shards, tiles):
    return [i * tiles // shards for i in range(shards + 1)]


def own_index():
    return lax.axis_index("dp") * lax.axis_size("rep") + lax.axis_index("rep")


def load_windows(w_refs, pieces, flat, edge, sem, shards):
    tiles = flat.shape[0] // TILE
    rows = [ref.shape[-2] for ref in w_refs]
    half = rows[0]
    base = tiles // shards * TILE
    me = own_index()
    copies = []
    for ref, (part, entries) in zip(w_refs, pieces):
        for pos, rel in entries:
            src = ref
            for k in pos:
                src = src.at[k]
            owner = jnp.bitwise_xor(me, rel)
            start = pl.multiple_of((owner * tiles // shards) * TILE, TILE)
            if part == 0:
                moves = [(src, flat.at[pl.ds(start, half)])]
            else:
                moves = [
                    (src.at[pl.ds(0, base - half)], flat.at[pl.ds(pl.multiple_of(start + half, TILE), base - half)]),
                    (src.at[pl.ds(base - half, 2 * TILE)], edge.at[owner]),
                ]
            for a, b in moves:
                copies.append(pltpu.make_async_copy(a, b, sem.at[len(copies)]))
                copies[-1].start()
    for copy in copies:
        copy.wait()
    starts = window_starts(shards, tiles)
    for i in range(shards):
        nxt = starts[i + 1]
        low = edge[i, 0:TILE, :]
        if nxt - starts[i] == base // TILE:
            if i + 1 < shards:
                flat[nxt * TILE : (nxt + 1) * TILE, :] = flat[nxt * TILE : (nxt + 1) * TILE, :] + low
        else:
            flat[(nxt - 1) * TILE : nxt * TILE, :] = low
            if i + 1 < shards:
                flat[nxt * TILE : (nxt + 1) * TILE, :] = flat[nxt * TILE : (nxt + 1) * TILE, :] + edge[i, TILE : 2 * TILE, :]


def store_windows(g_refs, flat, edge, sem, shards, vec_rows):
    tiles = flat.shape[0] // TILE
    half = g_refs[0].shape[-2]
    whole = 2 * half
    starts = window_starts(shards, tiles)
    last = lax.broadcasted_iota(jnp.int32, (TILE, LANES), 0) == TILE - 1
    for i in range(shards):
        low = starts[i] * TILE + whole - TILE
        if low + TILE <= flat.shape[0]:
            tile = flat[low : low + TILE, :].astype(F32)
        else:
            tile = jnp.zeros((TILE, LANES), F32)
        edge[i, 0:TILE, :] = jnp.where(last, vec_rows[i : i + 1], tile).astype(BF)
    me = own_index()
    copies = []
    for part in range(2):
        for rc in range(2):
            ref = g_refs[2 * rc + part]
            for r0 in range(2):
                for r1 in range(2):
                    rx, ry = (r0, r1) if part == 0 else (r1, r0)
                    for rz in range(4):
                        owner = jnp.bitwise_xor(me, rz * 8 + rx * 4 + rc * 2 + ry)
                        start = pl.multiple_of((owner * tiles // shards) * TILE, TILE)
                        dst = ref.at[r0].at[r1].at[rz]
                        if part == 0:
                            moves = [(flat.at[pl.ds(start, half)], dst)]
                        else:
                            moves = [
                                (flat.at[pl.ds(pl.multiple_of(start + half, TILE), half - TILE)], dst.at[pl.ds(0, half - TILE)]),
                                (edge.at[owner].at[pl.ds(0, TILE)], dst.at[pl.ds(half - TILE, TILE)]),
                            ]
                        for a, b in moves:
                            copies.append(pltpu.make_async_copy(a, b, sem.at[len(copies)]))
                            copies[-1].start()
    for copy in copies:
        copy.wait()


def pack_kernel(x_ref, a_ref, b_ref):
    me = own_index()
    v = x_ref[...]
    rows = v.shape[0]
    lane = lax.broadcasted_iota(jnp.int32, v.shape, 1)
    turned = pltpu.roll(v, 64, 1)
    moved = jnp.where(lane >= 64, turned, pltpu.roll(turned, 1, 0))
    odd = (me & 1) == 1
    v = jnp.where(odd, moved, v)
    shift = ((me * 192) & 2047) >> 7
    v = pltpu.roll(v, shift, 0).astype(BF)
    a_ref[...] = v[: rows // 2]
    b_ref[...] = v[rows // 2 :]


def finish_kernel(*refs):
    parts = []
    for h in range(2):
        total = None
        for ref in refs[4 * h : 4 * h + 4]:
            v = ref[...].astype(F32)
            total = v if total is None else total + v
        parts.append(total)
    out_ref, vec_ref = refs[8:]
    v = jnp.concatenate(parts, axis=0)
    rows = v.shape[0]
    vec_ref[...] = v[rows - 8 :]
    me = own_index()
    shift = ((me * 192) & 2047) >> 7
    v = pltpu.roll(v, rows - shift, 0)
    lane = lax.broadcasted_iota(jnp.int32, v.shape, 1)
    turned = pltpu.roll(v, 64, 1)
    moved = jnp.where(lane < 64, turned, pltpu.roll(turned, rows - 1, 0))
    odd = (me & 1) == 1
    out_ref[...] = jnp.where(odd, moved, v)


CHUNK = 512
STEP = 32
GSTEP = 16
AHEAD = 2


def core_kernel(*refs, width, length, shards, pieces, flat_rows):
    n_in = 1 if pieces is None else len(pieces)
    (x_ref, cot_ref, segr_ref, segc_ref) = refs[:4]
    w_refs = refs[4 : 4 + n_in]
    refs = refs[4 + n_in :]
    (y_ref, dx_ref) = refs[:2]
    n_out = 1 if pieces is None else 4
    g_refs = refs[2 : 2 + n_out]
    (wide, wa, wi, wo, b1, vec, xb, qkv, ab, ctx, xh1, iv1, xh2, iv2, h1b, slope, df, da, dqkv, dc, dr1, edge,
     bias, gb1, gvec, count_ref, sem) = refs[2 + n_out :]
    D = width
    T = length
    pairs = D // LANES
    flat = wide.at[pl.ds(0, flat_rows)]

    if pieces is None:
        cp = pltpu.make_async_copy(w_refs[0], flat, sem.at[0])
        cp.start()
        cp.wait()
    else:
        load_windows(w_refs, pieces, flat, edge, sem, shards)
    unpack_weights(flat, wa, wi, wo, b1, vec, D)

    scale = 0.125
    bias[...] = jnp.where(segc_ref[...] == segr_ref[...], 0.0, -1e30).astype(F32)

    count_ref[0] = 1
    single = count_ref[0]

    def phase(body):
        def step(_, carry):
            body()
            return carry

        lax.fori_loop(0, single, step, 0)

    hidden = FF * REC * T // LANES

    def put(which, chunk, row, val):
        for j in range(CHUNK // LANES):
            at = which * hidden + (chunk * (CHUNK // LANES) + j) * REC * T
            wide[pl.ds(row + at, val.shape[0]), :] = val[:, j * LANES : (j + 1) * LANES]

    def get(which, chunk, row, n):
        at = [which * hidden + (chunk * (CHUNK // LANES) + j) * REC * T for j in range(CHUNK // LANES)]
        return jnp.concatenate([wide[pl.ds(row + k, n), :] for k in at], axis=1)

    def project(r):
        rows = pl.ds(pl.multiple_of(r * T, T), T)
        x16 = dx_ref[...].astype(BF)
        xb[rows, :] = x16
        for j in range(3):
            p = dot(x16, wa[:, j * D : (j + 1) * D])
            if j == 0:
                p = p + vec[0:1, :]
            if j == 2:
                p = p + vec[1:2, :]
            p = p.astype(BF)
            for c in range(pairs):
                qkv[r, j * pairs + c] = p[:, c * LANES : (c + 1) * LANES]

    def attend(r):
        rows = pl.ds(pl.multiple_of(r * T, T), T)

        def score(h):
            return dot_t(qkv[r, h // 2] * (lane_mask(h % 2, BF) * scale).astype(BF), qkv[r, pairs + h // 2])

        pend = [score(h) for h in range(AHEAD)]
        left = None
        for h in range(HEADS):
            if h + AHEAD < HEADS:
                pend.append(score(h + AHEAD))
            full = pend.pop(0)
            parts = []
            for i in range(0, T, STEP):
                sc = full[i : i + STEP] + bias[i : i + STEP, :]
                ex = jnp.exp(sc - jnp.max(sc, axis=-1, keepdims=True))
                tot = jnp.sum(ex, axis=-1, keepdims=True)
                parts.append((ex * (1.0 / tot)).astype(BF))
                ab[r * HEADS + h, pl.ds(i, STEP), :] = parts[-1]
            out = dot(jnp.concatenate(parts, axis=0), qkv[r, 2 * pairs + h // 2] * lane_mask(h % 2, BF))
            if h % 2 == 0:
                left = out
            else:
                ctx[h // 2, rows, :] = (left + out).astype(BF)

    def feed(r):
        rows = pl.ds(pl.multiple_of(r * T, T), T)
        a = dot(jnp.concatenate([ctx[c, rows, :] for c in range(pairs)], axis=1), wa[:, 3 * D : 4 * D])
        for i in range(0, T, STEP):
            sub = pl.ds(i, STEP)
            hat, inv = norm_stats(dx_ref[sub, :] + (a[i : i + STEP] + vec[2:3, :]))
            xh1[r, sub, :] = hat
            iv1[r, sub, :] = jnp.broadcast_to(inv, (STEP, LANES))
            h1b[pl.ds(pl.multiple_of(r * T, T) + i, STEP), :] = (hat * vec[4:5, :] + vec[5:6, :]).astype(BF)
        h16 = h1b[rows, :]

        def up(c):
            return dot(h16, wi[:, c * CHUNK : (c + 1) * CHUNK])

        pend = [up(0)]
        f = None
        for c in range(FF // CHUNK):
            cols = slice(c * CHUNK, (c + 1) * CHUNK)
            if c + 1 < FF // CHUNK:
                pend.append(up(c + 1))
            u = pend.pop(0)
            parts = []
            for i in range(0, T, GSTEP):
                g, sl = gelu_pair(u[i : i + GSTEP] + b1[:, cols])
                parts.append(g.astype(BF))
                put(0, c, pl.multiple_of(r * T, T) + i, parts[-1])
                slope[r, pl.ds(i, GSTEP), cols] = sl
            part = dot(jnp.concatenate(parts, axis=0), wo[cols, :])
            f = part if f is None else f + part
        for i in range(0, T, STEP):
            sub = pl.ds(i, STEP)
            h1 = xh1[r, sub, :] * vec[4:5, :] + vec[5:6, :]
            hat, inv = norm_stats(h1 + (f[i : i + STEP] + vec[3:4, :]))
            xh2[r, sub, :] = hat
            iv2[r, sub, :] = jnp.broadcast_to(inv, (STEP, LANES))
            y = hat * vec[6:7, :] + vec[7:8, :]
            dx_ref[sub, :] = y

    def acc(ref, row, val):
        ref[row : row + 1, :] = ref[row : row + 1, :] + val

    def feed_back(r):
        rows = pl.ds(pl.multiple_of(r * T, T), T)
        sums = [jnp.zeros((8, D), F32) for _ in range(6)]

        def add(k, val):
            sums[k] = sums[k] + jnp.sum(val.reshape(STEP // 8, 8, D), axis=0)

        for i in range(0, T, STEP):
            sub = pl.ds(i, STEP)
            dy = dx_ref[sub, :]
            hat = xh2[r, sub, :]
            add(0, dy * hat)
            add(1, dy)
            dr2 = norm_grad(dy, hat, iv2[r, sub, 0:1], vec[6:7, :])
            dr1[sub, :] = dr2
            d16 = dr2.astype(BF)
            df[pl.ds(pl.multiple_of(r * T, T) + i, STEP), :] = d16
            add(2, d16.astype(F32))
        d16 = df[rows, :]

        def down(c):
            return dot_t(d16, wo[c * CHUNK : (c + 1) * CHUNK, :])

        pend = [down(0)]
        dh = None
        for c in range(FF // CHUNK):
            cols = slice(c * CHUNK, (c + 1) * CHUNK)
            if c + 1 < FF // CHUNK:
                pend.append(down(c + 1))
            t = pend.pop(0)
            tot = jnp.zeros((8, CHUNK), F32)
            parts = []
            for i in range(0, T, GSTEP):
                g16 = (t[i : i + GSTEP].astype(BF).astype(F32) * slope[r, pl.ds(i, GSTEP), cols]).astype(BF)
                parts.append(g16)
                put(1, c, pl.multiple_of(r * T, T) + i, g16)
                tot = tot + jnp.sum(g16.astype(F32).reshape(GSTEP // 8, 8, CHUNK), axis=0)
            gb1[0:1, cols] = gb1[0:1, cols] + colsum(tot)
            part = dot_t(jnp.concatenate(parts, axis=0), wi[:, cols])
            dh = part if dh is None else dh + part
        for i in range(0, T, STEP):
            sub = pl.ds(i, STEP)
            hat = xh1[r, sub, :]
            upstream = dr1[sub, :] + dh[i : i + STEP]
            add(3, upstream * hat)
            add(4, upstream)
            d1 = norm_grad(upstream, hat, iv1[r, sub, 0:1], vec[4:5, :])
            dr1[sub, :] = d1
            a16 = d1.astype(BF)
            da[pl.ds(pl.multiple_of(r * T, T) + i, STEP), :] = a16
            add(5, a16.astype(F32))
        for row, k in ((6, 0), (7, 1), (3, 2), (4, 3), (5, 4), (2, 5)):
            acc(gvec, row, colsum(sums[k]))
        c16 = dot_t(da[rows, :], wa[:, 3 * D : 4 * D]).astype(BF)
        for c in range(pairs):
            dc[c] = c16[:, c * LANES : (c + 1) * LANES]

    def attend_back(r):
        rows = pl.ds(pl.multiple_of(r * T, T), T)

        def rise(h):
            return dot_t(dc[h // 2] * lane_mask(h % 2, BF), qkv[r, 2 * pairs + h // 2])

        pend = [rise(h) for h in range(AHEAD)]
        for h in range(HEADS):
            if h + AHEAD < HEADS:
                pend.append(rise(h + AHEAD))
            full = pend.pop(0)
            p, e = h // 2, h % 2
            half = slice(64 * e, 64 * e + 64)
            if e == 0:
                qt = jnp.transpose(qkv[r, p])
                ct = jnp.transpose(dc[p])
                dkt, dvt = [], []
            p16 = ab[r * HEADS + h]
            parts = []
            for i in range(0, T, STEP):
                pf = p16[i : i + STEP].astype(F32)
                t = full[i : i + STEP] * pf
                parts.append((t - pf * jnp.sum(t, axis=-1, keepdims=True)).astype(BF))
            s16 = jnp.concatenate(parts, axis=0)
            part = dot(s16, qkv[r, pairs + p] * lane_mask(e, BF))
            dkt.append(dot(qt[half], s16))
            dvt.append(dot(ct[half], p16))
            if e == 0:
                dq = part
            else:
                dqkv[p, rows, :] = ((dq + part) * scale).astype(BF)
                dqkv[pairs + p, rows, :] = jnp.transpose((jnp.concatenate(dkt, axis=0) * scale).astype(BF))
                dqkv[2 * pairs + p, rows, :] = jnp.transpose(jnp.concatenate(dvt, axis=0).astype(BF))
    def project_back(r):
        rows = pl.ds(pl.multiple_of(r * T, T), T)
        for c in range(pairs):
            cols = slice(c * LANES, (c + 1) * LANES)
            gvec[0:1, cols] = gvec[0:1, cols] + colsum(dqkv[c, rows, :].astype(F32))
            gvec[1:2, cols] = gvec[1:2, cols] + colsum(dqkv[2 * pairs + c, rows, :].astype(F32))
        d3 = jnp.concatenate([dqkv[c, rows, :] for c in range(3 * pairs)], axis=1)
        dx_ref[...] = dr1[...] + dot_t(d3, wa[:, : 3 * D])

    gb1[...] = jnp.zeros_like(gb1)
    gvec[...] = jnp.zeros_like(gvec)
    dx_ref[...] = x_ref[...].astype(F32)

    def forward(r, carry):
        for part in (project, attend, feed):
            phase(functools.partial(part, r))
        return carry

    def backward(i, carry):
        for part in (feed_back, attend_back, project_back):
            phase(functools.partial(part, REC - 1 - i))
        return carry

    lax.fori_loop(0, REC, forward, 0)
    y_ref[...] = dx_ref[...]
    dx_ref[...] = cot_ref[...].astype(F32)
    lax.fori_loop(0, REC, backward, 0)

    def grad_qkvo():
        xt = jnp.transpose(xb[...])
        for j in range(3):
            d3 = jnp.concatenate([dqkv[j * pairs + c] for c in range(pairs)], axis=1)
            wa[:, j * D : (j + 1) * D] = dot(xt, d3).astype(BF)
        for c in range(pairs):
            wa[c * LANES : (c + 1) * LANES, 3 * D : 4 * D] = t_dot(ctx[c], da[...]).astype(BF)

    def grad_in():
        ht = jnp.transpose(h1b[...])
        for c in range(FF // CHUNK):
            cols = slice(c * CHUNK, (c + 1) * CHUNK)
            wi[:, cols] = dot(ht, get(1, c, 0, REC * T)).astype(BF)

    def grad_out():
        for c in range(FF // CHUNK):
            cols = slice(c * CHUNK, (c + 1) * CHUNK)
            wo[cols, :] = t_dot(get(0, c, 0, REC * T), df[...]).astype(BF)

    phase(grad_qkvo)
    phase(grad_in)
    phase(grad_out)
    pack_weights(flat, wa, wi, wo, D)
    per_out = D // LANES
    rows = [gb1[0:1, c * LANES : (c + 1) * LANES] for c in range(FF // LANES)]
    for r in range(8):
        rows = rows + [gvec[r : r + 1, c * LANES : (c + 1) * LANES] for c in range(per_out)]
    tail = jnp.concatenate(rows, axis=0)
    flat[flat.shape[0] - len(rows) : flat.shape[0], :] = tail.astype(BF)
    if pieces is None:
        cp = pltpu.make_async_copy(flat, g_refs[0], sem.at[0])
        cp.start()
        cp.wait()
    else:
        store_windows(g_refs, flat, edge, sem, shards, tail[FF // LANES :])


def core(x, cot, seg, flats, pieces, shards, rows):
    T, D = x.shape
    vm = pltpu.VMEM
    pairs = D // LANES
    scratch = [
        vm((max(2 * FF * REC * T // LANES, rows), LANES), BF),
        vm((D, 4 * D), BF), vm((D, FF), BF), vm((FF, D), BF), vm((1, FF), F32), vm((8, D), F32),
        vm((REC * T, D), BF), vm((REC, 3 * pairs, T, LANES), BF), vm((REC * HEADS, T, T), BF), vm((pairs, REC * T, LANES), BF),
        vm((REC, T, D), F32), vm((REC, T, LANES), F32), vm((REC, T, D), F32), vm((REC, T, LANES), F32),
        vm((REC * T, D), BF), vm((REC, T, FF), F32),
        vm((REC * T, D), BF), vm((REC * T, D), BF), vm((3 * pairs, REC * T, LANES), BF), vm((pairs, T, LANES), BF),
        vm((T, D), F32), vm((shards if pieces else 1, 2 * TILE, LANES), BF), vm((T, T), F32),
        vm((1, FF), F32), vm((8, D), F32),
        pltpu.SMEM((1,), jnp.int32), pltpu.SemaphoreType.DMA((96,)),
    ]
    if pieces is None:
        g_shapes = [jax.ShapeDtypeStruct((rows, LANES), BF)]
    else:
        half = flats[0].shape[-2]
        g_shapes = [jax.ShapeDtypeStruct((2, 2, 4, half, LANES), BF)] * 4
    in_vmem = pl.BlockSpec(memory_space=pltpu.VMEM)
    anywhere = pl.BlockSpec(memory_space=pl.ANY)
    return pl.pallas_call(
        functools.partial(core_kernel, width=D, length=T, shards=shards, pieces=pieces, flat_rows=rows),
        out_shape=tuple([jax.ShapeDtypeStruct((T, D), F32)] * 2 + g_shapes),
        in_specs=[in_vmem] * 4 + [anywhere] * len(flats),
        out_specs=tuple([in_vmem] * 2 + [anywhere] * len(g_shapes)),
        scratch_shapes=scratch,
        compiler_params=pltpu.CompilerParams(vmem_limit_bytes=59 * 1024 * 1024),
        name="layer_core",
    )(x, cot, seg.reshape(1, T), seg.reshape(T, 1), *flats)


AXES = ("dp", "rep")


def exchange(v, rel):
    count = lax.axis_size("dp") * lax.axis_size("rep")
    return lax.ppermute(v, AXES, [(j, j ^ rel) for j in range(count)])


RZ, RX, RC, RY = 8, 4, 2, 1


def gather_windows(a, b):
    out, pieces = [], []
    for part, own in enumerate((a, b)):
        first, second = (RX, RY) if part == 0 else (RY, RX)
        stack = jnp.stack([own] + [exchange(own, k * RZ) for k in (1, 2, 3)])
        near = exchange(stack, first)
        far = exchange(jnp.stack([stack, near]), second)
        for rc in (0, RC):
            for v, dims in ((stack, (0,)), (near, (first,)), (far, (second,))):
                out.append(v if rc == 0 else exchange(v, rc))
                if v is far:
                    ent = [((n, k), k * RZ + second + n * first + rc) for n in range(2) for k in range(4)]
                else:
                    ent = [((k,), k * RZ + dims[0] + rc) for k in range(4)]
                pieces.append((part, ent))
    order = sorted(range(len(out)), key=lambda i: pieces[i][0])
    return [out[i] for i in order], [pieces[i] for i in order]


def sum_windows(keeps, sends):
    res = []
    for part in range(2):
        first, second = (RX, RY) if part == 0 else (RY, RX)
        got = exchange(sends[part], RC)
        keep = keeps[part]
        got1 = exchange(keep[1] + got[1], first)
        mine = keep[0] + got[0]
        got2 = exchange(mine[1] + got1[1], second)
        mine = mine[0] + got1[0]
        v = mine + got2
        res.append([v[0]] + [exchange(v[k], k * RZ) for k in (1, 2, 3)])
    return res


def shards_fn(block_input, segment_ids, cotangent, master_weights, momentum, weight_average):
    width = block_input.shape[2]
    length = block_input.shape[1]
    count = lax.axis_size("dp") * lax.axis_size("rep")
    share = master_weights.shape[0]
    rows = share * count // LANES
    tiles = rows // TILE
    vec_len = 8 * width // count
    args = (block_input[0], cotangent[0], segment_ids[0])
    in_vmem = pl.BlockSpec(memory_space=pltpu.VMEM)
    if count == 32:
        window = (tiles // count + 2) * TILE
        padded = jnp.pad(master_weights, (0, window * LANES - share)).reshape(window, LANES)
        half = jax.ShapeDtypeStruct((window // 2, LANES), BF)
        a, b = pl.pallas_call(
            pack_kernel, out_shape=(half, half), in_specs=[in_vmem], out_specs=(in_vmem, in_vmem), name="pack_shard"
        )(padded)
        flats, pieces = gather_windows(a, b)
        block_output, input_grad, ka, kb, sa, sb = core(*args, flats, pieces, count, rows)
        parts = sum_windows((ka, kb), (sa, sb))
        grad, tail = pl.pallas_call(
            finish_kernel,
            out_shape=(jax.ShapeDtypeStruct((window, LANES), F32), jax.ShapeDtypeStruct((8, LANES), F32)),
            in_specs=[in_vmem] * 8,
            out_specs=(in_vmem, in_vmem),
            name="finish_shard",
        )(*parts[0], *parts[1])
        weight_grad = grad.reshape(-1)[:share]
        vector_grad = tail[7]
    else:
        flat = lax.all_gather(master_weights.astype(BF), AXES, axis=0, tiled=True).reshape(rows, LANES)
        block_output, input_grad, grad = core(*args, [flat], None, count, rows)
        grad = grad.reshape(-1).astype(F32)
        weight_grad = lax.psum_scatter(grad, AXES, scatter_dimension=0, tiled=True)
        vector_grad = lax.psum_scatter(grad[grad.shape[0] - 8 * width :], AXES, scatter_dimension=0, tiled=True)
    token_count = block_input.shape[0] * length * count
    rate = rate_base / math.sqrt(token_count)
    new_momentum = mom_decay * momentum + weight_grad
    new_weights = master_weights - rate * (weight_grad + mom_decay * new_momentum)
    new_average = avg_keep * weight_average + (1.0 - avg_keep) * new_weights
    return (
        block_output[None],
        input_grad[None],
        weight_grad,
        vector_grad,
        new_momentum,
        new_average,
        new_weights,
    )


def solution(mesh):
    three = P(AXES, None, None)
    two = P(AXES, None)
    one = P(AXES)
    return jax.shard_map(
        shards_fn,
        mesh=mesh,
        in_specs=(three, two, three, one, one, one),
        out_specs=(three, three, one, one, one, one, one),
        check_vma=False,
    )
```

```python
import functools
import math

import jax
import jax.numpy as jnp
from jax import lax
from jax.experimental import pallas as pl
from jax.experimental.pallas import tpu as pltpu
from jax.sharding import PartitionSpec as P

FF = 2048
HEADS = 8
REC = 2
TILE = 16
LANES = 128

norm_eps = 1e-05
mom_decay = 0.9
avg_keep = 0.8
rate_base = 0.006

BF = jnp.bfloat16
F32 = jnp.float32


def dot(a, b):
    return lax.dot_general(a, b, (((1,), (0,)), ((), ())), preferred_element_type=F32)


def dot_t(a, b):
    return lax.dot_general(a, b, (((1,), (1,)), ((), ())), preferred_element_type=F32)


def t_dot(a, b):
    return lax.dot_general(a, b, (((0,), (0,)), ((), ())), preferred_element_type=F32)


def one_hot_swap(outer, inner):
    size = outer * inner
    row = lax.broadcasted_iota(jnp.int32, (size, size), 0)
    col = lax.broadcasted_iota(jnp.int32, (size, size), 1)
    shift = inner.bit_length() - 1
    want = (row & (inner - 1)) * outer + (row >> shift)
    return jnp.where(col == want, 1.0, 0.0).astype(F32).astype(BF)


def matrix_blocks(wa, wi, wo, width):
    per = 4 * width // LANES
    base = 0
    for ref, per in ((wa, per), (wi, FF // LANES), (wo, width // LANES)):
        yield ref, per, base
        base = base + ref.shape[0] * per


def unpack_weights(flat, wa, wi, wo, b1, vec, width):
    for ref, per, base in matrix_blocks(wa, wi, wo, width):
        n = 256 // per
        swap = one_hot_swap(per, n)

        def body(g, carry, ref=ref, per=per, base=base, n=n, swap=swap):
            first = flat[pl.ds(pl.multiple_of(base + g * 512, 512), 256), :]
            second = flat[pl.ds(pl.multiple_of(base + g * 512, 512) + 256, 256), :]
            out = dot(swap, jnp.concatenate([first, second], axis=1)).astype(BF)
            row = pl.multiple_of(g * 2 * n, 2 * n)
            for c in range(per):
                piece = out[c * n : (c + 1) * n]
                cols = slice(c * LANES, (c + 1) * LANES)
                ref[pl.ds(row, 2 * n), cols] = jnp.concatenate([piece[:, :LANES], piece[:, LANES:]], axis=0)
            return carry

        lax.fori_loop(0, ref.shape[0] * per // 512, body, 0, unroll=8)
    per_out = width // LANES
    tail = flat[flat.shape[0] - FF // LANES - 8 * per_out : flat.shape[0], :].astype(F32)
    for c in range(FF // LANES):
        b1[0:1, c * LANES : (c + 1) * LANES] = tail[c : c + 1]
    for r in range(8):
        for c in range(per_out):
            k = FF // LANES + r * per_out + c
            vec[r : r + 1, c * LANES : (c + 1) * LANES] = tail[k : k + 1]


def pack_weights(flat, wa, wi, wo, width):
    for ref, per, base in matrix_blocks(wa, wi, wo, width):
        n = 256 // per
        swap = one_hot_swap(n, per)

        def body(g, carry, ref=ref, per=per, base=base, n=n, swap=swap):
            row = pl.multiple_of(g * 2 * n, 2 * n)
            pieces = []
            for c in range(per):
                v = ref[pl.ds(row, 2 * n), c * LANES : (c + 1) * LANES]
                pieces.append(jnp.concatenate([v[:n], v[n:]], axis=1))
            out = dot(swap, jnp.concatenate(pieces, axis=0)).astype(BF)
            first = pl.multiple_of(base + g * 512, 512)
            flat[pl.ds(first, 256), :] = out[:, :LANES]
            flat[pl.ds(first + 256, 256), :] = out[:, LANES:]
            return carry

        lax.fori_loop(0, ref.shape[0] * per // 512, body, 0, unroll=8)


def norm_stats(resid):
    center = resid - jnp.mean(resid, axis=-1, keepdims=True)
    variance = jnp.mean(center * center, axis=-1, keepdims=True)
    inv = lax.rsqrt(variance + norm_eps)
    return center * inv, inv


def norm_grad(upstream, normed, inv, gain):
    scaled = upstream * gain
    m0 = jnp.mean(scaled, axis=-1, keepdims=True)
    m1 = jnp.mean(scaled * normed, axis=-1, keepdims=True)
    return inv * (scaled - m0 - normed * m1)


def colsum(v):
    return jnp.sum(v, axis=0, keepdims=True)


def lane_mask(which, dtype):
    lane = lax.broadcasted_iota(jnp.int32, (1, LANES), 1)
    keep = (lane < 64) if which == 0 else (lane >= 64)
    return jnp.where(keep, 1.0, 0.0).astype(F32).astype(dtype)


C0 = math.sqrt(2.0 / math.pi)


def gelu_pair(u):
    u2 = u * u
    inner = u * (C0 + (C0 * 0.044715) * u2)
    half = 0.5 + 0.5 * jnp.tanh(inner)
    g = u * half
    slope = half + 2.0 * g * (1.0 - half) * (C0 + (3.0 * C0 * 0.044715) * u2)
    return g, slope


def window_starts(shards, tiles):
    return [i * tiles // shards for i in range(shards + 1)]


def own_index():
    return lax.axis_index("dp") * lax.axis_size("rep") + lax.axis_index("rep")


RZ, RX, RC, RY = 8, 4, 2, 1
STEPS = ((RX, RY), (RY, RX), (2 * RZ, RZ), (RZ, 2 * RZ))
SLOTS = 1 << len(STEPS)


def own_core(me):
    return (me // RC) & 1


def slot_owner(base, core, slot):
    owner = base
    for k, (zero, one) in enumerate(STEPS):
        if slot >> (len(STEPS) - 1 - k) & 1:
            owner = jnp.bitwise_xor(owner, jnp.where(core == 0, zero, one))
    return owner


def settle(ref, rows, sem):
    pltpu.make_async_copy(ref.at[pl.ds(0, rows)], ref.at[pl.ds(0, rows)], sem).wait()


def window_moves(owner, height, tiles, shards, edge_row):
    start = pl.multiple_of((owner * tiles // shards) * TILE, TILE)
    edge = pl.multiple_of(edge_row + owner * 2 * TILE, TILE)
    body = height - 2 * TILE
    return [(0, start, body), (body, edge, 2 * TILE)]


def load_windows(w_refs, wide, flat, sem, shards):
    tiles = flat.shape[0] // TILE
    height = w_refs[0].shape[0]
    edge_row = flat.shape[0] + TILE
    base = tiles // shards * TILE
    me = own_index()
    core = own_core(me)
    for n, ref in enumerate(w_refs):
        side, origin = (core, me) if n < SLOTS else (1 - core, jnp.bitwise_xor(me, RC))
        owner = slot_owner(origin, side, n % SLOTS)
        for at, to, rows in window_moves(owner, height, tiles, shards, edge_row):
            pltpu.make_async_copy(ref.at[pl.ds(at, rows)], wide.at[pl.ds(to, rows)], sem.at[0]).start()
    settle(wide, height * len(w_refs), sem.at[0])
    starts = window_starts(shards, tiles)

    def tile(row):
        return wide[row : row + TILE, :]

    for i in range(shards):
        nxt = starts[i + 1]
        row = edge_row + i * 2 * TILE
        if nxt - starts[i] != base // TILE:
            wide[(nxt - 1) * TILE : nxt * TILE, :] = tile(row)
            row = row + TILE
        if i + 1 < shards:
            wide[nxt * TILE : (nxt + 1) * TILE, :] = tile(nxt * TILE) + tile(row)


def store_windows(g_refs, wide, flat, sem, shards, vec_rows):
    tiles = flat.shape[0] // TILE
    height = g_refs[0].shape[1]
    edge_row = flat.shape[0] + TILE
    starts = window_starts(shards, tiles)
    last = lax.broadcasted_iota(jnp.int32, (TILE, LANES), 0) == TILE - 1
    for i in range(shards):
        low = starts[i] * TILE + height - 2 * TILE
        row = edge_row + i * 2 * TILE
        for k in range(2):
            at = low + k * TILE
            if at + TILE <= flat.shape[0]:
                tile = wide[at : at + TILE, :]
            else:
                tile = jnp.zeros((TILE, LANES), BF)
            if k == 1:
                tile = jnp.where(last, vec_rows[i : i + 1], tile.astype(F32)).astype(BF)
            wide[row + k * TILE : row + (k + 1) * TILE, :] = tile
    me = own_index()
    core = own_core(me)
    for n, ref in enumerate(g_refs):
        side, origin = (core, me) if n == 0 else (1 - core, jnp.bitwise_xor(me, RC))
        first = SLOTS // 2 if n == 1 else 0
        for k in range(ref.shape[0]):
            owner = slot_owner(origin, side, first + k)
            for at, to, rows in window_moves(owner, height, tiles, shards, edge_row):
                pltpu.make_async_copy(wide.at[pl.ds(to, rows)], ref.at[k].at[pl.ds(at, rows)], sem.at[n]).start()
    for n, ref in enumerate(g_refs):
        settle(wide, ref.shape[0] * ref.shape[1], sem.at[n])


def pack_kernel(x_ref, out_ref):
    me = own_index()
    v = x_ref[...]
    lane = lax.broadcasted_iota(jnp.int32, v.shape, 1)
    turned = pltpu.roll(v, 64, 1)
    moved = jnp.where(lane >= 64, turned, pltpu.roll(turned, 1, 0))
    odd = (me & 1) == 1
    v = jnp.where(odd, moved, v)
    shift = ((me * 192) & 2047) >> 7
    out_ref[...] = pltpu.roll(v, shift, 0).astype(BF)


def finish_kernel(*refs):
    out_ref, vec_ref = refs[-2:]
    me = own_index()
    v = None
    for ref in refs[:-2]:
        part = ref[...].astype(F32)
        v = part if v is None else v + part
    rows = v.shape[0]
    vec_ref[...] = v[rows - 8 :]
    shift = ((me * 192) & 2047) >> 7
    v = pltpu.roll(v, rows - shift, 0)
    lane = lax.broadcasted_iota(jnp.int32, v.shape, 1)
    turned = pltpu.roll(v, 64, 1)
    moved = jnp.where(lane < 64, turned, pltpu.roll(turned, rows - 1, 0))
    odd = (me & 1) == 1
    out_ref[...] = jnp.where(odd, moved, v)


CHUNK = 512
STEP = 32
GSTEP = 16
AHEAD = 2


def core_kernel(*refs, width, length, shards, windows, flat_rows):
    n_in = 2 * SLOTS if windows else 1
    (x_ref, cot_ref, segr_ref, segc_ref) = refs[:4]
    w_refs = refs[4 : 4 + n_in]
    refs = refs[4 + n_in :]
    (y_ref, dx_ref) = refs[:2]
    n_out = 3 if windows else 1
    g_refs = refs[2 : 2 + n_out]
    (wide, wa, wi, wo, b1, vec, xb, qkv, ab, ctx, xh1, iv1, xh2, iv2, h1b, slope, df, da, dqkv, dc, dr1,
     bias, gb1, gvec, count_ref, sem) = refs[2 + n_out :]
    D = width
    T = length
    pairs = D // LANES
    flat = wide.at[pl.ds(0, flat_rows)]

    if windows:
        load_windows(w_refs, wide, flat, sem, shards)
    else:
        cp = pltpu.make_async_copy(w_refs[0], flat, sem.at[0])
        cp.start()
        cp.wait()
    unpack_weights(flat, wa, wi, wo, b1, vec, D)

    scale = 0.125
    bias[...] = jnp.where(segc_ref[...] == segr_ref[...], 0.0, -1e30).astype(F32)

    count_ref[0] = 1
    single = count_ref[0]

    def phase(body):
        def step(_, carry):
            body()
            return carry

        lax.fori_loop(0, single, step, 0)

    hidden = FF * REC * T // LANES

    def put(which, chunk, row, val):
        for j in range(CHUNK // LANES):
            at = which * hidden + (chunk * (CHUNK // LANES) + j) * REC * T
            wide[pl.ds(row + at, val.shape[0]), :] = val[:, j * LANES : (j + 1) * LANES]

    def get(which, chunk, row, n):
        at = [which * hidden + (chunk * (CHUNK // LANES) + j) * REC * T for j in range(CHUNK // LANES)]
        return jnp.concatenate([wide[pl.ds(row + k, n), :] for k in at], axis=1)

    def project(r):
        rows = pl.ds(pl.multiple_of(r * T, T), T)
        x16 = dx_ref[...].astype(BF)
        xb[rows, :] = x16
        for j in range(3):
            p = dot(x16, wa[:, j * D : (j + 1) * D])
            if j == 0:
                p = p + vec[0:1, :]
            if j == 2:
                p = p + vec[1:2, :]
            p = p.astype(BF)
            for c in range(pairs):
                qkv[r, j * pairs + c] = p[:, c * LANES : (c + 1) * LANES]

    def attend(r):
        rows = pl.ds(pl.multiple_of(r * T, T), T)

        def score(h):
            return dot_t(qkv[r, h // 2] * (lane_mask(h % 2, BF) * scale).astype(BF), qkv[r, pairs + h // 2])

        pend = [score(h) for h in range(AHEAD)]
        left = None
        for h in range(HEADS):
            if h + AHEAD < HEADS:
                pend.append(score(h + AHEAD))
            full = pend.pop(0)
            parts = []
            for i in range(0, T, STEP):
                sc = full[i : i + STEP] + bias[i : i + STEP, :]
                ex = jnp.exp(sc - jnp.max(sc, axis=-1, keepdims=True))
                tot = jnp.sum(ex, axis=-1, keepdims=True)
                parts.append((ex * (1.0 / tot)).astype(BF))
                ab[r * HEADS + h, pl.ds(i, STEP), :] = parts[-1]
            out = dot(jnp.concatenate(parts, axis=0), qkv[r, 2 * pairs + h // 2] * lane_mask(h % 2, BF))
            if h % 2 == 0:
                left = out
            else:
                ctx[h // 2, rows, :] = (left + out).astype(BF)

    def feed(r):
        rows = pl.ds(pl.multiple_of(r * T, T), T)
        a = dot(jnp.concatenate([ctx[c, rows, :] for c in range(pairs)], axis=1), wa[:, 3 * D : 4 * D])
        for i in range(0, T, STEP):
            sub = pl.ds(i, STEP)
            hat, inv = norm_stats(dx_ref[sub, :] + (a[i : i + STEP] + vec[2:3, :]))
            xh1[r, sub, :] = hat
            iv1[r, sub, :] = jnp.broadcast_to(inv, (STEP, LANES))
            h1b[pl.ds(pl.multiple_of(r * T, T) + i, STEP), :] = (hat * vec[4:5, :] + vec[5:6, :]).astype(BF)
        h16 = h1b[rows, :]

        def up(c):
            return dot(h16, wi[:, c * CHUNK : (c + 1) * CHUNK])

        pend = [up(0)]
        f = None
        for c in range(FF // CHUNK):
            cols = slice(c * CHUNK, (c + 1) * CHUNK)
            if c + 1 < FF // CHUNK:
                pend.append(up(c + 1))
            u = pend.pop(0)
            parts = []
            for i in range(0, T, GSTEP):
                g, sl = gelu_pair(u[i : i + GSTEP] + b1[:, cols])
                parts.append(g.astype(BF))
                put(0, c, pl.multiple_of(r * T, T) + i, parts[-1])
                slope[r, pl.ds(i, GSTEP), cols] = sl
            part = dot(jnp.concatenate(parts, axis=0), wo[cols, :])
            f = part if f is None else f + part
        for i in range(0, T, STEP):
            sub = pl.ds(i, STEP)
            h1 = xh1[r, sub, :] * vec[4:5, :] + vec[5:6, :]
            hat, inv = norm_stats(h1 + (f[i : i + STEP] + vec[3:4, :]))
            xh2[r, sub, :] = hat
            iv2[r, sub, :] = jnp.broadcast_to(inv, (STEP, LANES))
            y = hat * vec[6:7, :] + vec[7:8, :]
            dx_ref[sub, :] = y

    def acc(ref, row, val):
        ref[row : row + 1, :] = ref[row : row + 1, :] + val

    def feed_back(r):
        rows = pl.ds(pl.multiple_of(r * T, T), T)
        sums = [jnp.zeros((8, D), F32) for _ in range(6)]

        def add(k, val):
            sums[k] = sums[k] + jnp.sum(val.reshape(STEP // 8, 8, D), axis=0)

        for i in range(0, T, STEP):
            sub = pl.ds(i, STEP)
            dy = dx_ref[sub, :]
            hat = xh2[r, sub, :]
            add(0, dy * hat)
            add(1, dy)
            dr2 = norm_grad(dy, hat, iv2[r, sub, 0:1], vec[6:7, :])
            dr1[sub, :] = dr2
            d16 = dr2.astype(BF)
            df[pl.ds(pl.multiple_of(r * T, T) + i, STEP), :] = d16
            add(2, d16.astype(F32))
        d16 = df[rows, :]

        def down(c):
            return dot_t(d16, wo[c * CHUNK : (c + 1) * CHUNK, :])

        pend = [down(0)]
        dh = None
        for c in range(FF // CHUNK):
            cols = slice(c * CHUNK, (c + 1) * CHUNK)
            if c + 1 < FF // CHUNK:
                pend.append(down(c + 1))
            t = pend.pop(0)
            tot = jnp.zeros((8, CHUNK), F32)
            parts = []
            for i in range(0, T, GSTEP):
                g16 = (t[i : i + GSTEP].astype(BF).astype(F32) * slope[r, pl.ds(i, GSTEP), cols]).astype(BF)
                parts.append(g16)
                put(1, c, pl.multiple_of(r * T, T) + i, g16)
                tot = tot + jnp.sum(g16.astype(F32).reshape(GSTEP // 8, 8, CHUNK), axis=0)
            gb1[0:1, cols] = gb1[0:1, cols] + colsum(tot)
            part = dot_t(jnp.concatenate(parts, axis=0), wi[:, cols])
            dh = part if dh is None else dh + part
        for i in range(0, T, STEP):
            sub = pl.ds(i, STEP)
            hat = xh1[r, sub, :]
            upstream = dr1[sub, :] + dh[i : i + STEP]
            add(3, upstream * hat)
            add(4, upstream)
            d1 = norm_grad(upstream, hat, iv1[r, sub, 0:1], vec[4:5, :])
            dr1[sub, :] = d1
            a16 = d1.astype(BF)
            da[pl.ds(pl.multiple_of(r * T, T) + i, STEP), :] = a16
            add(5, a16.astype(F32))
        for row, k in ((6, 0), (7, 1), (3, 2), (4, 3), (5, 4), (2, 5)):
            acc(gvec, row, colsum(sums[k]))
        c16 = dot_t(da[rows, :], wa[:, 3 * D : 4 * D]).astype(BF)
        for c in range(pairs):
            dc[c] = c16[:, c * LANES : (c + 1) * LANES]

    def attend_back(r):
        rows = pl.ds(pl.multiple_of(r * T, T), T)

        def rise(h):
            return dot_t(dc[h // 2] * lane_mask(h % 2, BF), qkv[r, 2 * pairs + h // 2])

        pend = [rise(h) for h in range(AHEAD)]
        for h in range(HEADS):
            if h + AHEAD < HEADS:
                pend.append(rise(h + AHEAD))
            full = pend.pop(0)
            p, e = h // 2, h % 2
            half = slice(64 * e, 64 * e + 64)
            if e == 0:
                qt = jnp.transpose(qkv[r, p])
                ct = jnp.transpose(dc[p])
                dkt, dvt = [], []
            p16 = ab[r * HEADS + h]
            parts = []
            for i in range(0, T, STEP):
                pf = p16[i : i + STEP].astype(F32)
                t = full[i : i + STEP] * pf
                parts.append((t - pf * jnp.sum(t, axis=-1, keepdims=True)).astype(BF))
            s16 = jnp.concatenate(parts, axis=0)
            part = dot(s16, qkv[r, pairs + p] * lane_mask(e, BF))
            dkt.append(dot(qt[half], s16))
            dvt.append(dot(ct[half], p16))
            if e == 0:
                dq = part
            else:
                dqkv[p, rows, :] = ((dq + part) * scale).astype(BF)
                dqkv[pairs + p, rows, :] = jnp.transpose((jnp.concatenate(dkt, axis=0) * scale).astype(BF))
                dqkv[2 * pairs + p, rows, :] = jnp.transpose(jnp.concatenate(dvt, axis=0).astype(BF))
    def project_back(r):
        rows = pl.ds(pl.multiple_of(r * T, T), T)
        for c in range(pairs):
            cols = slice(c * LANES, (c + 1) * LANES)
            gvec[0:1, cols] = gvec[0:1, cols] + colsum(dqkv[c, rows, :].astype(F32))
            gvec[1:2, cols] = gvec[1:2, cols] + colsum(dqkv[2 * pairs + c, rows, :].astype(F32))
        d3 = jnp.concatenate([dqkv[c, rows, :] for c in range(3 * pairs)], axis=1)
        dx_ref[...] = dr1[...] + dot_t(d3, wa[:, : 3 * D])

    gb1[...] = jnp.zeros_like(gb1)
    gvec[...] = jnp.zeros_like(gvec)
    dx_ref[...] = x_ref[...].astype(F32)

    def forward(r, carry):
        for part in (project, attend, feed):
            phase(functools.partial(part, r))
        return carry

    def backward(i, carry):
        for part in (feed_back, attend_back, project_back):
            phase(functools.partial(part, REC - 1 - i))
        return carry

    lax.fori_loop(0, REC, forward, 0)
    y_ref[...] = dx_ref[...]
    dx_ref[...] = cot_ref[...].astype(F32)
    lax.fori_loop(0, REC, backward, 0)

    def grad_qkvo():
        xt = jnp.transpose(xb[...])
        for j in range(3):
            d3 = jnp.concatenate([dqkv[j * pairs + c] for c in range(pairs)], axis=1)
            wa[:, j * D : (j + 1) * D] = dot(xt, d3).astype(BF)
        for c in range(pairs):
            wa[c * LANES : (c + 1) * LANES, 3 * D : 4 * D] = t_dot(ctx[c], da[...]).astype(BF)

    def grad_in():
        ht = jnp.transpose(h1b[...])
        for c in range(FF // CHUNK):
            cols = slice(c * CHUNK, (c + 1) * CHUNK)
            wi[:, cols] = dot(ht, get(1, c, 0, REC * T)).astype(BF)

    def grad_out():
        for c in range(FF // CHUNK):
            cols = slice(c * CHUNK, (c + 1) * CHUNK)
            wo[cols, :] = t_dot(get(0, c, 0, REC * T), df[...]).astype(BF)

    phase(grad_qkvo)
    phase(grad_in)
    phase(grad_out)
    pack_weights(flat, wa, wi, wo, D)
    per_out = D // LANES
    rows = [gb1[0:1, c * LANES : (c + 1) * LANES] for c in range(FF // LANES)]
    for r in range(8):
        rows = rows + [gvec[r : r + 1, c * LANES : (c + 1) * LANES] for c in range(per_out)]
    tail = jnp.concatenate(rows, axis=0)
    flat[flat.shape[0] - len(rows) : flat.shape[0], :] = tail.astype(BF)
    if windows:
        store_windows(g_refs, wide, flat, sem, shards, tail[FF // LANES :])
    else:
        cp = pltpu.make_async_copy(flat, g_refs[0], sem.at[0])
        cp.start()
        cp.wait()


def core(x, cot, seg, flats, windows, shards, rows):
    T, D = x.shape
    vm = pltpu.VMEM
    pairs = D // LANES
    scratch = [
        vm((max(2 * FF * REC * T // LANES, rows + TILE + 2 * TILE * shards), LANES), BF),
        vm((D, 4 * D), BF), vm((D, FF), BF), vm((FF, D), BF), vm((1, FF), F32), vm((8, D), F32),
        vm((REC * T, D), BF), vm((REC, 3 * pairs, T, LANES), BF), vm((REC * HEADS, T, T), BF), vm((pairs, REC * T, LANES), BF),
        vm((REC, T, D), F32), vm((REC, T, LANES), F32), vm((REC, T, D), F32), vm((REC, T, LANES), F32),
        vm((REC * T, D), BF), vm((REC, T, FF), F32),
        vm((REC * T, D), BF), vm((REC * T, D), BF), vm((3 * pairs, REC * T, LANES), BF), vm((pairs, T, LANES), BF),
        vm((T, D), F32), vm((T, T), F32),
        vm((1, FF), F32), vm((8, D), F32),
        pltpu.SMEM((1,), jnp.int32), pltpu.SemaphoreType.DMA((8,)),
    ]
    if windows:
        g_shapes = [jax.ShapeDtypeStruct((n, flats[0].shape[0], LANES), BF) for n in (SLOTS, SLOTS // 2, SLOTS // 2)]
    else:
        g_shapes = [jax.ShapeDtypeStruct((rows, LANES), BF)]
    in_vmem = pl.BlockSpec(memory_space=pltpu.VMEM)
    anywhere = pl.BlockSpec(memory_space=pl.ANY)
    return pl.pallas_call(
        functools.partial(core_kernel, width=D, length=T, shards=shards, windows=windows, flat_rows=rows),
        out_shape=tuple([jax.ShapeDtypeStruct((T, D), F32)] * 2 + g_shapes),
        in_specs=[in_vmem] * 4 + [anywhere] * len(flats),
        out_specs=tuple([in_vmem] * 2 + [anywhere] * len(g_shapes)),
        scratch_shapes=scratch,
        compiler_params=pltpu.CompilerParams(vmem_limit_bytes=59 * 1024 * 1024),
        name="layer_core",
    )(x, cot, seg.reshape(1, T), seg.reshape(T, 1), *flats)


AXES = ("dp", "rep")


def exchange(v, step):
    count = lax.axis_size("dp") * lax.axis_size("rep")
    zero, one = STEPS[step] if step < len(STEPS) else (RC, RC)
    return lax.ppermute(v, AXES, [(j, j ^ (one if j // RC & 1 else zero)) for j in range(count)])


def gather_windows(own):
    planes = [own, exchange(own, 3), exchange(own, 2)]
    planes.append(exchange(planes[1], 2))
    near = [None] * SLOTS
    for m, v in enumerate(planes):
        side = exchange(v, 0)
        near[m], near[8 + m], near[4 + m], near[12 + m] = v, side, exchange(v, 1), exchange(side, 1)
    return near + [exchange(v, 4) for v in near]


def total(*parts):
    v = parts[0].astype(F32)
    for part in parts[1:]:
        v = v + part.astype(F32)
    return v.astype(BF)


def sum_windows(keep, sent_first, sent_last):
    half = SLOTS // 2
    first, last = exchange(sent_first, 4), exchange(sent_last, 4)
    sums = {}
    for m in (3, 1, 2, 0):
        far = exchange(total(keep[half + 4 + m], first[4 + m]), 0)
        side = exchange(total(keep[half + m], first[m]), 0)
        far = exchange(total(keep[4 + m], last[4 + m], far), 1)
        sums[m] = (keep[m], last[m], side, far)
    turn = exchange(total(*sums[3]), 2)
    one = exchange(total(*sums[1], turn), 3)
    two = exchange(total(*sums[2]), 2)
    return (*sums[0], one, two)


def shards_fn(block_input, segment_ids, cotangent, master_weights, momentum, weight_average):
    width = block_input.shape[2]
    length = block_input.shape[1]
    count = lax.axis_size("dp") * lax.axis_size("rep")
    share = master_weights.shape[0]
    rows = share * count // LANES
    tiles = rows // TILE
    vec_len = 8 * width // count
    args = (block_input[0], cotangent[0], segment_ids[0])
    in_vmem = pl.BlockSpec(memory_space=pltpu.VMEM)
    if count == 32:
        window = (tiles // count + 2) * TILE
        padded = jnp.pad(master_weights, (0, window * LANES - share)).reshape(window, LANES)
        packed = pl.pallas_call(
            pack_kernel, out_shape=jax.ShapeDtypeStruct((window, LANES), BF), in_specs=[in_vmem], out_specs=in_vmem, name="pack_shard"
        )(padded)
        block_output, input_grad, *sums = core(*args, gather_windows(packed), True, count, rows)
        addends = sum_windows(*sums)
        grad, tail = pl.pallas_call(
            finish_kernel,
            out_shape=(jax.ShapeDtypeStruct((window, LANES), F32), jax.ShapeDtypeStruct((8, LANES), F32)),
            in_specs=[in_vmem] * len(addends),
            out_specs=(in_vmem, in_vmem),
            name="finish_shard",
        )(*addends)
        weight_grad = grad.reshape(-1)[:share]
        vector_grad = tail[7]
    else:
        flat = lax.all_gather(master_weights.astype(BF), AXES, axis=0, tiled=True).reshape(rows, LANES)
        block_output, input_grad, grad = core(*args, [flat], False, count, rows)
        grad = grad.reshape(-1).astype(F32)
        weight_grad = lax.psum_scatter(grad, AXES, scatter_dimension=0, tiled=True)
        vector_grad = lax.psum_scatter(grad[grad.shape[0] - 8 * width :], AXES, scatter_dimension=0, tiled=True)
    token_count = block_input.shape[0] * length * count
    rate = rate_base / math.sqrt(token_count)
    new_momentum = mom_decay * momentum + weight_grad
    new_weights = master_weights - rate * (weight_grad + mom_decay * new_momentum)
    new_average = avg_keep * weight_average + (1.0 - avg_keep) * new_weights
    return (
        block_output[None],
        input_grad[None],
        weight_grad,
        vector_grad,
        new_momentum,
        new_average,
        new_weights,
    )


def solution(mesh):
    three = P(AXES, None, None)
    two = P(AXES, None)
    one = P(AXES)
    return jax.shard_map(
        shards_fn,
        mesh=mesh,
        in_specs=(three, two, three, one, one, one),
        out_specs=(three, three, one, one, one, one, one),
        check_vma=False,
    )
```

```python
import functools
import math

import jax
import jax.numpy as jnp
from jax import lax
from jax.experimental import pallas as pl
from jax.experimental.pallas import tpu as pltpu
from jax.sharding import PartitionSpec as P

FF = 2048
HEADS = 8
REC = 2
TILE = 16
LANES = 128

norm_eps = 1e-05
mom_decay = 0.9
avg_keep = 0.8
rate_base = 0.006

BF = jnp.bfloat16
F32 = jnp.float32


def dot(a, b):
    return lax.dot_general(a, b, (((1,), (0,)), ((), ())), preferred_element_type=F32)


def dot_t(a, b):
    return lax.dot_general(a, b, (((1,), (1,)), ((), ())), preferred_element_type=F32)


def t_dot(a, b):
    return lax.dot_general(a, b, (((0,), (0,)), ((), ())), preferred_element_type=F32)


def one_hot_swap(outer, inner):
    size = outer * inner
    row = lax.broadcasted_iota(jnp.int32, (size, size), 0)
    col = lax.broadcasted_iota(jnp.int32, (size, size), 1)
    shift = inner.bit_length() - 1
    want = (row & (inner - 1)) * outer + (row >> shift)
    return jnp.where(col == want, 1.0, 0.0).astype(F32).astype(BF)


def matrix_blocks(wa, wi, wo, width):
    per = 4 * width // LANES
    base = 0
    for ref, per in ((wa, per), (wi, FF // LANES), (wo, width // LANES)):
        yield ref, per, base
        base = base + ref.shape[0] * per


def unpack_weights(flat, wa, wi, wo, b1, vec, width):
    for ref, per, base in matrix_blocks(wa, wi, wo, width):
        n = 256 // per
        swap = one_hot_swap(per, n)

        def body(g, carry, ref=ref, per=per, base=base, n=n, swap=swap):
            first = flat[pl.ds(pl.multiple_of(base + g * 512, 512), 256), :]
            second = flat[pl.ds(pl.multiple_of(base + g * 512, 512) + 256, 256), :]
            out = dot(swap, jnp.concatenate([first, second], axis=1)).astype(BF)
            row = pl.multiple_of(g * 2 * n, 2 * n)
            for c in range(per):
                piece = out[c * n : (c + 1) * n]
                cols = slice(c * LANES, (c + 1) * LANES)
                ref[pl.ds(row, 2 * n), cols] = jnp.concatenate([piece[:, :LANES], piece[:, LANES:]], axis=0)
            return carry

        lax.fori_loop(0, ref.shape[0] * per // 512, body, 0, unroll=8)
    per_out = width // LANES
    tail = flat[flat.shape[0] - FF // LANES - 8 * per_out : flat.shape[0], :].astype(F32)
    for c in range(FF // LANES):
        b1[0:1, c * LANES : (c + 1) * LANES] = tail[c : c + 1]
    for r in range(8):
        for c in range(per_out):
            k = FF // LANES + r * per_out + c
            vec[r : r + 1, c * LANES : (c + 1) * LANES] = tail[k : k + 1]


def pack_weights(flat, wa, wi, wo, width):
    for ref, per, base in matrix_blocks(wa, wi, wo, width):
        n = 256 // per
        swap = one_hot_swap(n, per)

        def body(g, carry, ref=ref, per=per, base=base, n=n, swap=swap):
            row = pl.multiple_of(g * 2 * n, 2 * n)
            pieces = []
            for c in range(per):
                v = ref[pl.ds(row, 2 * n), c * LANES : (c + 1) * LANES]
                pieces.append(jnp.concatenate([v[:n], v[n:]], axis=1))
            out = dot(swap, jnp.concatenate(pieces, axis=0)).astype(BF)
            first = pl.multiple_of(base + g * 512, 512)
            flat[pl.ds(first, 256), :] = out[:, :LANES]
            flat[pl.ds(first + 256, 256), :] = out[:, LANES:]
            return carry

        lax.fori_loop(0, ref.shape[0] * per // 512, body, 0, unroll=8)


def norm_stats(resid):
    center = resid - jnp.mean(resid, axis=-1, keepdims=True)
    variance = jnp.mean(center * center, axis=-1, keepdims=True)
    inv = lax.rsqrt(variance + norm_eps)
    return center * inv, inv


def norm_grad(upstream, normed, inv, gain):
    scaled = upstream * gain
    m0 = jnp.mean(scaled, axis=-1, keepdims=True)
    m1 = jnp.mean(scaled * normed, axis=-1, keepdims=True)
    return inv * (scaled - m0 - normed * m1)


def colsum(v):
    return jnp.sum(v, axis=0, keepdims=True)


def lane_mask(which, dtype):
    lane = lax.broadcasted_iota(jnp.int32, (1, LANES), 1)
    keep = (lane < 64) if which == 0 else (lane >= 64)
    return jnp.where(keep, 1.0, 0.0).astype(F32).astype(dtype)


C0 = math.sqrt(2.0 / math.pi)


def gelu_pair(u):
    u2 = u * u
    inner = u * (C0 + (C0 * 0.044715) * u2)
    half = 0.5 + 0.5 * jnp.tanh(inner)
    g = u * half
    slope = half + 2.0 * g * (1.0 - half) * (C0 + (3.0 * C0 * 0.044715) * u2)
    return g, slope


def window_starts(shards, tiles):
    return [i * tiles // shards for i in range(shards + 1)]


def own_index():
    return lax.axis_index("dp") * lax.axis_size("rep") + lax.axis_index("rep")


RZ, RX, RC, RY = 8, 4, 2, 1
STEPS = ((RX, RY), (RY, RX), (2 * RZ, RZ), (RZ, 2 * RZ))
SLOTS = 1 << len(STEPS)
PLANES = (3, 2, 1, 0)


def own_core(me):
    return (me // RC) & 1


def slot_owner(base, core, slot):
    owner = base
    for k, (zero, one) in enumerate(STEPS):
        if slot >> (len(STEPS) - 1 - k) & 1:
            owner = jnp.bitwise_xor(owner, jnp.where(core == 0, zero, one))
    return owner


def settle(ref, rows, sem):
    pltpu.make_async_copy(ref.at[pl.ds(0, rows)], ref.at[pl.ds(0, rows)], sem).wait()


def window_moves(owner, height, tiles, shards, edge_row):
    start = pl.multiple_of((owner * tiles // shards) * TILE, TILE)
    edge = pl.multiple_of(edge_row + owner * 2 * TILE, TILE)
    body = height - 2 * TILE
    return [(0, start, body), (body, edge, 2 * TILE)]


def load_windows(w_refs, wide, flat, sem, shards):
    tiles = flat.shape[0] // TILE
    height = w_refs[0].shape[0]
    edge_row = flat.shape[0] + TILE
    base = tiles // shards * TILE
    me = own_index()
    core = own_core(me)
    for n, ref in enumerate(w_refs):
        side, origin = (core, me) if n < SLOTS else (1 - core, jnp.bitwise_xor(me, RC))
        owner = slot_owner(origin, side, n % SLOTS)
        for at, to, rows in window_moves(owner, height, tiles, shards, edge_row):
            pltpu.make_async_copy(ref.at[pl.ds(at, rows)], wide.at[pl.ds(to, rows)], sem.at[0]).start()
    settle(wide, height * shards, sem.at[0])
    starts = window_starts(shards, tiles)

    def tile(row):
        return wide[row : row + TILE, :]

    for i in range(shards):
        nxt = starts[i + 1]
        row = edge_row + i * 2 * TILE
        if nxt - starts[i] != base // TILE:
            wide[(nxt - 1) * TILE : nxt * TILE, :] = tile(row)
            row = row + TILE
        if i + 1 < shards:
            wide[nxt * TILE : (nxt + 1) * TILE, :] = tile(nxt * TILE) + tile(row)


def store_windows(g_refs, wide, flat, sem, shards, vec_rows):
    tiles = flat.shape[0] // TILE
    height = g_refs[0].shape[1]
    edge_row = flat.shape[0] + TILE
    starts = window_starts(shards, tiles)
    last = lax.broadcasted_iota(jnp.int32, (TILE, LANES), 0) == TILE - 1
    for i in range(shards):
        low = starts[i] * TILE + height - 2 * TILE
        row = edge_row + i * 2 * TILE
        for k in range(2):
            at = low + k * TILE
            if at + TILE <= flat.shape[0]:
                tile = wide[at : at + TILE, :]
            else:
                tile = jnp.zeros((TILE, LANES), BF)
            if k == 1:
                tile = jnp.where(last, vec_rows[i : i + 1], tile.astype(F32)).astype(BF)
            wide[row + k * TILE : row + (k + 1) * TILE, :] = tile
    me = own_index()
    core = own_core(me)
    for n, ref in enumerate(g_refs):
        side, origin = (core, me) if n == 0 else (1 - core, jnp.bitwise_xor(me, RC))
        for k in range(ref.shape[0]):
            slot = k if n == 0 else 4 * k + PLANES[n - 1]
            owner = slot_owner(origin, side, slot)
            for at, to, rows in window_moves(owner, height, tiles, shards, edge_row):
                pltpu.make_async_copy(wide.at[pl.ds(to, rows)], ref.at[k].at[pl.ds(at, rows)], sem.at[n]).start()
    for n, ref in enumerate(g_refs):
        settle(wide, ref.shape[0] * ref.shape[1], sem.at[n])


CHUNK = 512
STEP = 32
GSTEP = 16
AHEAD = 2


def core_kernel(*refs, width, length, shards, windows, flat_rows):
    n_in = 2 * SLOTS if windows else 1
    (x_ref, cot_ref, seg_ref) = refs[:3]
    w_refs = refs[3 : 3 + n_in]
    refs = refs[3 + n_in :]
    (y_ref, dx_ref) = refs[:2]
    n_out = 1 + len(PLANES) if windows else 1
    g_refs = refs[2 : 2 + n_out]
    (wide, wa, wi, wo, b1, vec, xb, qkv, ab, ctx, xh1, iv1, xh2, iv2, h1b, slope, df, da, dqkv, dc, dr1,
     bias, gb1, gvec, count_ref, sem) = refs[2 + n_out :]
    D = width
    T = length
    pairs = D // LANES
    flat = wide.at[pl.ds(0, flat_rows)]

    if windows:
        load_windows(w_refs, wide, flat, sem, shards)
    else:
        cp = pltpu.make_async_copy(w_refs[0], flat, sem.at[0])
        cp.start()
        cp.wait()
    unpack_weights(flat, wa, wi, wo, b1, vec, D)

    scale = 0.125
    seg = seg_ref[...].astype(F32)
    column = jnp.transpose(jnp.broadcast_to(seg, (LANES, T)))[:, 0:1]
    bias[...] = jnp.where(column == seg, 0.0, -1e30).astype(F32)

    count_ref[0] = 1
    single = count_ref[0]

    def phase(body):
        def step(_, carry):
            body()
            return carry

        lax.fori_loop(0, single, step, 0)

    hidden = FF * REC * T // LANES

    def put(which, chunk, row, val):
        for j in range(CHUNK // LANES):
            at = which * hidden + (chunk * (CHUNK // LANES) + j) * REC * T
            wide[pl.ds(row + at, val.shape[0]), :] = val[:, j * LANES : (j + 1) * LANES]

    def get(which, chunk, row, n):
        at = [which * hidden + (chunk * (CHUNK // LANES) + j) * REC * T for j in range(CHUNK // LANES)]
        return jnp.concatenate([wide[pl.ds(row + k, n), :] for k in at], axis=1)

    def project(r):
        rows = pl.ds(pl.multiple_of(r * T, T), T)
        x16 = dx_ref[...].astype(BF)
        xb[rows, :] = x16
        for j in range(3):
            p = dot(x16, wa[:, j * D : (j + 1) * D])
            if j == 0:
                p = p + vec[0:1, :]
            if j == 2:
                p = p + vec[1:2, :]
            p = p.astype(BF)
            for c in range(pairs):
                qkv[r, j * pairs + c] = p[:, c * LANES : (c + 1) * LANES]

    def attend(r):
        rows = pl.ds(pl.multiple_of(r * T, T), T)

        def score(h):
            return dot_t(qkv[r, h // 2] * (lane_mask(h % 2, BF) * scale).astype(BF), qkv[r, pairs + h // 2])

        pend = [score(h) for h in range(AHEAD)]
        left = None
        for h in range(HEADS):
            if h + AHEAD < HEADS:
                pend.append(score(h + AHEAD))
            full = pend.pop(0)
            parts = []
            for i in range(0, T, STEP):
                sc = full[i : i + STEP] + bias[i : i + STEP, :]
                ex = jnp.exp(sc - jnp.max(sc, axis=-1, keepdims=True))
                tot = jnp.sum(ex, axis=-1, keepdims=True)
                parts.append((ex * (1.0 / tot)).astype(BF))
                ab[r * HEADS + h, pl.ds(i, STEP), :] = parts[-1]
            out = dot(jnp.concatenate(parts, axis=0), qkv[r, 2 * pairs + h // 2] * lane_mask(h % 2, BF))
            if h % 2 == 0:
                left = out
            else:
                ctx[h // 2, rows, :] = (left + out).astype(BF)

    def feed(r):
        rows = pl.ds(pl.multiple_of(r * T, T), T)
        a = dot(jnp.concatenate([ctx[c, rows, :] for c in range(pairs)], axis=1), wa[:, 3 * D : 4 * D])
        for i in range(0, T, STEP):
            sub = pl.ds(i, STEP)
            hat, inv = norm_stats(dx_ref[sub, :] + (a[i : i + STEP] + vec[2:3, :]))
            xh1[r, sub, :] = hat
            iv1[r, sub, :] = jnp.broadcast_to(inv, (STEP, LANES))
            h1b[pl.ds(pl.multiple_of(r * T, T) + i, STEP), :] = (hat * vec[4:5, :] + vec[5:6, :]).astype(BF)
        h16 = h1b[rows, :]

        def up(c):
            return dot(h16, wi[:, c * CHUNK : (c + 1) * CHUNK])

        pend = [up(0)]
        f = None
        for c in range(FF // CHUNK):
            cols = slice(c * CHUNK, (c + 1) * CHUNK)
            if c + 1 < FF // CHUNK:
                pend.append(up(c + 1))
            u = pend.pop(0)
            parts = []
            for i in range(0, T, GSTEP):
                g, sl = gelu_pair(u[i : i + GSTEP] + b1[:, cols])
                parts.append(g.astype(BF))
                put(0, c, pl.multiple_of(r * T, T) + i, parts[-1])
                slope[r, pl.ds(i, GSTEP), cols] = sl
            part = dot(jnp.concatenate(parts, axis=0), wo[cols, :])
            f = part if f is None else f + part
        for i in range(0, T, STEP):
            sub = pl.ds(i, STEP)
            h1 = xh1[r, sub, :] * vec[4:5, :] + vec[5:6, :]
            hat, inv = norm_stats(h1 + (f[i : i + STEP] + vec[3:4, :]))
            xh2[r, sub, :] = hat
            iv2[r, sub, :] = jnp.broadcast_to(inv, (STEP, LANES))
            y = hat * vec[6:7, :] + vec[7:8, :]
            dx_ref[sub, :] = y

    def acc(ref, row, val):
        ref[row : row + 1, :] = ref[row : row + 1, :] + val

    def feed_back(r):
        rows = pl.ds(pl.multiple_of(r * T, T), T)
        sums = [jnp.zeros((8, D), F32) for _ in range(6)]

        def add(k, val):
            sums[k] = sums[k] + jnp.sum(val.reshape(STEP // 8, 8, D), axis=0)

        for i in range(0, T, STEP):
            sub = pl.ds(i, STEP)
            dy = dx_ref[sub, :]
            hat = xh2[r, sub, :]
            add(0, dy * hat)
            add(1, dy)
            dr2 = norm_grad(dy, hat, iv2[r, sub, 0:1], vec[6:7, :])
            dr1[sub, :] = dr2
            d16 = dr2.astype(BF)
            df[pl.ds(pl.multiple_of(r * T, T) + i, STEP), :] = d16
            add(2, d16.astype(F32))
        d16 = df[rows, :]

        def down(c):
            return dot_t(d16, wo[c * CHUNK : (c + 1) * CHUNK, :])

        pend = [down(0)]
        dh = None
        for c in range(FF // CHUNK):
            cols = slice(c * CHUNK, (c + 1) * CHUNK)
            if c + 1 < FF // CHUNK:
                pend.append(down(c + 1))
            t = pend.pop(0)
            tot = jnp.zeros((8, CHUNK), F32)
            parts = []
            for i in range(0, T, GSTEP):
                g16 = (t[i : i + GSTEP].astype(BF).astype(F32) * slope[r, pl.ds(i, GSTEP), cols]).astype(BF)
                parts.append(g16)
                put(1, c, pl.multiple_of(r * T, T) + i, g16)
                tot = tot + jnp.sum(g16.astype(F32).reshape(GSTEP // 8, 8, CHUNK), axis=0)
            gb1[0:1, cols] = gb1[0:1, cols] + colsum(tot)
            part = dot_t(jnp.concatenate(parts, axis=0), wi[:, cols])
            dh = part if dh is None else dh + part
        for i in range(0, T, STEP):
            sub = pl.ds(i, STEP)
            hat = xh1[r, sub, :]
            upstream = dr1[sub, :] + dh[i : i + STEP]
            add(3, upstream * hat)
            add(4, upstream)
            d1 = norm_grad(upstream, hat, iv1[r, sub, 0:1], vec[4:5, :])
            dr1[sub, :] = d1
            a16 = d1.astype(BF)
            da[pl.ds(pl.multiple_of(r * T, T) + i, STEP), :] = a16
            add(5, a16.astype(F32))
        for row, k in ((6, 0), (7, 1), (3, 2), (4, 3), (5, 4), (2, 5)):
            acc(gvec, row, colsum(sums[k]))
        c16 = dot_t(da[rows, :], wa[:, 3 * D : 4 * D]).astype(BF)
        for c in range(pairs):
            dc[c] = c16[:, c * LANES : (c + 1) * LANES]

    def attend_back(r):
        rows = pl.ds(pl.multiple_of(r * T, T), T)

        def rise(h):
            return dot_t(dc[h // 2] * lane_mask(h % 2, BF), qkv[r, 2 * pairs + h // 2])

        pend = [rise(h) for h in range(AHEAD)]
        for h in range(HEADS):
            if h + AHEAD < HEADS:
                pend.append(rise(h + AHEAD))
            full = pend.pop(0)
            p, e = h // 2, h % 2
            half = slice(64 * e, 64 * e + 64)
            if e == 0:
                qt = jnp.transpose(qkv[r, p])
                ct = jnp.transpose(dc[p])
                dkt, dvt = [], []
            p16 = ab[r * HEADS + h]
            parts = []
            for i in range(0, T, STEP):
                pf = p16[i : i + STEP].astype(F32)
                t = full[i : i + STEP] * pf
                parts.append((t - pf * jnp.sum(t, axis=-1, keepdims=True)).astype(BF))
            s16 = jnp.concatenate(parts, axis=0)
            part = dot(s16, qkv[r, pairs + p] * lane_mask(e, BF))
            dkt.append(dot(qt[half], s16))
            dvt.append(dot(ct[half], p16))
            if e == 0:
                dq = part
            else:
                dqkv[p, rows, :] = ((dq + part) * scale).astype(BF)
                dqkv[pairs + p, rows, :] = jnp.transpose((jnp.concatenate(dkt, axis=0) * scale).astype(BF))
                dqkv[2 * pairs + p, rows, :] = jnp.transpose(jnp.concatenate(dvt, axis=0).astype(BF))
    def project_back(r):
        rows = pl.ds(pl.multiple_of(r * T, T), T)
        for c in range(pairs):
            cols = slice(c * LANES, (c + 1) * LANES)
            gvec[0:1, cols] = gvec[0:1, cols] + colsum(dqkv[c, rows, :].astype(F32))
            gvec[1:2, cols] = gvec[1:2, cols] + colsum(dqkv[2 * pairs + c, rows, :].astype(F32))
        d3 = jnp.concatenate([dqkv[c, rows, :] for c in range(3 * pairs)], axis=1)
        dx_ref[...] = dr1[...] + dot_t(d3, wa[:, : 3 * D])

    gb1[...] = jnp.zeros_like(gb1)
    gvec[...] = jnp.zeros_like(gvec)
    dx_ref[...] = x_ref[...].astype(F32)

    def forward(r, carry):
        for part in (project, attend, feed):
            phase(functools.partial(part, r))
        return carry

    def backward(i, carry):
        for part in (feed_back, attend_back, project_back):
            phase(functools.partial(part, REC - 1 - i))
        return carry

    lax.fori_loop(0, REC, forward, 0)
    y_ref[...] = dx_ref[...]
    dx_ref[...] = cot_ref[...].astype(F32)
    lax.fori_loop(0, REC, backward, 0)

    def grad_qkvo():
        xt = jnp.transpose(xb[...])
        for j in range(3):
            d3 = jnp.concatenate([dqkv[j * pairs + c] for c in range(pairs)], axis=1)
            wa[:, j * D : (j + 1) * D] = dot(xt, d3).astype(BF)
        for c in range(pairs):
            wa[c * LANES : (c + 1) * LANES, 3 * D : 4 * D] = t_dot(ctx[c], da[...]).astype(BF)

    def grad_in():
        ht = jnp.transpose(h1b[...])
        for c in range(FF // CHUNK):
            cols = slice(c * CHUNK, (c + 1) * CHUNK)
            wi[:, cols] = dot(ht, get(1, c, 0, REC * T)).astype(BF)

    def grad_out():
        for c in range(FF // CHUNK):
            cols = slice(c * CHUNK, (c + 1) * CHUNK)
            wo[cols, :] = t_dot(get(0, c, 0, REC * T), df[...]).astype(BF)

    phase(grad_qkvo)
    phase(grad_in)
    phase(grad_out)
    pack_weights(flat, wa, wi, wo, D)
    per_out = D // LANES
    rows = [gb1[0:1, c * LANES : (c + 1) * LANES] for c in range(FF // LANES)]
    for r in range(8):
        rows = rows + [gvec[r : r + 1, c * LANES : (c + 1) * LANES] for c in range(per_out)]
    tail = jnp.concatenate(rows, axis=0)
    flat[flat.shape[0] - len(rows) : flat.shape[0], :] = tail.astype(BF)
    if windows:
        store_windows(g_refs, wide, flat, sem, shards, tail[FF // LANES :])
    else:
        cp = pltpu.make_async_copy(flat, g_refs[0], sem.at[0])
        cp.start()
        cp.wait()


def core(x, cot, seg, flats, windows, shards, rows):
    T, D = x.shape
    vm = pltpu.VMEM
    pairs = D // LANES
    scratch = [
        vm((max(2 * FF * REC * T // LANES, rows + TILE + 2 * TILE * shards), LANES), BF),
        vm((D, 4 * D), BF), vm((D, FF), BF), vm((FF, D), BF), vm((1, FF), F32), vm((8, D), F32),
        vm((REC * T, D), BF), vm((REC, 3 * pairs, T, LANES), BF), vm((REC * HEADS, T, T), BF), vm((pairs, REC * T, LANES), BF),
        vm((REC, T, D), F32), vm((REC, T, LANES), F32), vm((REC, T, D), F32), vm((REC, T, LANES), F32),
        vm((REC * T, D), BF), vm((REC, T, FF), F32),
        vm((REC * T, D), BF), vm((REC * T, D), BF), vm((3 * pairs, REC * T, LANES), BF), vm((pairs, T, LANES), BF),
        vm((T, D), F32), vm((T, T), F32),
        vm((1, FF), F32), vm((8, D), F32),
        pltpu.SMEM((1,), jnp.int32), pltpu.SemaphoreType.DMA((8,)),
    ]
    if windows:
        g_shapes = [jax.ShapeDtypeStruct((n, flats[0].shape[0], LANES), BF) for n in (SLOTS, 4, 4, 4, 4)]
    else:
        g_shapes = [jax.ShapeDtypeStruct((rows, LANES), BF)]
    in_vmem = pl.BlockSpec(memory_space=pltpu.VMEM)
    anywhere = pl.BlockSpec(memory_space=pl.ANY)
    return pl.pallas_call(
        functools.partial(core_kernel, width=D, length=T, shards=shards, windows=windows, flat_rows=rows),
        out_shape=tuple([jax.ShapeDtypeStruct((T, D), F32)] * 2 + g_shapes),
        in_specs=[in_vmem] * 3 + [anywhere] * len(flats),
        out_specs=tuple([in_vmem] * 2 + [anywhere] * len(g_shapes)),
        scratch_shapes=scratch,
        compiler_params=pltpu.CompilerParams(vmem_limit_bytes=59 * 1024 * 1024),
        name="layer_core",
    )(x, cot, seg, *flats)


AXES = ("dp", "rep")


def exchange(v, step):
    count = lax.axis_size("dp") * lax.axis_size("rep")
    zero, one = STEPS[step] if step < len(STEPS) else (RC, RC)
    return lax.ppermute(v, AXES, [(j, j ^ (one if j // RC & 1 else zero)) for j in range(count)])


def after(v, earlier):
    return lax.optimization_barrier((v, earlier))[0]


def gather_windows(own):
    next_plane = exchange(own, 3)
    near = [None] * SLOTS
    planes = [own, next_plane, exchange(after(own, next_plane), 2), exchange(next_plane, 2)]
    for m, v in enumerate(planes):
        side = exchange(v, 0)
        near[m], near[8 + m], near[4 + m], near[12 + m] = v, side, exchange(v, 1), exchange(side, 1)
    return near + [exchange(v, 4) for v in near]


def total(*parts):
    v = parts[0].astype(F32)
    for part in parts[1:]:
        v = v + part.astype(F32)
    return v.astype(BF)


def sum_windows(keep, *sent):
    got = {m: exchange(v, 4) for m, v in zip(PLANES, sent)}
    far, side, back, last = {}, {}, {}, [None]

    def add(*parts):
        if last[0] is not None:
            parts = (*parts[:-1], after(parts[-1], last[0]))
        last[0] = total(*parts)
        return last[0]

    def near_far(m):
        far[m] = exchange(add(keep[12 + m], got[m][3]), 0)
        side[m] = exchange(add(keep[8 + m], got[m][2]), 0)

    def second(m):
        back[m] = exchange(add(keep[4 + m], got[m][1], far[m]), 1)

    def plane(m):
        return (keep[m], got[m][0], side[m], back[m])

    near_far(3)
    near_far(2)
    second(3)
    second(2)
    near_far(1)
    turn = exchange(add(*plane(3)), 2)
    two = exchange(add(*plane(2)), 2)
    near_far(0)
    second(1)
    second(0)
    one = exchange(add(*plane(1), turn), 3)
    return (*plane(0), one, two)


def shards_fn(block_input, segment_ids, cotangent, master_weights, momentum, weight_average):
    width = block_input.shape[2]
    length = block_input.shape[1]
    count = lax.axis_size("dp") * lax.axis_size("rep")
    share = master_weights.shape[0]
    rows = share * count // LANES
    tiles = rows // TILE
    args = (block_input[0], cotangent[0], segment_ids)
    if count == 32:
        window = (tiles // count + 2) * TILE
        first = (own_index() * share) % (TILE * LANES)
        padded = jnp.pad(master_weights, (TILE * LANES, window * LANES - share))
        own = lax.dynamic_slice(padded, (TILE * LANES - first,), (window * LANES,)).astype(BF).reshape(window, LANES)
        block_output, input_grad, *sums = core(*args, gather_windows(own), True, count, rows)
        addends = sum_windows(*sums)
        grad = addends[0].astype(F32)
        for addend in addends[1:]:
            grad = grad + addend.astype(F32)
        weight_grad = lax.dynamic_slice(grad.reshape(-1), (first,), (share,))
        vector_grad = grad[window - 1]
    else:
        flat = lax.all_gather(master_weights.astype(BF), AXES, axis=0, tiled=True).reshape(rows, LANES)
        block_output, input_grad, grad = core(*args, [flat], False, count, rows)
        grad = grad.reshape(-1).astype(F32)
        weight_grad = lax.psum_scatter(grad, AXES, scatter_dimension=0, tiled=True)
        vector_grad = lax.psum_scatter(grad[grad.shape[0] - 8 * width :], AXES, scatter_dimension=0, tiled=True)
    token_count = block_input.shape[0] * length * count
    rate = rate_base / math.sqrt(token_count)
    new_momentum = mom_decay * momentum + weight_grad
    new_weights = master_weights - rate * (weight_grad + mom_decay * new_momentum)
    new_average = avg_keep * weight_average + (1.0 - avg_keep) * new_weights
    return (
        block_output[None],
        input_grad[None],
        weight_grad,
        vector_grad,
        new_momentum,
        new_average,
        new_weights,
    )


def solution(mesh):
    three = P(AXES, None, None)
    two = P(AXES, None)
    one = P(AXES)
    return jax.shard_map(
        shards_fn,
        mesh=mesh,
        in_specs=(three, two, three, one, one, one),
        out_specs=(three, three, one, one, one, one, one),
        check_vma=False,
    )
```

```python
import functools
import math

import jax
import jax.numpy as jnp
from jax import lax
from jax.experimental import pallas as pl
from jax.experimental.pallas import tpu as pltpu
from jax.sharding import PartitionSpec as P

FF = 2048
HEADS = 8
REC = 2
TILE = 8
LANES = 128

norm_eps = 1e-05
mom_decay = 0.9
avg_keep = 0.8
rate_base = 0.006

BF = jnp.bfloat16
F32 = jnp.float32


def dot(a, b):
    return lax.dot_general(a, b, (((1,), (0,)), ((), ())), preferred_element_type=F32)


def dot_t(a, b):
    return lax.dot_general(a, b, (((1,), (1,)), ((), ())), preferred_element_type=F32)


def t_dot(a, b):
    return lax.dot_general(a, b, (((0,), (0,)), ((), ())), preferred_element_type=F32)


def one_hot_swap(outer, inner):
    size = outer * inner
    row = lax.broadcasted_iota(jnp.int32, (size, size), 0)
    col = lax.broadcasted_iota(jnp.int32, (size, size), 1)
    shift = inner.bit_length() - 1
    want = (row & (inner - 1)) * outer + (row >> shift)
    return jnp.where(col == want, 1.0, 0.0).astype(F32).astype(BF)


def matrix_blocks(wa, wi, wo, width):
    per = 4 * width // LANES
    base = 0
    for ref, per in ((wa, per), (wi, FF // LANES), (wo, width // LANES)):
        yield ref, per, base
        base = base + ref.shape[0] * per


def unpack_weights(flat, wa, wi, wo, b1, vec, width):
    for ref, per, base in matrix_blocks(wa, wi, wo, width):
        n = 256 // per
        swap = one_hot_swap(per, n)

        def body(g, carry, ref=ref, per=per, base=base, n=n, swap=swap):
            first = flat[pl.ds(pl.multiple_of(base + g * 512, 512), 256), :]
            second = flat[pl.ds(pl.multiple_of(base + g * 512, 512) + 256, 256), :]
            out = dot(swap, jnp.concatenate([first, second], axis=1)).astype(BF)
            row = pl.multiple_of(g * 2 * n, 2 * n)
            for c in range(per):
                piece = out[c * n : (c + 1) * n]
                cols = slice(c * LANES, (c + 1) * LANES)
                ref[pl.ds(row, 2 * n), cols] = jnp.concatenate([piece[:, :LANES], piece[:, LANES:]], axis=0)
            return carry

        lax.fori_loop(0, ref.shape[0] * per // 512, body, 0, unroll=8)
    per_out = width // LANES
    tail = flat[flat.shape[0] - FF // LANES - 8 * per_out : flat.shape[0], :].astype(F32)
    for c in range(FF // LANES):
        b1[0:1, c * LANES : (c + 1) * LANES] = tail[c : c + 1]
    for r in range(8):
        for c in range(per_out):
            k = FF // LANES + r * per_out + c
            vec[r : r + 1, c * LANES : (c + 1) * LANES] = tail[k : k + 1]


def pack_weights(flat, wa, wi, wo, width):
    for ref, per, base in matrix_blocks(wa, wi, wo, width):
        n = 256 // per
        swap = one_hot_swap(n, per)

        def body(g, carry, ref=ref, per=per, base=base, n=n, swap=swap):
            row = pl.multiple_of(g * 2 * n, 2 * n)
            pieces = []
            for c in range(per):
                v = ref[pl.ds(row, 2 * n), c * LANES : (c + 1) * LANES]
                pieces.append(jnp.concatenate([v[:n], v[n:]], axis=1))
            out = dot(swap, jnp.concatenate(pieces, axis=0)).astype(BF)
            first = pl.multiple_of(base + g * 512, 512)
            flat[pl.ds(first, 256), :] = out[:, :LANES]
            flat[pl.ds(first + 256, 256), :] = out[:, LANES:]
            return carry

        lax.fori_loop(0, ref.shape[0] * per // 512, body, 0, unroll=8)


def norm_stats(resid):
    center = resid - jnp.mean(resid, axis=-1, keepdims=True)
    variance = jnp.mean(center * center, axis=-1, keepdims=True)
    inv = lax.rsqrt(variance + norm_eps)
    return center * inv, inv


def norm_grad(upstream, normed, inv, gain):
    scaled = upstream * gain
    m0 = jnp.mean(scaled, axis=-1, keepdims=True)
    m1 = jnp.mean(scaled * normed, axis=-1, keepdims=True)
    return inv * (scaled - m0 - normed * m1)


def colsum(v):
    return jnp.sum(v, axis=0, keepdims=True)


def lane_mask(which, dtype):
    lane = lax.broadcasted_iota(jnp.int32, (1, LANES), 1)
    keep = (lane < 64) if which == 0 else (lane >= 64)
    return jnp.where(keep, 1.0, 0.0).astype(F32).astype(dtype)


C0 = math.sqrt(2.0 / math.pi)


def gelu_pair(u):
    u2 = u * u
    inner = u * (C0 + (C0 * 0.044715) * u2)
    half = 0.5 + 0.5 * jnp.tanh(inner)
    g = u * half
    slope = half + 2.0 * g * (1.0 - half) * (C0 + (3.0 * C0 * 0.044715) * u2)
    return g, slope


def window_starts(shards, tiles):
    return [i * tiles // shards for i in range(shards + 1)]


def own_index():
    return lax.axis_index("dp") * lax.axis_size("rep") + lax.axis_index("rep")


RZ, RX, RC, RY = 8, 4, 2, 1
STEPS = ((RX, RY), (RY, RX), (2 * RZ, RZ), (RZ, 2 * RZ))
SLOTS = 1 << len(STEPS)
PLANES = (3, 2, 1, 0)


def own_core(me):
    return (me // RC) & 1


def slot_owner(base, core, slot):
    owner = base
    for k, (zero, one) in enumerate(STEPS):
        if slot >> (len(STEPS) - 1 - k) & 1:
            owner = jnp.bitwise_xor(owner, jnp.where(core == 0, zero, one))
    return owner


def settle(ref, rows, sem):
    pltpu.make_async_copy(ref.at[pl.ds(0, rows)], ref.at[pl.ds(0, rows)], sem).wait()


def window_moves(owner, height, tiles, shards, edge_row):
    start = pl.multiple_of((owner * tiles // shards) * TILE, TILE)
    edge = pl.multiple_of(edge_row + owner * 2 * TILE, TILE)
    body = height - 2 * TILE
    return [(0, start, body), (body, edge, 2 * TILE)]


def load_windows(w_refs, wide, flat, sem, shards, prepare):
    tiles = flat.shape[0] // TILE
    height = w_refs[0].shape[0]
    edge_row = flat.shape[0] + TILE
    base = tiles // shards * TILE
    me = own_index()
    core = own_core(me)
    for n, ref in enumerate(w_refs):
        side, origin = (core, me) if n < SLOTS else (1 - core, jnp.bitwise_xor(me, RC))
        owner = slot_owner(origin, side, n % SLOTS)
        for at, to, rows in window_moves(owner, height, tiles, shards, edge_row):
            pltpu.make_async_copy(ref.at[pl.ds(at, rows)], wide.at[pl.ds(to, rows)], sem.at[0]).start()
    prepare()
    settle(wide, height * shards, sem.at[0])
    starts = window_starts(shards, tiles)

    def tile(row):
        return wide[row : row + TILE, :]

    for i in range(shards):
        nxt = starts[i + 1]
        row = edge_row + i * 2 * TILE
        if nxt - starts[i] != base // TILE:
            wide[(nxt - 1) * TILE : nxt * TILE, :] = tile(row)
            row = row + TILE
        if i + 1 < shards:
            wide[nxt * TILE : (nxt + 1) * TILE, :] = tile(nxt * TILE) + tile(row)


def store_windows(g_refs, wide, flat, sem, shards, vec_rows):
    tiles = flat.shape[0] // TILE
    height = g_refs[0].shape[1]
    edge_row = flat.shape[0] + TILE
    starts = window_starts(shards, tiles)
    last = lax.broadcasted_iota(jnp.int32, (TILE, LANES), 0) == TILE - 1
    for i in range(shards):
        low = starts[i] * TILE + height - 2 * TILE
        row = edge_row + i * 2 * TILE
        for k in range(2):
            at = low + k * TILE
            if at + TILE <= flat.shape[0]:
                tile = wide[at : at + TILE, :]
            else:
                tile = jnp.zeros((TILE, LANES), BF)
            if k == 1:
                tile = jnp.where(last, vec_rows[i : i + 1], tile.astype(F32)).astype(BF)
            wide[row + k * TILE : row + (k + 1) * TILE, :] = tile
    me = own_index()
    core = own_core(me)
    for n, ref in enumerate(g_refs):
        side, origin = (core, me) if n == 0 else (1 - core, jnp.bitwise_xor(me, RC))
        for k in range(ref.shape[0]):
            plane = k // 4 if n == 0 else PLANES[n - 1]
            slot = 4 * (k % 4) + plane
            owner = slot_owner(origin, side, slot)
            for at, to, rows in window_moves(owner, height, tiles, shards, edge_row):
                pltpu.make_async_copy(wide.at[pl.ds(to, rows)], ref.at[k].at[pl.ds(at, rows)], sem.at[n]).start()
    for n, ref in enumerate(g_refs):
        settle(wide, ref.shape[0] * ref.shape[1], sem.at[n])


CHUNK = 512
STEP = 32
GSTEP = 16
AHEAD = 2


def core_kernel(*refs, width, length, shards, windows, flat_rows):
    n_in = 2 * SLOTS if windows else 1
    (x_ref, cot_ref, seg_ref) = refs[:3]
    w_refs = refs[3 : 3 + n_in]
    refs = refs[3 + n_in :]
    (y_ref, dx_ref) = refs[:2]
    n_out = 1 + len(PLANES) if windows else 1
    g_refs = refs[2 : 2 + n_out]
    (wide, wa, wi, wo, b1, vec, xb, qkv, ab, ctx, xh1, iv1, xh2, iv2, h1b, slope, df, da, dqkv, dc, dr1,
     bias, gb1, gvec, count_ref, sem) = refs[2 + n_out :]
    D = width
    T = length
    pairs = D // LANES
    flat = wide.at[pl.ds(0, flat_rows)]

    count_ref[0] = 1
    single = count_ref[0]
    scale = 0.125

    def prepare():
        seg = seg_ref[...].astype(F32)
        column = jnp.transpose(jnp.broadcast_to(seg, (LANES, T)))[:, 0:1]
        bias[...] = jnp.where(column == seg, 0.0, -1e30).astype(F32)
        dx_ref[...] = x_ref[...].astype(F32)
        gvec[...] = jnp.zeros_like(gvec)

    if windows:
        load_windows(w_refs, wide, flat, sem, shards, prepare)
    else:
        cp = pltpu.make_async_copy(w_refs[0], flat, sem.at[0])
        cp.start()
        prepare()
        cp.wait()
    unpack_weights(flat, wa, wi, wo, b1, vec, D)

    def phase(body):
        def step(_, carry):
            body()
            return carry

        lax.fori_loop(0, single, step, 0)

    hidden = FF * REC * T // LANES

    def put(which, chunk, row, val):
        for j in range(CHUNK // LANES):
            at = which * hidden + (chunk * (CHUNK // LANES) + j) * REC * T
            wide[pl.ds(row + at, val.shape[0]), :] = val[:, j * LANES : (j + 1) * LANES]

    def get(which, chunk, row, n):
        at = [which * hidden + (chunk * (CHUNK // LANES) + j) * REC * T for j in range(CHUNK // LANES)]
        return jnp.concatenate([wide[pl.ds(row + k, n), :] for k in at], axis=1)

    def project(r):
        rows = pl.ds(pl.multiple_of(r * T, T), T)
        x16 = dx_ref[...].astype(BF)
        xb[rows, :] = x16
        for j in range(3):
            p = dot(x16, wa[:, j * D : (j + 1) * D])
            if j == 0:
                p = p + vec[0:1, :]
            if j == 2:
                p = p + vec[1:2, :]
            p = p.astype(BF)
            for c in range(pairs):
                qkv[r, j * pairs + c] = p[:, c * LANES : (c + 1) * LANES]

    def attend(r):
        rows = pl.ds(pl.multiple_of(r * T, T), T)

        def score(h):
            return dot_t(qkv[r, h // 2] * (lane_mask(h % 2, BF) * scale).astype(BF), qkv[r, pairs + h // 2])

        pend = [score(h) for h in range(AHEAD)]
        left = None
        for h in range(HEADS):
            if h + AHEAD < HEADS:
                pend.append(score(h + AHEAD))
            full = pend.pop(0)
            parts = []
            for i in range(0, T, STEP):
                sc = full[i : i + STEP] + bias[i : i + STEP, :]
                ex = jnp.exp(sc - jnp.max(sc, axis=-1, keepdims=True))
                tot = jnp.sum(ex, axis=-1, keepdims=True)
                parts.append((ex * (1.0 / tot)).astype(BF))
                ab[r * HEADS + h, pl.ds(i, STEP), :] = parts[-1]
            out = dot(jnp.concatenate(parts, axis=0), qkv[r, 2 * pairs + h // 2] * lane_mask(h % 2, BF))
            if h % 2 == 0:
                left = out
            else:
                ctx[h // 2, rows, :] = (left + out).astype(BF)

    def feed(r):
        rows = pl.ds(pl.multiple_of(r * T, T), T)
        a = dot(jnp.concatenate([ctx[c, rows, :] for c in range(pairs)], axis=1), wa[:, 3 * D : 4 * D])
        for i in range(0, T, STEP):
            sub = pl.ds(i, STEP)
            hat, inv = norm_stats(dx_ref[sub, :] + (a[i : i + STEP] + vec[2:3, :]))
            xh1[r, sub, :] = hat
            iv1[r, sub, :] = jnp.broadcast_to(inv, (STEP, LANES))
            h1b[pl.ds(pl.multiple_of(r * T, T) + i, STEP), :] = (hat * vec[4:5, :] + vec[5:6, :]).astype(BF)
        h16 = h1b[rows, :]

        def up(c):
            return dot(h16, wi[:, c * CHUNK : (c + 1) * CHUNK])

        pend = [up(c) for c in range(AHEAD)]
        f = None
        for c in range(FF // CHUNK):
            cols = slice(c * CHUNK, (c + 1) * CHUNK)
            if c + AHEAD < FF // CHUNK:
                pend.append(up(c + AHEAD))
            u = pend.pop(0)
            parts = []
            for i in range(0, T, GSTEP):
                g, sl = gelu_pair(u[i : i + GSTEP] + b1[:, cols])
                parts.append(g.astype(BF))
                put(0, c, pl.multiple_of(r * T, T) + i, parts[-1])
                slope[r, pl.ds(i, GSTEP), cols] = sl.astype(BF)
            part = dot(jnp.concatenate(parts, axis=0), wo[cols, :])
            f = part if f is None else f + part
        for i in range(0, T, STEP):
            sub = pl.ds(i, STEP)
            h1 = xh1[r, sub, :] * vec[4:5, :] + vec[5:6, :]
            hat, inv = norm_stats(h1 + (f[i : i + STEP] + vec[3:4, :]))
            xh2[r, sub, :] = hat
            iv2[r, sub, :] = jnp.broadcast_to(inv, (STEP, LANES))
            y = hat * vec[6:7, :] + vec[7:8, :]
            dx_ref[sub, :] = y

    def acc(ref, row, val):
        ref[row : row + 1, :] = ref[row : row + 1, :] + val

    def feed_back(r):
        rows = pl.ds(pl.multiple_of(r * T, T), T)
        sums = [jnp.zeros((8, D), F32) for _ in range(6)]

        def add(k, val):
            sums[k] = sums[k] + jnp.sum(val.reshape(STEP // 8, 8, D), axis=0)

        for i in range(0, T, STEP):
            sub = pl.ds(i, STEP)
            dy = dx_ref[sub, :]
            hat = xh2[r, sub, :]
            add(0, dy * hat)
            add(1, dy)
            dr2 = norm_grad(dy, hat, iv2[r, sub, 0:1], vec[6:7, :])
            dr1[sub, :] = dr2
            d16 = dr2.astype(BF)
            df[pl.ds(pl.multiple_of(r * T, T) + i, STEP), :] = d16
            add(2, d16.astype(F32))
        d16 = df[rows, :]

        def down(c):
            return dot_t(d16, wo[c * CHUNK : (c + 1) * CHUNK, :])

        pend = [down(c) for c in range(AHEAD)]
        dh = None
        for c in range(FF // CHUNK):
            cols = slice(c * CHUNK, (c + 1) * CHUNK)
            if c + AHEAD < FF // CHUNK:
                pend.append(down(c + AHEAD))
            t = pend.pop(0)
            parts = []
            for i in range(0, T, GSTEP):
                g16 = t[i : i + GSTEP].astype(BF) * slope[r, pl.ds(i, GSTEP), cols]
                parts.append(g16)
                put(1, c, pl.multiple_of(r * T, T) + i, g16)
            part = dot_t(jnp.concatenate(parts, axis=0), wi[:, cols])
            dh = part if dh is None else dh + part
        for i in range(0, T, STEP):
            sub = pl.ds(i, STEP)
            hat = xh1[r, sub, :]
            upstream = dr1[sub, :] + dh[i : i + STEP]
            add(3, upstream * hat)
            add(4, upstream)
            d1 = norm_grad(upstream, hat, iv1[r, sub, 0:1], vec[4:5, :])
            dr1[sub, :] = d1
            a16 = d1.astype(BF)
            da[pl.ds(pl.multiple_of(r * T, T) + i, STEP), :] = a16
            add(5, a16.astype(F32))
        for row, k in ((6, 0), (7, 1), (3, 2), (4, 3), (5, 4), (2, 5)):
            acc(gvec, row, colsum(sums[k]))
        c16 = dot_t(da[rows, :], wa[:, 3 * D : 4 * D]).astype(BF)
        for c in range(pairs):
            dc[c] = c16[:, c * LANES : (c + 1) * LANES]

    def attend_back(r):
        rows = pl.ds(pl.multiple_of(r * T, T), T)

        def rise(h):
            return dot_t(dc[h // 2] * lane_mask(h % 2, BF), qkv[r, 2 * pairs + h // 2])

        pend = [rise(h) for h in range(AHEAD)]
        for h in range(HEADS):
            if h + AHEAD < HEADS:
                pend.append(rise(h + AHEAD))
            full = pend.pop(0)
            p, e = h // 2, h % 2
            half = slice(64 * e, 64 * e + 64)
            if e == 0:
                qt = jnp.transpose(qkv[r, p])
                ct = jnp.transpose(dc[p])
                dkt, dvt = [], []
            p16 = ab[r * HEADS + h]
            parts = []
            for i in range(0, T, STEP):
                pf = p16[i : i + STEP].astype(F32)
                t = full[i : i + STEP] * pf
                parts.append((t - pf * jnp.sum(t, axis=-1, keepdims=True)).astype(BF))
            s16 = jnp.concatenate(parts, axis=0)
            part = dot(s16, qkv[r, pairs + p] * lane_mask(e, BF))
            dkt.append(dot(qt[half], s16))
            dvt.append(dot(ct[half], p16))
            if e == 0:
                dq = part
            else:
                dqkv[p, rows, :] = ((dq + part) * scale).astype(BF)
                dqkv[pairs + p, rows, :] = jnp.transpose((jnp.concatenate(dkt, axis=0) * scale).astype(BF))
                dqkv[2 * pairs + p, rows, :] = jnp.transpose(jnp.concatenate(dvt, axis=0).astype(BF))
    def project_back(r):
        rows = pl.ds(pl.multiple_of(r * T, T), T)
        for c in range(pairs):
            cols = slice(c * LANES, (c + 1) * LANES)
            gvec[0:1, cols] = gvec[0:1, cols] + colsum(dqkv[c, rows, :].astype(F32))
            gvec[1:2, cols] = gvec[1:2, cols] + colsum(dqkv[2 * pairs + c, rows, :].astype(F32))
        d3 = jnp.concatenate([dqkv[c, rows, :] for c in range(3 * pairs)], axis=1)
        dx_ref[...] = dr1[...] + dot_t(d3, wa[:, : 3 * D])

    def forward(r, carry):
        for part in (project, attend, feed):
            phase(functools.partial(part, r))
        return carry

    def backward(i, carry):
        for part in (feed_back, attend_back, project_back):
            phase(functools.partial(part, REC - 1 - i))
        return carry

    lax.fori_loop(0, REC, forward, 0)
    y_ref[...] = dx_ref[...]
    dx_ref[...] = cot_ref[...].astype(F32)
    lax.fori_loop(0, REC, backward, 0)

    def grad_qkvo():
        xt = jnp.transpose(xb[...])
        for j in range(3):
            d3 = jnp.concatenate([dqkv[j * pairs + c] for c in range(pairs)], axis=1)
            wa[:, j * D : (j + 1) * D] = dot(xt, d3).astype(BF)
        for c in range(pairs):
            wa[c * LANES : (c + 1) * LANES, 3 * D : 4 * D] = t_dot(ctx[c], da[...]).astype(BF)

    def grad_in():
        ht = jnp.concatenate([jnp.transpose(h1b[...]), jnp.ones((16, REC * T), BF)], axis=0)
        for c in range(FF // CHUNK):
            cols = slice(c * CHUNK, (c + 1) * CHUNK)
            grad = dot(ht, get(1, c, 0, REC * T))
            wi[:, cols] = grad[:D].astype(BF)
            gb1[0:1, cols] = grad[D : D + 1]

    def grad_out():
        for c in range(FF // CHUNK):
            cols = slice(c * CHUNK, (c + 1) * CHUNK)
            wo[cols, :] = t_dot(get(0, c, 0, REC * T), df[...]).astype(BF)

    phase(grad_qkvo)
    phase(grad_in)
    phase(grad_out)
    pack_weights(flat, wa, wi, wo, D)
    per_out = D // LANES
    rows = [gb1[0:1, c * LANES : (c + 1) * LANES] for c in range(FF // LANES)]
    for r in range(8):
        rows = rows + [gvec[r : r + 1, c * LANES : (c + 1) * LANES] for c in range(per_out)]
    tail = jnp.concatenate(rows, axis=0)
    flat[flat.shape[0] - len(rows) : flat.shape[0], :] = tail.astype(BF)
    if windows:
        store_windows(g_refs, wide, flat, sem, shards, tail[FF // LANES :])
    else:
        cp = pltpu.make_async_copy(flat, g_refs[0], sem.at[0])
        cp.start()
        cp.wait()


def core(x, cot, seg, flats, windows, shards, rows):
    T, D = x.shape
    vm = pltpu.VMEM
    pairs = D // LANES
    scratch = [
        vm((max(2 * FF * REC * T // LANES, rows + TILE + 2 * TILE * shards), LANES), BF),
        vm((D, 4 * D), BF), vm((D, FF), BF), vm((FF, D), BF), vm((1, FF), F32), vm((8, D), F32),
        vm((REC * T, D), BF), vm((REC, 3 * pairs, T, LANES), BF), vm((REC * HEADS, T, T), BF), vm((pairs, REC * T, LANES), BF),
        vm((REC, T, D), F32), vm((REC, T, LANES), F32), vm((REC, T, D), F32), vm((REC, T, LANES), F32),
        vm((REC * T, D), BF), vm((REC, T, FF), BF),
        vm((REC * T, D), BF), vm((REC * T, D), BF), vm((3 * pairs, REC * T, LANES), BF), vm((pairs, T, LANES), BF),
        vm((T, D), F32), vm((T, T), F32),
        vm((1, FF), F32), vm((8, D), F32),
        pltpu.SMEM((1,), jnp.int32), pltpu.SemaphoreType.DMA((8,)),
    ]
    if windows:
        g_shapes = [jax.ShapeDtypeStruct((n, flats[0].shape[0], LANES), BF) for n in (SLOTS, 4, 4, 4, 4)]
    else:
        g_shapes = [jax.ShapeDtypeStruct((rows, LANES), BF)]
    in_vmem = pl.BlockSpec(memory_space=pltpu.VMEM)
    anywhere = pl.BlockSpec(memory_space=pl.ANY)
    return pl.pallas_call(
        functools.partial(core_kernel, width=D, length=T, shards=shards, windows=windows, flat_rows=rows),
        out_shape=tuple([jax.ShapeDtypeStruct((T, D), F32)] * 2 + g_shapes),
        in_specs=[in_vmem] * 3 + [anywhere] * len(flats),
        out_specs=tuple([in_vmem] * 2 + [anywhere] * len(g_shapes)),
        scratch_shapes=scratch,
        compiler_params=pltpu.CompilerParams(vmem_limit_bytes=54 * 1024 * 1024),
        name="layer_core",
    )(x, cot, seg, *flats)


AXES = ("dp", "rep")


def exchange(v, step):
    count = lax.axis_size("dp") * lax.axis_size("rep")
    zero, one = STEPS[step] if step < len(STEPS) else (RC, RC)
    return lax.ppermute(v, AXES, [(j, j ^ (one if j // RC & 1 else zero)) for j in range(count)])


def after(v, earlier):
    return lax.optimization_barrier((v, earlier))[0]


def gather_windows(own):
    next_plane = exchange(own, 3)
    near = [None] * SLOTS
    planes = [own, next_plane, exchange(after(own, next_plane), 2), exchange(next_plane, 2)]
    for m, v in enumerate(planes):
        side = exchange(v, 0)
        near[m], near[8 + m], near[4 + m], near[12 + m] = v, side, exchange(v, 1), exchange(side, 1)
    return near + [exchange(v, 4) for v in near]


def total(*parts):
    v = parts[0].astype(F32)
    for part in parts[1:]:
        v = v + part.astype(F32)
    return v.astype(BF)


def sum_windows(keep, *sent):
    got = {m: exchange(v, 4) for m, v in zip(PLANES, sent)}
    side, back, last = {}, {}, [None]

    def add(*parts):
        if last[0] is not None:
            parts = (*parts[:-1], after(parts[-1], last[0]))
        last[0] = total(*parts)
        return last[0]

    def pair(m):
        side[m] = exchange(add(keep[4 * m + 2 : 4 * m + 4], got[m][2:]), 0)

    def second(m):
        back[m] = exchange(add(keep[4 * m + 1], got[m][1], side[m][1]), 1)

    def plane(m):
        return (keep[4 * m], got[m][0], side[m][0], back[m])

    pair(3)
    pair(2)
    pair(1)
    second(3)
    second(2)
    pair(0)
    turn = exchange(add(*plane(3)), 2)
    second(1)
    two = exchange(add(*plane(2)), 2)
    second(0)
    one = exchange(add(*plane(1), turn), 3)
    return (*plane(0), one, two)


def shards_fn(block_input, segment_ids, cotangent, master_weights, momentum, weight_average):
    width = block_input.shape[2]
    length = block_input.shape[1]
    count = lax.axis_size("dp") * lax.axis_size("rep")
    share = master_weights.shape[0]
    rows = share * count // LANES
    tiles = rows // TILE
    args = (block_input[0], cotangent[0], segment_ids)
    if count == 32:
        window = (tiles // count + 2) * TILE
        first = (own_index() * share) % (TILE * LANES)
        padded = jnp.pad(master_weights, (TILE * LANES, window * LANES - share))
        own = lax.dynamic_slice(padded, (TILE * LANES - first,), (window * LANES,)).astype(BF).reshape(window, LANES)
        block_output, input_grad, *sums = core(*args, gather_windows(own), True, count, rows)
        addends = sum_windows(*sums)
        grad = addends[0].astype(F32)
        for addend in addends[1:]:
            grad = grad + addend.astype(F32)
        weight_grad = lax.dynamic_slice(grad.reshape(-1), (first,), (share,))
        vector_grad = grad[window - 1]
    else:
        flat = lax.all_gather(master_weights.astype(BF), AXES, axis=0, tiled=True).reshape(rows, LANES)
        block_output, input_grad, grad = core(*args, [flat], False, count, rows)
        grad = grad.reshape(-1).astype(F32)
        weight_grad = lax.psum_scatter(grad, AXES, scatter_dimension=0, tiled=True)
        vector_grad = lax.psum_scatter(grad[grad.shape[0] - 8 * width :], AXES, scatter_dimension=0, tiled=True)
    token_count = block_input.shape[0] * length * count
    rate = rate_base / math.sqrt(token_count)
    new_momentum = mom_decay * momentum + weight_grad
    new_weights = master_weights - rate * (weight_grad + mom_decay * new_momentum)
    new_average = avg_keep * weight_average + (1.0 - avg_keep) * new_weights
    return (
        block_output[None],
        input_grad[None],
        weight_grad,
        vector_grad,
        new_momentum,
        new_average,
        new_weights,
    )


def solution(mesh):
    three = P(AXES, None, None)
    two = P(AXES, None)
    one = P(AXES)
    return jax.shard_map(
        shards_fn,
        mesh=mesh,
        in_specs=(three, two, three, one, one, one),
        out_specs=(three, three, one, one, one, one, one),
        check_vma=False,
    )
```

```python
import functools
import math

import jax
import jax.numpy as jnp
from jax import lax
from jax.experimental import pallas as pl
from jax.experimental.pallas import tpu as pltpu
from jax.sharding import PartitionSpec as P

FF = 2048
HEADS = 8
REC = 2
TILE = 8
LANES = 128

norm_eps = 1e-05
mom_decay = 0.9
avg_keep = 0.8
rate_base = 0.006

BF = jnp.bfloat16
F32 = jnp.float32


def dot(a, b):
    return lax.dot_general(a, b, (((1,), (0,)), ((), ())), preferred_element_type=F32)


def dot_t(a, b):
    return lax.dot_general(a, b, (((1,), (1,)), ((), ())), preferred_element_type=F32)


def t_dot(a, b):
    return lax.dot_general(a, b, (((0,), (0,)), ((), ())), preferred_element_type=F32)


def one_hot_swap(outer, inner):
    size = outer * inner
    row = lax.broadcasted_iota(jnp.int32, (size, size), 0)
    col = lax.broadcasted_iota(jnp.int32, (size, size), 1)
    shift = inner.bit_length() - 1
    want = (row & (inner - 1)) * outer + (row >> shift)
    return jnp.where(col == want, 1.0, 0.0).astype(F32).astype(BF)


def matrix_blocks(wa, wi, wo, width):
    per = 4 * width // LANES
    base = 0
    for ref, per in ((wa, per), (wi, FF // LANES), (wo, width // LANES)):
        yield ref, per, base
        base = base + ref.shape[0] * per


def unpack_weights(flat, wa, wi, wo, b1, vec, width):
    for ref, per, base in matrix_blocks(wa, wi, wo, width):
        n = 256 // per
        swap = one_hot_swap(per, n)

        def body(g, carry, ref=ref, per=per, base=base, n=n, swap=swap):
            first = flat[pl.ds(pl.multiple_of(base + g * 512, 512), 256), :]
            second = flat[pl.ds(pl.multiple_of(base + g * 512, 512) + 256, 256), :]
            out = dot(swap, jnp.concatenate([first, second], axis=1)).astype(BF)
            row = pl.multiple_of(g * 2 * n, 2 * n)
            for c in range(per):
                piece = out[c * n : (c + 1) * n]
                cols = slice(c * LANES, (c + 1) * LANES)
                ref[pl.ds(row, 2 * n), cols] = jnp.concatenate([piece[:, :LANES], piece[:, LANES:]], axis=0)
            return carry

        lax.fori_loop(0, ref.shape[0] * per // 512, body, 0, unroll=8)
    per_out = width // LANES
    tail = flat[flat.shape[0] - FF // LANES - 8 * per_out : flat.shape[0], :].astype(F32)
    for c in range(FF // LANES):
        b1[0:1, c * LANES : (c + 1) * LANES] = tail[c : c + 1]
    for r in range(8):
        for c in range(per_out):
            k = FF // LANES + r * per_out + c
            vec[r : r + 1, c * LANES : (c + 1) * LANES] = tail[k : k + 1]


def pack_weights(flat, wa, wi, wo, width):
    for ref, per, base in matrix_blocks(wa, wi, wo, width):
        n = 256 // per
        swap = one_hot_swap(n, per)

        def body(g, carry, ref=ref, per=per, base=base, n=n, swap=swap):
            row = pl.multiple_of(g * 2 * n, 2 * n)
            pieces = []
            for c in range(per):
                v = ref[pl.ds(row, 2 * n), c * LANES : (c + 1) * LANES]
                pieces.append(jnp.concatenate([v[:n], v[n:]], axis=1))
            out = dot(swap, jnp.concatenate(pieces, axis=0)).astype(BF)
            first = pl.multiple_of(base + g * 512, 512)
            flat[pl.ds(first, 256), :] = out[:, :LANES]
            flat[pl.ds(first + 256, 256), :] = out[:, LANES:]
            return carry

        lax.fori_loop(0, ref.shape[0] * per // 512, body, 0, unroll=8)


def norm_stats(resid):
    center = resid - jnp.mean(resid, axis=-1, keepdims=True)
    variance = jnp.mean(center * center, axis=-1, keepdims=True)
    inv = lax.rsqrt(variance + norm_eps)
    return center * inv, inv


def norm_grad(upstream, normed, inv, gain):
    scaled = upstream * gain
    m0 = jnp.mean(scaled, axis=-1, keepdims=True)
    m1 = jnp.mean(scaled * normed, axis=-1, keepdims=True)
    return inv * (scaled - m0 - normed * m1)


def colsum(v):
    return jnp.sum(v, axis=0, keepdims=True)


def lane_mask(which, dtype):
    lane = lax.broadcasted_iota(jnp.int32, (1, LANES), 1)
    keep = (lane < 64) if which == 0 else (lane >= 64)
    return jnp.where(keep, 1.0, 0.0).astype(F32).astype(dtype)


C0 = math.sqrt(2.0 / math.pi)


def gelu_pair(u):
    u2 = u * u
    inner = u * (C0 + (C0 * 0.044715) * u2)
    half = 0.5 + 0.5 * jnp.tanh(inner)
    g = u * half
    slope = half + 2.0 * g * (1.0 - half) * (C0 + (3.0 * C0 * 0.044715) * u2)
    return g, slope


def window_starts(shards, tiles):
    return [i * tiles // shards for i in range(shards + 1)]


def own_index():
    return lax.axis_index("dp") * lax.axis_size("rep") + lax.axis_index("rep")


RZ, RX, RC, RY = 8, 4, 2, 1
STEPS = ((RX, RY), (RY, RX), (2 * RZ, RZ), (RZ, 2 * RZ))
SLOTS = 1 << len(STEPS)
PLANES = (3, 2, 1, 0)


def own_core(me):
    return (me // RC) & 1


def slot_owner(base, core, slot):
    owner = base
    for k, (zero, one) in enumerate(STEPS):
        if slot >> (len(STEPS) - 1 - k) & 1:
            owner = jnp.bitwise_xor(owner, jnp.where(core == 0, zero, one))
    return owner


def settle(ref, rows, sem):
    pltpu.make_async_copy(ref.at[pl.ds(0, rows)], ref.at[pl.ds(0, rows)], sem).wait()


def window_moves(owner, height, tiles, shards, edge_row):
    start = pl.multiple_of((owner * tiles // shards) * TILE, TILE)
    edge = pl.multiple_of(edge_row + owner * 2 * TILE, TILE)
    body = height - 2 * TILE
    return [(0, start, body), (body, edge, 2 * TILE)]


def load_windows(w_refs, wide, flat, sem, shards, prepare):
    tiles = flat.shape[0] // TILE
    height = w_refs[0].shape[0]
    edge_row = flat.shape[0] + TILE
    base = tiles // shards * TILE
    me = own_index()
    core = own_core(me)
    for n, ref in enumerate(w_refs):
        side, origin = (core, me) if n < SLOTS else (1 - core, jnp.bitwise_xor(me, RC))
        owner = slot_owner(origin, side, n % SLOTS)
        for at, to, rows in window_moves(owner, height, tiles, shards, edge_row):
            pltpu.make_async_copy(ref.at[pl.ds(at, rows)], wide.at[pl.ds(to, rows)], sem.at[0]).start()
    prepare()
    settle(wide, height * shards, sem.at[0])
    starts = window_starts(shards, tiles)

    def tile(row):
        return wide[row : row + TILE, :]

    for i in range(shards):
        nxt = starts[i + 1]
        row = edge_row + i * 2 * TILE
        if nxt - starts[i] != base // TILE:
            wide[(nxt - 1) * TILE : nxt * TILE, :] = tile(row)
            row = row + TILE
        if i + 1 < shards:
            wide[nxt * TILE : (nxt + 1) * TILE, :] = tile(nxt * TILE) + tile(row)


def store_windows(g_refs, wide, flat, sem, shards, vec_rows):
    tiles = flat.shape[0] // TILE
    height = g_refs[0].shape[1]
    edge_row = flat.shape[0] + TILE
    starts = window_starts(shards, tiles)
    last = lax.broadcasted_iota(jnp.int32, (TILE, LANES), 0) == TILE - 1
    for i in range(shards):
        low = starts[i] * TILE + height - 2 * TILE
        row = edge_row + i * 2 * TILE
        for k in range(2):
            at = low + k * TILE
            if at + TILE <= flat.shape[0]:
                tile = wide[at : at + TILE, :]
            else:
                tile = jnp.zeros((TILE, LANES), BF)
            if k == 1:
                tile = jnp.where(last, vec_rows[i : i + 1], tile.astype(F32)).astype(BF)
            wide[row + k * TILE : row + (k + 1) * TILE, :] = tile
    me = own_index()
    core = own_core(me)
    for n, ref in enumerate(g_refs):
        side, origin = (core, me) if n == 0 else (1 - core, jnp.bitwise_xor(me, RC))
        for k in range(ref.shape[0]):
            plane = k // 4 if n == 0 else PLANES[n - 1]
            slot = 4 * (k % 4) + plane
            owner = slot_owner(origin, side, slot)
            for at, to, rows in window_moves(owner, height, tiles, shards, edge_row):
                pltpu.make_async_copy(wide.at[pl.ds(to, rows)], ref.at[k].at[pl.ds(at, rows)], sem.at[n]).start()
    for n, ref in enumerate(g_refs):
        settle(wide, ref.shape[0] * ref.shape[1], sem.at[n])


CHUNK = 512
STEP = 32
GSTEP = 16
AHEAD = 2


def core_kernel(*refs, width, length, shards, windows, flat_rows):
    n_in = 2 * SLOTS if windows else 1
    (x_ref, cot_ref, seg_ref) = refs[:3]
    w_refs = refs[3 : 3 + n_in]
    refs = refs[3 + n_in :]
    (y_ref, dx_ref) = refs[:2]
    n_out = 1 + len(PLANES) if windows else 1
    g_refs = refs[2 : 2 + n_out]
    (wide, wa, wi, wo, b1, vec, xb, qkv, ab, ctx, xh1, iv1, xh2, iv2, h1b, slope, df, da, dqkv, dc, dr1,
     bias, gb1, gvec, count_ref, sem) = refs[2 + n_out :]
    D = width
    T = length
    pairs = D // LANES
    flat = wide.at[pl.ds(0, flat_rows)]

    count_ref[0] = 1
    single = count_ref[0]
    scale = 0.125

    def prepare():
        seg = seg_ref[...].astype(F32)
        column = jnp.transpose(jnp.broadcast_to(seg, (LANES, T)))[:, 0:1]
        bias[...] = jnp.where(column == seg, 0.0, -1e30).astype(F32)
        dx_ref[...] = x_ref[...].astype(F32)
        gvec[...] = jnp.zeros_like(gvec)

    if windows:
        load_windows(w_refs, wide, flat, sem, shards, prepare)
    else:
        cp = pltpu.make_async_copy(w_refs[0], flat, sem.at[0])
        cp.start()
        prepare()
        cp.wait()
    unpack_weights(flat, wa, wi, wo, b1, vec, D)

    def phase(body):
        def step(_, carry):
            body()
            return carry

        lax.fori_loop(0, single, step, 0)

    hidden = FF * REC * T // LANES

    def put(which, chunk, row, val):
        for j in range(CHUNK // LANES):
            at = which * hidden + (chunk * (CHUNK // LANES) + j) * REC * T
            wide[pl.ds(row + at, val.shape[0]), :] = val[:, j * LANES : (j + 1) * LANES]

    def get(which, chunk, row, n):
        at = [which * hidden + (chunk * (CHUNK // LANES) + j) * REC * T for j in range(CHUNK // LANES)]
        return jnp.concatenate([wide[pl.ds(row + k, n), :] for k in at], axis=1)

    def project(r):
        rows = pl.ds(pl.multiple_of(r * T, T), T)
        x16 = dx_ref[...].astype(BF)
        xb[rows, :] = x16
        for j in range(3):
            p = dot(x16, wa[:, j * D : (j + 1) * D])
            if j == 0:
                p = p + vec[0:1, :]
            if j == 2:
                p = p + vec[1:2, :]
            p = p.astype(BF)
            for c in range(pairs):
                qkv[r, j * pairs + c] = p[:, c * LANES : (c + 1) * LANES]

    def attend(r):
        rows = pl.ds(pl.multiple_of(r * T, T), T)

        def score(h):
            return dot_t(qkv[r, h // 2] * (lane_mask(h % 2, BF) * scale).astype(BF), qkv[r, pairs + h // 2])

        pend = [score(h) for h in range(AHEAD)]
        left = None
        for h in range(HEADS):
            if h + AHEAD < HEADS:
                pend.append(score(h + AHEAD))
            full = pend.pop(0)
            parts = []
            for i in range(0, T, STEP):
                sc = full[i : i + STEP] + bias[i : i + STEP, :]
                ex = jnp.exp(sc - jnp.max(sc, axis=-1, keepdims=True))
                tot = jnp.sum(ex, axis=-1, keepdims=True)
                parts.append((ex * (1.0 / tot)).astype(BF))
                ab[r * HEADS + h, pl.ds(i, STEP), :] = parts[-1]
            out = dot(jnp.concatenate(parts, axis=0), qkv[r, 2 * pairs + h // 2] * lane_mask(h % 2, BF))
            if h % 2 == 0:
                left = out
            else:
                ctx[h // 2, rows, :] = (left + out).astype(BF)

    def feed(r):
        rows = pl.ds(pl.multiple_of(r * T, T), T)
        a = dot(jnp.concatenate([ctx[c, rows, :] for c in range(pairs)], axis=1), wa[:, 3 * D : 4 * D])
        for i in range(0, T, STEP):
            sub = pl.ds(i, STEP)
            hat, inv = norm_stats(dx_ref[sub, :] + (a[i : i + STEP] + vec[2:3, :]))
            xh1[r, sub, :] = hat
            iv1[r, sub, :] = jnp.broadcast_to(inv, (STEP, LANES))
            h1b[pl.ds(pl.multiple_of(r * T, T) + i, STEP), :] = (hat * vec[4:5, :] + vec[5:6, :]).astype(BF)
        h16 = h1b[rows, :]

        def up(c):
            return dot(h16, wi[:, c * CHUNK : (c + 1) * CHUNK])

        pend = [up(c) for c in range(AHEAD)]
        f = None
        for c in range(FF // CHUNK):
            cols = slice(c * CHUNK, (c + 1) * CHUNK)
            if c + AHEAD < FF // CHUNK:
                pend.append(up(c + AHEAD))
            u = pend.pop(0)
            parts = []
            for i in range(0, T, GSTEP):
                g, sl = gelu_pair(u[i : i + GSTEP] + b1[:, cols])
                parts.append(g.astype(BF))
                put(0, c, pl.multiple_of(r * T, T) + i, parts[-1])
                slope[r, pl.ds(i, GSTEP), cols] = sl.astype(BF)
            part = dot(jnp.concatenate(parts, axis=0), wo[cols, :])
            f = part if f is None else f + part
        for i in range(0, T, STEP):
            sub = pl.ds(i, STEP)
            h1 = xh1[r, sub, :] * vec[4:5, :] + vec[5:6, :]
            hat, inv = norm_stats(h1 + (f[i : i + STEP] + vec[3:4, :]))
            xh2[r, sub, :] = hat
            iv2[r, sub, :] = jnp.broadcast_to(inv, (STEP, LANES))
            y = hat * vec[6:7, :] + vec[7:8, :]
            dx_ref[sub, :] = y

    def acc(ref, row, val):
        ref[row : row + 1, :] = ref[row : row + 1, :] + val

    def feed_back(r):
        rows = pl.ds(pl.multiple_of(r * T, T), T)
        sums = [jnp.zeros((8, D), F32) for _ in range(6)]

        def add(k, val):
            sums[k] = sums[k] + jnp.sum(val.reshape(STEP // 8, 8, D), axis=0)

        for i in range(0, T, STEP):
            sub = pl.ds(i, STEP)
            dy = dx_ref[sub, :]
            hat = xh2[r, sub, :]
            add(0, dy * hat)
            add(1, dy)
            dr2 = norm_grad(dy, hat, iv2[r, sub, 0:1], vec[6:7, :])
            dr1[sub, :] = dr2
            d16 = dr2.astype(BF)
            df[pl.ds(pl.multiple_of(r * T, T) + i, STEP), :] = d16
            add(2, d16.astype(F32))
        d16 = df[rows, :]

        def down(c):
            return dot_t(d16, wo[c * CHUNK : (c + 1) * CHUNK, :])

        pend = [down(c) for c in range(AHEAD)]
        dh = None
        for c in range(FF // CHUNK):
            cols = slice(c * CHUNK, (c + 1) * CHUNK)
            if c + AHEAD < FF // CHUNK:
                pend.append(down(c + AHEAD))
            t = pend.pop(0)
            parts = []
            for i in range(0, T, GSTEP):
                g16 = t[i : i + GSTEP].astype(BF) * slope[r, pl.ds(i, GSTEP), cols]
                parts.append(g16)
                put(1, c, pl.multiple_of(r * T, T) + i, g16)
            part = dot_t(jnp.concatenate(parts, axis=0), wi[:, cols])
            dh = part if dh is None else dh + part
        for i in range(0, T, STEP):
            sub = pl.ds(i, STEP)
            hat = xh1[r, sub, :]
            upstream = dr1[sub, :] + dh[i : i + STEP]
            add(3, upstream * hat)
            add(4, upstream)
            d1 = norm_grad(upstream, hat, iv1[r, sub, 0:1], vec[4:5, :])
            dr1[sub, :] = d1
            a16 = d1.astype(BF)
            da[pl.ds(pl.multiple_of(r * T, T) + i, STEP), :] = a16
            add(5, a16.astype(F32))
        for row, k in ((6, 0), (7, 1), (3, 2), (4, 3), (5, 4), (2, 5)):
            acc(gvec, row, colsum(sums[k]))
        c16 = dot_t(da[rows, :], wa[:, 3 * D : 4 * D]).astype(BF)
        for c in range(pairs):
            dc[c] = c16[:, c * LANES : (c + 1) * LANES]

    def attend_back(r):
        rows = pl.ds(pl.multiple_of(r * T, T), T)

        def rise(h):
            return dot_t(dc[h // 2] * lane_mask(h % 2, BF), qkv[r, 2 * pairs + h // 2])

        pend = [rise(h) for h in range(AHEAD)]
        for h in range(HEADS):
            if h + AHEAD < HEADS:
                pend.append(rise(h + AHEAD))
            full = pend.pop(0)
            p, e = h // 2, h % 2
            half = slice(64 * e, 64 * e + 64)
            if e == 0:
                qt = jnp.transpose(qkv[r, p])
                ct = jnp.transpose(dc[p])
                dkt, dvt = [], []
            p16 = ab[r * HEADS + h]
            parts = []
            for i in range(0, T, STEP):
                pf = p16[i : i + STEP].astype(F32)
                t = full[i : i + STEP] * pf
                parts.append((t - pf * jnp.sum(t, axis=-1, keepdims=True)).astype(BF))
            s16 = jnp.concatenate(parts, axis=0)
            part = dot(s16, qkv[r, pairs + p] * lane_mask(e, BF))
            dkt.append(dot(qt[half], s16))
            dvt.append(dot(ct[half], p16))
            if e == 0:
                dq = part
            else:
                dqkv[p, rows, :] = ((dq + part) * scale).astype(BF)
                dqkv[pairs + p, rows, :] = jnp.transpose((jnp.concatenate(dkt, axis=0) * scale).astype(BF))
                dqkv[2 * pairs + p, rows, :] = jnp.transpose(jnp.concatenate(dvt, axis=0).astype(BF))
    def project_back(r):
        rows = pl.ds(pl.multiple_of(r * T, T), T)
        for c in range(pairs):
            cols = slice(c * LANES, (c + 1) * LANES)
            gvec[0:1, cols] = gvec[0:1, cols] + colsum(dqkv[c, rows, :].astype(F32))
            gvec[1:2, cols] = gvec[1:2, cols] + colsum(dqkv[2 * pairs + c, rows, :].astype(F32))
        d3 = jnp.concatenate([dqkv[c, rows, :] for c in range(3 * pairs)], axis=1)
        dx_ref[...] = dr1[...] + dot_t(d3, wa[:, : 3 * D])

    def forward(r, carry):
        for part in (project, attend, feed):
            phase(functools.partial(part, r))
        return carry

    def backward(i, carry):
        for part in (feed_back, attend_back, project_back):
            phase(functools.partial(part, REC - 1 - i))
        return carry

    lax.fori_loop(0, REC, forward, 0)
    y_ref[...] = dx_ref[...]
    dx_ref[...] = cot_ref[...].astype(F32)
    lax.fori_loop(0, REC, backward, 0)

    def grad_qkvo():
        xt = jnp.transpose(xb[...])
        for j in range(3):
            d3 = jnp.concatenate([dqkv[j * pairs + c] for c in range(pairs)], axis=1)
            wa[:, j * D : (j + 1) * D] = dot(xt, d3).astype(BF)
        for c in range(pairs):
            wa[c * LANES : (c + 1) * LANES, 3 * D : 4 * D] = t_dot(ctx[c], da[...]).astype(BF)

    def grad_in():
        ht = jnp.concatenate([jnp.transpose(h1b[...]), jnp.ones((16, REC * T), BF)], axis=0)
        for c in range(FF // CHUNK):
            cols = slice(c * CHUNK, (c + 1) * CHUNK)
            grad = dot(ht, get(1, c, 0, REC * T))
            wi[:, cols] = grad[:D].astype(BF)
            gb1[0:1, cols] = grad[D : D + 1]

    def grad_out():
        for c in range(FF // CHUNK):
            cols = slice(c * CHUNK, (c + 1) * CHUNK)
            wo[cols, :] = t_dot(get(0, c, 0, REC * T), df[...]).astype(BF)

    phase(grad_qkvo)
    phase(grad_in)
    phase(grad_out)
    pack_weights(flat, wa, wi, wo, D)
    per_out = D // LANES
    rows = [gb1[0:1, c * LANES : (c + 1) * LANES] for c in range(FF // LANES)]
    for r in range(8):
        rows = rows + [gvec[r : r + 1, c * LANES : (c + 1) * LANES] for c in range(per_out)]
    tail = jnp.concatenate(rows, axis=0)
    flat[flat.shape[0] - len(rows) : flat.shape[0], :] = tail.astype(BF)
    if windows:
        store_windows(g_refs, wide, flat, sem, shards, tail[FF // LANES :])
    else:
        cp = pltpu.make_async_copy(flat, g_refs[0], sem.at[0])
        cp.start()
        cp.wait()


def core(x, cot, seg, flats, windows, shards, rows):
    T, D = x.shape
    vm = pltpu.VMEM
    pairs = D // LANES
    scratch = [
        vm((max(2 * FF * REC * T // LANES, rows + TILE + 2 * TILE * shards), LANES), BF),
        vm((D, 4 * D), BF), vm((D, FF), BF), vm((FF, D), BF), vm((1, FF), F32), vm((8, D), F32),
        vm((REC * T, D), BF), vm((REC, 3 * pairs, T, LANES), BF), vm((REC * HEADS, T, T), BF), vm((pairs, REC * T, LANES), BF),
        vm((REC, T, D), F32), vm((REC, T, LANES), F32), vm((REC, T, D), F32), vm((REC, T, LANES), F32),
        vm((REC * T, D), BF), vm((REC, T, FF), BF),
        vm((REC * T, D), BF), vm((REC * T, D), BF), vm((3 * pairs, REC * T, LANES), BF), vm((pairs, T, LANES), BF),
        vm((T, D), F32), vm((T, T), F32),
        vm((1, FF), F32), vm((8, D), F32),
        pltpu.SMEM((1,), jnp.int32), pltpu.SemaphoreType.DMA((8,)),
    ]
    if windows:
        g_shapes = [jax.ShapeDtypeStruct((n, flats[0].shape[0], LANES), BF) for n in (SLOTS, 4, 4, 4, 4)]
    else:
        g_shapes = [jax.ShapeDtypeStruct((rows, LANES), BF)]
    in_vmem = pl.BlockSpec(memory_space=pltpu.VMEM)
    anywhere = pl.BlockSpec(memory_space=pl.ANY)
    return pl.pallas_call(
        functools.partial(core_kernel, width=D, length=T, shards=shards, windows=windows, flat_rows=rows),
        out_shape=tuple([jax.ShapeDtypeStruct((T, D), F32)] * 2 + g_shapes),
        in_specs=[in_vmem] * 3 + [anywhere] * len(flats),
        out_specs=tuple([in_vmem] * 2 + [anywhere] * len(g_shapes)),
        scratch_shapes=scratch,
        compiler_params=pltpu.CompilerParams(vmem_limit_bytes=54 * 1024 * 1024),
        name="layer_core",
    )(x, cot, seg, *flats)


AXES = ("dp", "rep")


def exchange(v, step):
    count = lax.axis_size("dp") * lax.axis_size("rep")
    zero, one = STEPS[step] if step < len(STEPS) else (RC, RC)
    return lax.ppermute(v, AXES, [(j, j ^ (one if j // RC & 1 else zero)) for j in range(count)])


def after(v, earlier):
    return lax.optimization_barrier((v, earlier))[0]


def gather_windows(own):
    next_plane = exchange(own, 3)
    near = [None] * SLOTS
    planes = [own, next_plane, exchange(after(own, next_plane), 2), exchange(next_plane, 2)]
    for m, v in enumerate(planes):
        side = exchange(v, 0)
        near[m], near[8 + m], near[4 + m], near[12 + m] = v, side, exchange(v, 1), exchange(side, 1)
    late = near[8 + 2]
    return near + [exchange(after(v, late) if n % 4 < 2 else v, 4) for n, v in enumerate(near)]


def total(*parts):
    v = parts[0].astype(F32)
    for part in parts[1:]:
        v = v + part.astype(F32)
    return v.astype(BF)


def sum_windows(keep, *sent):
    got = {m: exchange(v, 4) for m, v in zip(PLANES, sent)}
    side, back, last = {}, {}, [None]

    def add(*parts):
        if last[0] is not None:
            parts = (*parts[:-1], after(parts[-1], last[0]))
        last[0] = total(*parts)
        return last[0]

    def single(m):
        far = exchange(add(keep[4 * m + 3], got[m][3]), 0)
        side[m] = (exchange(add(keep[4 * m + 2], got[m][2]), 0), far)

    def pair(m):
        side[m] = exchange(add(keep[4 * m + 2 : 4 * m + 4], got[m][2:]), 0)

    def second(m):
        back[m] = exchange(add(keep[4 * m + 1], got[m][1], side[m][1]), 1)

    def plane(m):
        return (keep[4 * m], got[m][0], side[m][0], back[m])

    single(3)
    single(2)
    second(3)
    second(2)
    pair(1)
    pair(0)
    turn = exchange(add(*plane(3)), 2)
    second(1)
    two = exchange(add(*plane(2)), 2)
    one = exchange(add(*plane(1), turn), 3)
    second(0)
    return (*plane(0), one, two)


def shards_fn(block_input, segment_ids, cotangent, master_weights, momentum, weight_average):
    width = block_input.shape[2]
    length = block_input.shape[1]
    count = lax.axis_size("dp") * lax.axis_size("rep")
    share = master_weights.shape[0]
    rows = share * count // LANES
    tiles = rows // TILE
    args = (block_input[0], cotangent[0], segment_ids)
    if count == 32:
        window = (tiles // count + 2) * TILE
        first = (own_index() * share) % (TILE * LANES)
        padded = jnp.pad(master_weights, (TILE * LANES, window * LANES - share))
        own = lax.dynamic_slice(padded, (TILE * LANES - first,), (window * LANES,)).astype(BF).reshape(window, LANES)
        block_output, input_grad, *sums = core(*args, gather_windows(own), True, count, rows)
        addends = sum_windows(*sums)
        grad = addends[0].astype(F32)
        for addend in addends[1:]:
            grad = grad + addend.astype(F32)
        weight_grad = lax.dynamic_slice(grad.reshape(-1), (first,), (share,))
        vector_grad = grad[window - 1]
    else:
        flat = lax.all_gather(master_weights.astype(BF), AXES, axis=0, tiled=True).reshape(rows, LANES)
        block_output, input_grad, grad = core(*args, [flat], False, count, rows)
        grad = grad.reshape(-1).astype(F32)
        weight_grad = lax.psum_scatter(grad, AXES, scatter_dimension=0, tiled=True)
        vector_grad = lax.psum_scatter(grad[grad.shape[0] - 8 * width :], AXES, scatter_dimension=0, tiled=True)
    token_count = block_input.shape[0] * length * count
    rate = rate_base / math.sqrt(token_count)
    new_momentum = mom_decay * momentum + weight_grad
    new_weights = master_weights - rate * (weight_grad + mom_decay * new_momentum)
    new_average = avg_keep * weight_average + (1.0 - avg_keep) * new_weights
    return (
        block_output[None],
        input_grad[None],
        weight_grad,
        vector_grad,
        new_momentum,
        new_average,
        new_weights,
    )


def solution(mesh):
    three = P(AXES, None, None)
    two = P(AXES, None)
    one = P(AXES)
    return jax.shard_map(
        shards_fn,
        mesh=mesh,
        in_specs=(three, two, three, one, one, one),
        out_specs=(three, three, one, one, one, one, one),
        check_vma=False,
    )
```

```python
import functools
import math

import jax
import jax.numpy as jnp
from jax import lax
from jax.experimental import pallas as pl
from jax.experimental.pallas import tpu as pltpu
from jax.sharding import PartitionSpec as P

FF = 2048
HEADS = 8
REC = 2
TILE = 8
LANES = 128

norm_eps = 1e-05
mom_decay = 0.9
avg_keep = 0.8
rate_base = 0.006

BF = jnp.bfloat16
F32 = jnp.float32


def dot(a, b):
    return lax.dot_general(a, b, (((1,), (0,)), ((), ())), preferred_element_type=F32)


def dot_t(a, b):
    return lax.dot_general(a, b, (((1,), (1,)), ((), ())), preferred_element_type=F32)


def t_dot(a, b):
    return lax.dot_general(a, b, (((0,), (0,)), ((), ())), preferred_element_type=F32)


def one_hot_swap(outer, inner):
    size = outer * inner
    row = lax.broadcasted_iota(jnp.int32, (size, size), 0)
    col = lax.broadcasted_iota(jnp.int32, (size, size), 1)
    shift = inner.bit_length() - 1
    want = (row & (inner - 1)) * outer + (row >> shift)
    return jnp.where(col == want, 1.0, 0.0).astype(F32).astype(BF)


def matrix_blocks(wa, wi, wo, width):
    per = 4 * width // LANES
    base = 0
    for ref, per in ((wa, per), (wi, FF // LANES), (wo, width // LANES)):
        yield ref, per, base
        base = base + ref.shape[0] * per


def unpack_weights(flat, wa, wi, wo, b1, vec, width):
    for ref, per, base in matrix_blocks(wa, wi, wo, width):
        n = 256 // per
        swap = one_hot_swap(per, n)

        def body(g, carry, ref=ref, per=per, base=base, n=n, swap=swap):
            first = flat[pl.ds(pl.multiple_of(base + g * 512, 512), 256), :]
            second = flat[pl.ds(pl.multiple_of(base + g * 512, 512) + 256, 256), :]
            out = dot(swap, jnp.concatenate([first, second], axis=1)).astype(BF)
            row = pl.multiple_of(g * 2 * n, 2 * n)
            for c in range(per):
                piece = out[c * n : (c + 1) * n]
                cols = slice(c * LANES, (c + 1) * LANES)
                ref[pl.ds(row, 2 * n), cols] = jnp.concatenate([piece[:, :LANES], piece[:, LANES:]], axis=0)
            return carry

        lax.fori_loop(0, ref.shape[0] * per // 512, body, 0, unroll=16)
    per_out = width // LANES
    tail = flat[flat.shape[0] - FF // LANES - 8 * per_out : flat.shape[0], :].astype(F32)
    for c in range(FF // LANES):
        b1[0:1, c * LANES : (c + 1) * LANES] = tail[c : c + 1]
    for r in range(8):
        for c in range(per_out):
            k = FF // LANES + r * per_out + c
            vec[r : r + 1, c * LANES : (c + 1) * LANES] = tail[k : k + 1]


def pack_weights(flat, wa, wi, wo, width):
    for ref, per, base in matrix_blocks(wa, wi, wo, width):
        n = 256 // per
        swap = one_hot_swap(n, per)

        def body(g, carry, ref=ref, per=per, base=base, n=n, swap=swap):
            row = pl.multiple_of(g * 2 * n, 2 * n)
            pieces = []
            for c in range(per):
                v = ref[pl.ds(row, 2 * n), c * LANES : (c + 1) * LANES]
                pieces.append(jnp.concatenate([v[:n], v[n:]], axis=1))
            out = dot(swap, jnp.concatenate(pieces, axis=0)).astype(BF)
            first = pl.multiple_of(base + g * 512, 512)
            flat[pl.ds(first, 256), :] = out[:, :LANES]
            flat[pl.ds(first + 256, 256), :] = out[:, LANES:]
            return carry

        lax.fori_loop(0, ref.shape[0] * per // 512, body, 0, unroll=16)


def norm_stats(resid):
    center = resid - jnp.mean(resid, axis=-1, keepdims=True)
    variance = jnp.mean(center * center, axis=-1, keepdims=True)
    inv = lax.rsqrt(variance + norm_eps)
    return center * inv, inv


def norm_grad(upstream, normed, inv, gain):
    scaled = upstream * gain
    m0 = jnp.mean(scaled, axis=-1, keepdims=True)
    m1 = jnp.mean(scaled * normed, axis=-1, keepdims=True)
    return inv * (scaled - m0 - normed * m1)


def colsum(v):
    return jnp.sum(v, axis=0, keepdims=True)


def lane_mask(which, dtype):
    lane = lax.broadcasted_iota(jnp.int32, (1, LANES), 1)
    keep = (lane < 64) if which == 0 else (lane >= 64)
    return jnp.where(keep, 1.0, 0.0).astype(F32).astype(dtype)


C0 = math.sqrt(2.0 / math.pi)


def gelu_pair(u):
    u2 = u * u
    inner = u * (C0 + (C0 * 0.044715) * u2)
    half = 0.5 + 0.5 * jnp.tanh(inner)
    g = u * half
    slope = half + 2.0 * g * (1.0 - half) * (C0 + (3.0 * C0 * 0.044715) * u2)
    return g, slope


def window_starts(shards, tiles):
    return [i * tiles // shards for i in range(shards + 1)]


def own_index():
    return lax.axis_index("dp") * lax.axis_size("rep") + lax.axis_index("rep")


RZ, RX, RC, RY = 8, 4, 2, 1
STEPS = ((RX, RY), (RY, RX), (2 * RZ, RZ), (RZ, 2 * RZ))
SLOTS = 1 << len(STEPS)
PLANES = (3, 2, 1, 0)


def own_core(me):
    return (me // RC) & 1


def slot_owner(base, core, slot):
    owner = base
    for k, (zero, one) in enumerate(STEPS):
        if slot >> (len(STEPS) - 1 - k) & 1:
            owner = jnp.bitwise_xor(owner, jnp.where(core == 0, zero, one))
    return owner


def settle(ref, rows, sem):
    pltpu.make_async_copy(ref.at[pl.ds(0, rows)], ref.at[pl.ds(0, rows)], sem).wait()


def window_moves(owner, height, tiles, shards, edge_row):
    start = pl.multiple_of((owner * tiles // shards) * TILE, TILE)
    edge = pl.multiple_of(edge_row + owner * 2 * TILE, TILE)
    body = height - 2 * TILE
    return [(0, start, body), (body, edge, 2 * TILE)]


def load_windows(w_refs, wide, flat, sem, shards, prepare):
    tiles = flat.shape[0] // TILE
    height = w_refs[0].shape[0]
    edge_row = flat.shape[0] + TILE
    base = tiles // shards * TILE
    me = own_index()
    core = own_core(me)
    for n, ref in enumerate(w_refs):
        side, origin = (core, me) if n < SLOTS else (1 - core, jnp.bitwise_xor(me, RC))
        owner = slot_owner(origin, side, n % SLOTS)
        for at, to, rows in window_moves(owner, height, tiles, shards, edge_row):
            pltpu.make_async_copy(ref.at[pl.ds(at, rows)], wide.at[pl.ds(to, rows)], sem.at[0]).start()
    prepare()
    settle(wide, height * shards, sem.at[0])
    starts = window_starts(shards, tiles)

    def tile(row):
        return wide[row : row + TILE, :]

    for i in range(shards):
        nxt = starts[i + 1]
        row = edge_row + i * 2 * TILE
        if nxt - starts[i] != base // TILE:
            wide[(nxt - 1) * TILE : nxt * TILE, :] = tile(row)
            row = row + TILE
        if i + 1 < shards:
            wide[nxt * TILE : (nxt + 1) * TILE, :] = tile(nxt * TILE) + tile(row)


def store_windows(g_refs, wide, flat, sem, shards, vec_rows):
    tiles = flat.shape[0] // TILE
    height = g_refs[0].shape[1]
    edge_row = flat.shape[0] + TILE
    starts = window_starts(shards, tiles)
    last = lax.broadcasted_iota(jnp.int32, (TILE, LANES), 0) == TILE - 1
    for i in range(shards):
        low = starts[i] * TILE + height - 2 * TILE
        row = edge_row + i * 2 * TILE
        for k in range(2):
            at = low + k * TILE
            if at + TILE <= flat.shape[0]:
                tile = wide[at : at + TILE, :]
            else:
                tile = jnp.zeros((TILE, LANES), BF)
            if k == 1:
                tile = jnp.where(last, vec_rows[i : i + 1], tile.astype(F32)).astype(BF)
            wide[row + k * TILE : row + (k + 1) * TILE, :] = tile
    me = own_index()
    core = own_core(me)
    for n, ref in enumerate(g_refs):
        side, origin = (core, me) if n == 0 else (1 - core, jnp.bitwise_xor(me, RC))
        for k in range(ref.shape[0]):
            plane = k // 4 if n == 0 else PLANES[n - 1]
            slot = 4 * (k % 4) + plane
            owner = slot_owner(origin, side, slot)
            for at, to, rows in window_moves(owner, height, tiles, shards, edge_row):
                pltpu.make_async_copy(wide.at[pl.ds(to, rows)], ref.at[k].at[pl.ds(at, rows)], sem.at[n]).start()
    for n, ref in enumerate(g_refs):
        settle(wide, ref.shape[0] * ref.shape[1], sem.at[n])


CHUNK = 512
STEP = 32
GSTEP = 16
AHEAD = 2


def core_kernel(*refs, width, length, shards, windows, flat_rows):
    n_in = 2 * SLOTS if windows else 1
    (x_ref, cot_ref, seg_ref) = refs[:3]
    w_refs = refs[3 : 3 + n_in]
    refs = refs[3 + n_in :]
    (y_ref, dx_ref) = refs[:2]
    n_out = 1 + len(PLANES) if windows else 1
    g_refs = refs[2 : 2 + n_out]
    (wide, wa, wi, wo, b1, vec, xb, qkv, ab, ctx, xh1, iv1, xh2, iv2, h1b, slope, df, da, dqkv, dc, dr1,
     bias, gb1, gvec, count_ref, sem) = refs[2 + n_out :]
    D = width
    T = length
    pairs = D // LANES
    flat = wide.at[pl.ds(0, flat_rows)]

    count_ref[0] = 1
    single = count_ref[0]
    scale = 0.125

    def prepare():
        seg = seg_ref[...].astype(F32)
        column = jnp.transpose(jnp.broadcast_to(seg, (LANES, T)))[:, 0:1]
        bias[...] = jnp.where(column == seg, 0.0, -1e30).astype(F32)
        dx_ref[...] = x_ref[...].astype(F32)
        gvec[...] = jnp.zeros_like(gvec)

    if windows:
        load_windows(w_refs, wide, flat, sem, shards, prepare)
    else:
        cp = pltpu.make_async_copy(w_refs[0], flat, sem.at[0])
        cp.start()
        prepare()
        cp.wait()
    unpack_weights(flat, wa, wi, wo, b1, vec, D)

    def phase(body):
        def step(_, carry):
            body()
            return carry

        lax.fori_loop(0, single, step, 0)

    hidden = FF * REC * T // LANES

    def put(which, chunk, row, val):
        for j in range(CHUNK // LANES):
            at = which * hidden + (chunk * (CHUNK // LANES) + j) * REC * T
            wide[pl.ds(row + at, val.shape[0]), :] = val[:, j * LANES : (j + 1) * LANES]

    def get(which, chunk, row, n):
        at = [which * hidden + (chunk * (CHUNK // LANES) + j) * REC * T for j in range(CHUNK // LANES)]
        return jnp.concatenate([wide[pl.ds(row + k, n), :] for k in at], axis=1)

    def project(r):
        rows = pl.ds(pl.multiple_of(r * T, T), T)
        x16 = dx_ref[...].astype(BF)
        xb[rows, :] = x16
        for j in range(3):
            p = dot(x16, wa[:, j * D : (j + 1) * D])
            if j == 0:
                p = p + vec[0:1, :]
            if j == 2:
                p = p + vec[1:2, :]
            p = p.astype(BF)
            for c in range(pairs):
                qkv[r, j * pairs + c] = p[:, c * LANES : (c + 1) * LANES]

    def attend(r):
        rows = pl.ds(pl.multiple_of(r * T, T), T)

        def score(h):
            return dot_t(qkv[r, h // 2] * (lane_mask(h % 2, BF) * scale).astype(BF), qkv[r, pairs + h // 2])

        pend = [score(h) for h in range(AHEAD)]
        left = None
        for h in range(HEADS):
            if h + AHEAD < HEADS:
                pend.append(score(h + AHEAD))
            full = pend.pop(0)
            parts = []
            for i in range(0, T, STEP):
                sc = full[i : i + STEP] + bias[i : i + STEP, :]
                ex = jnp.exp(sc - jnp.max(sc, axis=-1, keepdims=True))
                tot = jnp.sum(ex, axis=-1, keepdims=True)
                parts.append((ex * (1.0 / tot)).astype(BF))
                ab[r * HEADS + h, pl.ds(i, STEP), :] = parts[-1]
            out = dot(jnp.concatenate(parts, axis=0), qkv[r, 2 * pairs + h // 2] * lane_mask(h % 2, BF))
            if h % 2 == 0:
                left = out
            else:
                ctx[h // 2, rows, :] = (left + out).astype(BF)

    def feed(r):
        rows = pl.ds(pl.multiple_of(r * T, T), T)
        a = dot(jnp.concatenate([ctx[c, rows, :] for c in range(pairs)], axis=1), wa[:, 3 * D : 4 * D])
        for i in range(0, T, STEP):
            sub = pl.ds(i, STEP)
            hat, inv = norm_stats(dx_ref[sub, :] + (a[i : i + STEP] + vec[2:3, :]))
            xh1[r, sub, :] = hat
            iv1[r, sub, :] = jnp.broadcast_to(inv, (STEP, LANES))
            h1b[pl.ds(pl.multiple_of(r * T, T) + i, STEP), :] = (hat * vec[4:5, :] + vec[5:6, :]).astype(BF)
        h16 = h1b[rows, :]

        def up(c):
            return dot(h16, wi[:, c * CHUNK : (c + 1) * CHUNK])

        pend = [up(c) for c in range(AHEAD)]
        f = None
        for c in range(FF // CHUNK):
            cols = slice(c * CHUNK, (c + 1) * CHUNK)
            if c + AHEAD < FF // CHUNK:
                pend.append(up(c + AHEAD))
            u = pend.pop(0)
            parts = []
            for i in range(0, T, GSTEP):
                g, sl = gelu_pair(u[i : i + GSTEP] + b1[:, cols])
                parts.append(g.astype(BF))
                put(0, c, pl.multiple_of(r * T, T) + i, parts[-1])
                slope[r, pl.ds(i, GSTEP), cols] = sl.astype(BF)
            part = dot(jnp.concatenate(parts, axis=0), wo[cols, :])
            f = part if f is None else f + part
        for i in range(0, T, STEP):
            sub = pl.ds(i, STEP)
            h1 = xh1[r, sub, :] * vec[4:5, :] + vec[5:6, :]
            hat, inv = norm_stats(h1 + (f[i : i + STEP] + vec[3:4, :]))
            xh2[r, sub, :] = hat
            iv2[r, sub, :] = jnp.broadcast_to(inv, (STEP, LANES))
            y = hat * vec[6:7, :] + vec[7:8, :]
            dx_ref[sub, :] = y

    def acc(ref, row, val):
        ref[row : row + 1, :] = ref[row : row + 1, :] + val

    def feed_back(r):
        rows = pl.ds(pl.multiple_of(r * T, T), T)
        sums = [jnp.zeros((8, D), F32) for _ in range(6)]

        def add(k, val):
            sums[k] = sums[k] + jnp.sum(val.reshape(STEP // 8, 8, D), axis=0)

        for i in range(0, T, STEP):
            sub = pl.ds(i, STEP)
            dy = dx_ref[sub, :]
            hat = xh2[r, sub, :]
            add(0, dy * hat)
            add(1, dy)
            dr2 = norm_grad(dy, hat, iv2[r, sub, 0:1], vec[6:7, :])
            dr1[sub, :] = dr2
            d16 = dr2.astype(BF)
            df[pl.ds(pl.multiple_of(r * T, T) + i, STEP), :] = d16
            add(2, d16.astype(F32))
        d16 = df[rows, :]

        def down(c):
            return dot_t(d16, wo[c * CHUNK : (c + 1) * CHUNK, :])

        pend = [down(c) for c in range(AHEAD)]
        dh = None
        for c in range(FF // CHUNK):
            cols = slice(c * CHUNK, (c + 1) * CHUNK)
            if c + AHEAD < FF // CHUNK:
                pend.append(down(c + AHEAD))
            t = pend.pop(0)
            parts = []
            for i in range(0, T, GSTEP):
                g16 = t[i : i + GSTEP].astype(BF) * slope[r, pl.ds(i, GSTEP), cols]
                parts.append(g16)
                put(1, c, pl.multiple_of(r * T, T) + i, g16)
            part = dot_t(jnp.concatenate(parts, axis=0), wi[:, cols])
            dh = part if dh is None else dh + part
        for i in range(0, T, STEP):
            sub = pl.ds(i, STEP)
            hat = xh1[r, sub, :]
            upstream = dr1[sub, :] + dh[i : i + STEP]
            add(3, upstream * hat)
            add(4, upstream)
            d1 = norm_grad(upstream, hat, iv1[r, sub, 0:1], vec[4:5, :])
            dr1[sub, :] = d1
            a16 = d1.astype(BF)
            da[pl.ds(pl.multiple_of(r * T, T) + i, STEP), :] = a16
            add(5, a16.astype(F32))
        for row, k in ((6, 0), (7, 1), (3, 2), (4, 3), (5, 4), (2, 5)):
            acc(gvec, row, colsum(sums[k]))
        c16 = dot_t(da[rows, :], wa[:, 3 * D : 4 * D]).astype(BF)
        for c in range(pairs):
            dc[c] = c16[:, c * LANES : (c + 1) * LANES]

    def attend_back(r):
        rows = pl.ds(pl.multiple_of(r * T, T), T)

        def rise(h):
            return dot_t(dc[h // 2] * lane_mask(h % 2, BF), qkv[r, 2 * pairs + h // 2])

        pend = [rise(h) for h in range(AHEAD)]
        for h in range(HEADS):
            if h + AHEAD < HEADS:
                pend.append(rise(h + AHEAD))
            full = pend.pop(0)
            p, e = h // 2, h % 2
            half = slice(64 * e, 64 * e + 64)
            if e == 0:
                qt = jnp.transpose(qkv[r, p])
                ct = jnp.transpose(dc[p])
                dkt, dvt = [], []
            p16 = ab[r * HEADS + h]
            parts = []
            for i in range(0, T, STEP):
                pf = p16[i : i + STEP].astype(F32)
                t = full[i : i + STEP] * pf
                parts.append((t - pf * jnp.sum(t, axis=-1, keepdims=True)).astype(BF))
            s16 = jnp.concatenate(parts, axis=0)
            part = dot(s16, qkv[r, pairs + p] * lane_mask(e, BF))
            dkt.append(dot(qt[half], s16))
            dvt.append(dot(ct[half], p16))
            if e == 0:
                dq = part
            else:
                dqkv[p, rows, :] = ((dq + part) * scale).astype(BF)
                dqkv[pairs + p, rows, :] = jnp.transpose((jnp.concatenate(dkt, axis=0) * scale).astype(BF))
                dqkv[2 * pairs + p, rows, :] = jnp.transpose(jnp.concatenate(dvt, axis=0).astype(BF))
    def project_back(r):
        rows = pl.ds(pl.multiple_of(r * T, T), T)
        for c in range(pairs):
            cols = slice(c * LANES, (c + 1) * LANES)
            gvec[0:1, cols] = gvec[0:1, cols] + colsum(dqkv[c, rows, :].astype(F32))
            gvec[1:2, cols] = gvec[1:2, cols] + colsum(dqkv[2 * pairs + c, rows, :].astype(F32))
        d3 = jnp.concatenate([dqkv[c, rows, :] for c in range(3 * pairs)], axis=1)
        dx_ref[...] = dr1[...] + dot_t(d3, wa[:, : 3 * D])

    def forward(r, carry):
        def first():
            project(r)
            attend(r)

        phase(first)
        phase(functools.partial(feed, r))
        return carry

    def backward(i, carry):
        r = REC - 1 - i

        def second():
            attend_back(r)
            project_back(r)

        phase(functools.partial(feed_back, r))
        phase(second)
        return carry

    lax.fori_loop(0, REC, forward, 0)
    y_ref[...] = dx_ref[...]
    dx_ref[...] = cot_ref[...].astype(F32)
    lax.fori_loop(0, REC, backward, 0)

    def grad_qkvo():
        xt = jnp.transpose(xb[...])
        for j in range(3):
            d3 = jnp.concatenate([dqkv[j * pairs + c] for c in range(pairs)], axis=1)
            wa[:, j * D : (j + 1) * D] = dot(xt, d3).astype(BF)
        for c in range(pairs):
            wa[c * LANES : (c + 1) * LANES, 3 * D : 4 * D] = t_dot(ctx[c], da[...]).astype(BF)

    def grad_in():
        ht = jnp.concatenate([jnp.transpose(h1b[...]), jnp.ones((16, REC * T), BF)], axis=0)
        for c in range(FF // CHUNK):
            cols = slice(c * CHUNK, (c + 1) * CHUNK)
            grad = dot(ht, get(1, c, 0, REC * T))
            wi[:, cols] = grad[:D].astype(BF)
            gb1[0:1, cols] = grad[D : D + 1]

    def grad_out():
        for c in range(FF // CHUNK):
            cols = slice(c * CHUNK, (c + 1) * CHUNK)
            wo[cols, :] = t_dot(get(0, c, 0, REC * T), df[...]).astype(BF)

    def grads():
        grad_qkvo()
        grad_in()
        grad_out()

    phase(grads)
    pack_weights(flat, wa, wi, wo, D)
    per_out = D // LANES
    rows = [gb1[0:1, c * LANES : (c + 1) * LANES] for c in range(FF // LANES)]
    for r in range(8):
        rows = rows + [gvec[r : r + 1, c * LANES : (c + 1) * LANES] for c in range(per_out)]
    tail = jnp.concatenate(rows, axis=0)
    flat[flat.shape[0] - len(rows) : flat.shape[0], :] = tail.astype(BF)
    if windows:
        store_windows(g_refs, wide, flat, sem, shards, tail[FF // LANES :])
    else:
        cp = pltpu.make_async_copy(flat, g_refs[0], sem.at[0])
        cp.start()
        cp.wait()


def core(x, cot, seg, flats, windows, shards, rows):
    T, D = x.shape
    vm = pltpu.VMEM
    pairs = D // LANES
    scratch = [
        vm((max(2 * FF * REC * T // LANES, rows + TILE + 2 * TILE * shards), LANES), BF),
        vm((D, 4 * D), BF), vm((D, FF), BF), vm((FF, D), BF), vm((1, FF), F32), vm((8, D), F32),
        vm((REC * T, D), BF), vm((REC, 3 * pairs, T, LANES), BF), vm((REC * HEADS, T, T), BF), vm((pairs, REC * T, LANES), BF),
        vm((REC, T, D), F32), vm((REC, T, LANES), F32), vm((REC, T, D), F32), vm((REC, T, LANES), F32),
        vm((REC * T, D), BF), vm((REC, T, FF), BF),
        vm((REC * T, D), BF), vm((REC * T, D), BF), vm((3 * pairs, REC * T, LANES), BF), vm((pairs, T, LANES), BF),
        vm((T, D), F32), vm((T, T), F32),
        vm((1, FF), F32), vm((8, D), F32),
        pltpu.SMEM((1,), jnp.int32), pltpu.SemaphoreType.DMA((8,)),
    ]
    if windows:
        g_shapes = [jax.ShapeDtypeStruct((n, flats[0].shape[0], LANES), BF) for n in (SLOTS, 4, 4, 4, 4)]
    else:
        g_shapes = [jax.ShapeDtypeStruct((rows, LANES), BF)]
    in_vmem = pl.BlockSpec(memory_space=pltpu.VMEM)
    anywhere = pl.BlockSpec(memory_space=pl.ANY)
    return pl.pallas_call(
        functools.partial(core_kernel, width=D, length=T, shards=shards, windows=windows, flat_rows=rows),
        out_shape=tuple([jax.ShapeDtypeStruct((T, D), F32)] * 2 + g_shapes),
        in_specs=[in_vmem] * 3 + [anywhere] * len(flats),
        out_specs=tuple([in_vmem] * 2 + [anywhere] * len(g_shapes)),
        scratch_shapes=scratch,
        compiler_params=pltpu.CompilerParams(vmem_limit_bytes=54 * 1024 * 1024),
        name="layer_core",
    )(x, cot, seg, *flats)


AXES = ("dp", "rep")


def exchange(v, step):
    count = lax.axis_size("dp") * lax.axis_size("rep")
    zero, one = STEPS[step] if step < len(STEPS) else (RC, RC)
    return lax.ppermute(v, AXES, [(j, j ^ (one if j // RC & 1 else zero)) for j in range(count)])


def after(v, earlier):
    return lax.optimization_barrier((v, earlier))[0]


def gather_windows(own):
    next_plane = exchange(own, 3)
    near = [None] * SLOTS
    planes = [own, next_plane, exchange(after(own, next_plane), 2), exchange(next_plane, 2)]
    for m, v in enumerate(planes):
        side = exchange(v, 0)
        near[m], near[8 + m], near[4 + m], near[12 + m] = v, side, exchange(v, 1), exchange(side, 1)
    late = near[8 + 2]
    return near + [exchange(after(v, late) if n % 4 < 2 else v, 4) for n, v in enumerate(near)]


def total(*parts):
    v = parts[0].astype(F32)
    for part in parts[1:]:
        v = v + part.astype(F32)
    return v.astype(BF)


def sum_windows(keep, *sent):
    got = {m: exchange(v, 4) for m, v in zip(PLANES, sent)}
    side, back, last = {}, {}, [None]

    def add(*parts):
        if last[0] is not None:
            parts = (*parts[:-1], after(parts[-1], last[0]))
        last[0] = total(*parts)
        return last[0]

    def single(m):
        far = exchange(add(keep[4 * m + 3], got[m][3]), 0)
        side[m] = (exchange(add(keep[4 * m + 2], got[m][2]), 0), far)

    def pair(m):
        side[m] = exchange(add(keep[4 * m + 2 : 4 * m + 4], got[m][2:]), 0)

    def second(m):
        back[m] = exchange(add(keep[4 * m + 1], got[m][1], side[m][1]), 1)

    def plane(m):
        return (keep[4 * m], got[m][0], side[m][0], back[m])

    single(3)
    single(2)
    second(3)
    second(2)
    pair(1)
    pair(0)
    turn = exchange(add(*plane(3)), 2)
    second(1)
    two = exchange(add(*plane(2)), 2)
    one = exchange(add(*plane(1), turn), 3)
    second(0)
    return (*plane(0), one, two)


def shards_fn(block_input, segment_ids, cotangent, master_weights, momentum, weight_average):
    width = block_input.shape[2]
    length = block_input.shape[1]
    count = lax.axis_size("dp") * lax.axis_size("rep")
    share = master_weights.shape[0]
    rows = share * count // LANES
    tiles = rows // TILE
    args = (block_input[0], cotangent[0], segment_ids)
    if count == 32:
        window = (tiles // count + 2) * TILE
        first = (own_index() * share) % (TILE * LANES)
        padded = jnp.pad(master_weights, (TILE * LANES, window * LANES - share))
        own = lax.dynamic_slice(padded, (TILE * LANES - first,), (window * LANES,)).astype(BF).reshape(window, LANES)
        block_output, input_grad, *sums = core(*args, gather_windows(own), True, count, rows)
        addends = sum_windows(*sums)
        grad = addends[0].astype(F32)
        for addend in addends[1:]:
            grad = grad + addend.astype(F32)
        weight_grad = lax.dynamic_slice(grad.reshape(-1), (first,), (share,))
        vector_grad = grad[window - 1]
    else:
        flat = lax.all_gather(master_weights.astype(BF), AXES, axis=0, tiled=True).reshape(rows, LANES)
        block_output, input_grad, grad = core(*args, [flat], False, count, rows)
        grad = grad.reshape(-1).astype(F32)
        weight_grad = lax.psum_scatter(grad, AXES, scatter_dimension=0, tiled=True)
        vector_grad = lax.psum_scatter(grad[grad.shape[0] - 8 * width :], AXES, scatter_dimension=0, tiled=True)
    token_count = block_input.shape[0] * length * count
    rate = rate_base / math.sqrt(token_count)
    new_momentum = mom_decay * momentum + weight_grad
    new_weights = master_weights - rate * (weight_grad + mom_decay * new_momentum)
    new_average = avg_keep * weight_average + (1.0 - avg_keep) * new_weights
    return (
        block_output[None],
        input_grad[None],
        weight_grad,
        vector_grad,
        new_momentum,
        new_average,
        new_weights,
    )


def solution(mesh):
    three = P(AXES, None, None)
    two = P(AXES, None)
    one = P(AXES)
    return jax.shard_map(
        shards_fn,
        mesh=mesh,
        in_specs=(three, two, three, one, one, one),
        out_specs=(three, three, one, one, one, one, one),
        check_vma=False,
    )
```

```python
import functools
import math

import jax
import jax.numpy as jnp
from jax import lax
from jax.experimental import pallas as pl
from jax.experimental.pallas import tpu as pltpu
from jax.sharding import PartitionSpec as P

FF = 2048
HEADS = 8
REC = 2
TILE = 8
LANES = 128

norm_eps = 1e-05
mom_decay = 0.9
avg_keep = 0.8
rate_base = 0.006

BF = jnp.bfloat16
F32 = jnp.float32


def dot(a, b):
    return lax.dot_general(a, b, (((1,), (0,)), ((), ())), preferred_element_type=F32)


def dot_t(a, b):
    return lax.dot_general(a, b, (((1,), (1,)), ((), ())), preferred_element_type=F32)


def t_dot(a, b):
    return lax.dot_general(a, b, (((0,), (0,)), ((), ())), preferred_element_type=F32)


def one_hot_swap(outer, inner):
    size = outer * inner
    row = lax.broadcasted_iota(jnp.int32, (size, size), 0)
    col = lax.broadcasted_iota(jnp.int32, (size, size), 1)
    shift = inner.bit_length() - 1
    want = (row & (inner - 1)) * outer + (row >> shift)
    return jnp.where(col == want, 1.0, 0.0).astype(F32).astype(BF)


def matrix_blocks(wa, wi, wo, width):
    per = 4 * width // LANES
    base = 0
    for ref, per in ((wa, per), (wi, FF // LANES), (wo, width // LANES)):
        yield ref, per, base
        base = base + ref.shape[0] * per


def unpack_weights(flat, wa, wi, wo, b1, vec, width):
    for ref, per, base in matrix_blocks(wa, wi, wo, width):
        n = 256 // per
        swap = one_hot_swap(per, n)

        def body(g, carry, ref=ref, per=per, base=base, n=n, swap=swap):
            first = flat[pl.ds(pl.multiple_of(base + g * 512, 512), 256), :]
            second = flat[pl.ds(pl.multiple_of(base + g * 512, 512) + 256, 256), :]
            out = dot(swap, jnp.concatenate([first, second], axis=1)).astype(BF)
            row = pl.multiple_of(g * 2 * n, 2 * n)
            for c in range(per):
                piece = out[c * n : (c + 1) * n]
                cols = slice(c * LANES, (c + 1) * LANES)
                ref[pl.ds(row, 2 * n), cols] = jnp.concatenate([piece[:, :LANES], piece[:, LANES:]], axis=0)
            return carry

        lax.fori_loop(0, ref.shape[0] * per // 512, body, 0, unroll=16)
    per_out = width // LANES
    tail = flat[flat.shape[0] - FF // LANES - 8 * per_out : flat.shape[0], :].astype(F32)
    for c in range(FF // LANES):
        b1[0:1, c * LANES : (c + 1) * LANES] = tail[c : c + 1]
    for r in range(8):
        for c in range(per_out):
            k = FF // LANES + r * per_out + c
            vec[r : r + 1, c * LANES : (c + 1) * LANES] = tail[k : k + 1]


def pack_weights(flat, wa, wi, wo, width):
    for ref, per, base in matrix_blocks(wa, wi, wo, width):
        n = 256 // per
        swap = one_hot_swap(n, per)

        def body(g, carry, ref=ref, per=per, base=base, n=n, swap=swap):
            row = pl.multiple_of(g * 2 * n, 2 * n)
            pieces = []
            for c in range(per):
                v = ref[pl.ds(row, 2 * n), c * LANES : (c + 1) * LANES]
                pieces.append(jnp.concatenate([v[:n], v[n:]], axis=1))
            out = dot(swap, jnp.concatenate(pieces, axis=0)).astype(BF)
            first = pl.multiple_of(base + g * 512, 512)
            flat[pl.ds(first, 256), :] = out[:, :LANES]
            flat[pl.ds(first + 256, 256), :] = out[:, LANES:]
            return carry

        lax.fori_loop(0, ref.shape[0] * per // 512, body, 0, unroll=16)


def norm_stats(resid):
    center = resid - jnp.mean(resid, axis=-1, keepdims=True)
    variance = jnp.mean(center * center, axis=-1, keepdims=True)
    inv = lax.rsqrt(variance + norm_eps)
    return center * inv, inv


def norm_grad(upstream, normed, inv, gain):
    scaled = upstream * gain
    m0 = jnp.mean(scaled, axis=-1, keepdims=True)
    m1 = jnp.mean(scaled * normed, axis=-1, keepdims=True)
    return inv * (scaled - m0 - normed * m1)


def colsum(v):
    return jnp.sum(v, axis=0, keepdims=True)


def lane_mask(which, dtype):
    lane = lax.broadcasted_iota(jnp.int32, (1, LANES), 1)
    keep = (lane < 64) if which == 0 else (lane >= 64)
    return jnp.where(keep, 1.0, 0.0).astype(F32).astype(dtype)


C0 = math.sqrt(2.0 / math.pi)


def gelu_pair(u):
    u2 = u * u
    inner = u * (C0 + (C0 * 0.044715) * u2)
    half = 0.5 + 0.5 * jnp.tanh(inner)
    g = u * half
    slope = half + 2.0 * g * (1.0 - half) * (C0 + (3.0 * C0 * 0.044715) * u2)
    return g, slope


def window_starts(shards, tiles):
    return [i * tiles // shards for i in range(shards + 1)]


def own_index():
    return lax.axis_index("dp") * lax.axis_size("rep") + lax.axis_index("rep")


RZ, RX, RC, RY = 8, 4, 2, 1
STEPS = ((RX, RY), (RY, RX), (2 * RZ, RZ), (RZ, 2 * RZ))
SLOTS = 1 << len(STEPS)
PLANES = (3, 2, 1, 0)


def own_core(me):
    return (me // RC) & 1


def slot_owner(base, core, slot):
    owner = base
    for k, (zero, one) in enumerate(STEPS):
        if slot >> (len(STEPS) - 1 - k) & 1:
            owner = jnp.bitwise_xor(owner, jnp.where(core == 0, zero, one))
    return owner


def settle(ref, rows, sem):
    pltpu.make_async_copy(ref.at[pl.ds(0, rows)], ref.at[pl.ds(0, rows)], sem).wait()


def window_moves(owner, height, tiles, shards, edge_row):
    start = pl.multiple_of((owner * tiles // shards) * TILE, TILE)
    edge = pl.multiple_of(edge_row + owner * 2 * TILE, TILE)
    body = height - 2 * TILE
    return [(0, start, body), (body, edge, 2 * TILE)]


def load_windows(w_refs, wide, flat, sem, shards, prepare):
    tiles = flat.shape[0] // TILE
    height = w_refs[0].shape[0]
    edge_row = flat.shape[0] + TILE
    base = tiles // shards * TILE
    me = own_index()
    core = own_core(me)
    for n, ref in enumerate(w_refs):
        side, origin = (core, me) if n < SLOTS else (1 - core, jnp.bitwise_xor(me, RC))
        owner = slot_owner(origin, side, n % SLOTS)
        for at, to, rows in window_moves(owner, height, tiles, shards, edge_row):
            pltpu.make_async_copy(ref.at[pl.ds(at, rows)], wide.at[pl.ds(to, rows)], sem.at[0]).start()
    prepare()
    settle(wide, height * shards, sem.at[0])
    starts = window_starts(shards, tiles)

    def tile(row):
        return wide[row : row + TILE, :]

    for i in range(shards):
        nxt = starts[i + 1]
        row = edge_row + i * 2 * TILE
        if nxt - starts[i] != base // TILE:
            wide[(nxt - 1) * TILE : nxt * TILE, :] = tile(row)
            row = row + TILE
        if i + 1 < shards:
            wide[nxt * TILE : (nxt + 1) * TILE, :] = tile(nxt * TILE) + tile(row)


def store_windows(g_refs, wide, flat, sem, shards, vec_rows):
    tiles = flat.shape[0] // TILE
    height = g_refs[0].shape[1]
    edge_row = flat.shape[0] + TILE
    starts = window_starts(shards, tiles)
    last = lax.broadcasted_iota(jnp.int32, (TILE, LANES), 0) == TILE - 1
    for i in range(shards):
        low = starts[i] * TILE + height - 2 * TILE
        row = edge_row + i * 2 * TILE
        for k in range(2):
            at = low + k * TILE
            if at + TILE <= flat.shape[0]:
                tile = wide[at : at + TILE, :]
            else:
                tile = jnp.zeros((TILE, LANES), BF)
            if k == 1:
                tile = jnp.where(last, vec_rows[i : i + 1], tile.astype(F32)).astype(BF)
            wide[row + k * TILE : row + (k + 1) * TILE, :] = tile
    me = own_index()
    core = own_core(me)
    for n, ref in enumerate(g_refs):
        side, origin = (core, me) if n == 0 else (1 - core, jnp.bitwise_xor(me, RC))
        for k in range(ref.shape[0]):
            plane = k // 4 if n == 0 else PLANES[n - 1]
            slot = 4 * (k % 4) + plane
            owner = slot_owner(origin, side, slot)
            for at, to, rows in window_moves(owner, height, tiles, shards, edge_row):
                pltpu.make_async_copy(wide.at[pl.ds(to, rows)], ref.at[k].at[pl.ds(at, rows)], sem.at[n]).start()
    for n, ref in enumerate(g_refs):
        settle(wide, ref.shape[0] * ref.shape[1], sem.at[n])


CHUNK = 512
STEP = 32
GSTEP = 16
AHEAD = 2


def core_kernel(*refs, width, length, shards, windows, flat_rows):
    n_in = 2 * SLOTS if windows else 1
    (x_ref, cot_ref, seg_ref) = refs[:3]
    w_refs = refs[3 : 3 + n_in]
    refs = refs[3 + n_in :]
    (y_ref, dx_ref) = refs[:2]
    n_out = 1 + len(PLANES) if windows else 1
    g_refs = refs[2 : 2 + n_out]
    (wide, wa, wi, wo, b1, vec, xb, qkv, ab, ctx, xh1, iv1, xh2, iv2, h1b, slope, df, da, dqkv, dc, dr1,
     bias, gb1, gvec, count_ref, sem) = refs[2 + n_out :]
    D = width
    T = length
    pairs = D // LANES
    flat = wide.at[pl.ds(0, flat_rows)]

    count_ref[0] = 1
    single = count_ref[0]
    scale = 0.125

    def prepare():
        seg = seg_ref[...].astype(F32)
        column = jnp.transpose(jnp.broadcast_to(seg, (LANES, T)))[:, 0:1]
        bias[...] = jnp.where(column == seg, 0.0, -1e30).astype(F32)
        dx_ref[...] = x_ref[...].astype(F32)
        gvec[...] = jnp.zeros_like(gvec)

    if windows:
        load_windows(w_refs, wide, flat, sem, shards, prepare)
    else:
        cp = pltpu.make_async_copy(w_refs[0], flat, sem.at[0])
        cp.start()
        prepare()
        cp.wait()
    unpack_weights(flat, wa, wi, wo, b1, vec, D)

    def phase(body):
        def step(_, carry):
            body()
            return carry

        lax.fori_loop(0, single, step, 0)

    hidden = FF * REC * T // LANES

    def put(which, chunk, row, val):
        for j in range(CHUNK // LANES):
            at = which * hidden + (chunk * (CHUNK // LANES) + j) * REC * T
            wide[pl.ds(row + at, val.shape[0]), :] = val[:, j * LANES : (j + 1) * LANES]

    def get(which, chunk, row, n):
        at = [which * hidden + (chunk * (CHUNK // LANES) + j) * REC * T for j in range(CHUNK // LANES)]
        return jnp.concatenate([wide[pl.ds(row + k, n), :] for k in at], axis=1)

    def project(r):
        rows = pl.ds(pl.multiple_of(r * T, T), T)
        x16 = dx_ref[...].astype(BF)
        xb[rows, :] = x16
        for j in range(3):
            p = dot(x16, wa[:, j * D : (j + 1) * D])
            if j == 0:
                p = p + vec[0:1, :]
            if j == 2:
                p = p + vec[1:2, :]
            p = p.astype(BF)
            for c in range(pairs):
                qkv[r, j * pairs + c] = p[:, c * LANES : (c + 1) * LANES]

    def attend(r):
        rows = pl.ds(pl.multiple_of(r * T, T), T)

        def score(h):
            return dot_t(qkv[r, h // 2] * (lane_mask(h % 2, BF) * scale).astype(BF), qkv[r, pairs + h // 2])

        pend = [score(h) for h in range(AHEAD)]
        left = None
        for h in range(HEADS):
            if h + AHEAD < HEADS:
                pend.append(score(h + AHEAD))
            full = pend.pop(0)
            parts = []
            for i in range(0, T, STEP):
                sc = full[i : i + STEP] + bias[i : i + STEP, :]
                ex = jnp.exp(sc - jnp.max(sc, axis=-1, keepdims=True))
                tot = jnp.sum(ex, axis=-1, keepdims=True)
                parts.append((ex * (1.0 / tot)).astype(BF))
                ab[r * HEADS + h, pl.ds(i, STEP), :] = parts[-1]
            out = dot(jnp.concatenate(parts, axis=0), qkv[r, 2 * pairs + h // 2] * lane_mask(h % 2, BF))
            if h % 2 == 0:
                left = out
            else:
                ctx[h // 2, rows, :] = (left + out).astype(BF)

    def feed(r):
        rows = pl.ds(pl.multiple_of(r * T, T), T)
        a = dot(jnp.concatenate([ctx[c, rows, :] for c in range(pairs)], axis=1), wa[:, 3 * D : 4 * D])
        for i in range(0, T, STEP):
            sub = pl.ds(i, STEP)
            hat, inv = norm_stats(dx_ref[sub, :] + (a[i : i + STEP] + vec[2:3, :]))
            xh1[r, sub, :] = hat
            iv1[r, sub, :] = jnp.broadcast_to(inv, (STEP, LANES))
            h1b[pl.ds(pl.multiple_of(r * T, T) + i, STEP), :] = (hat * vec[4:5, :] + vec[5:6, :]).astype(BF)
        h16 = h1b[rows, :]

        def up(c):
            return dot(h16, wi[:, c * CHUNK : (c + 1) * CHUNK])

        pend = [up(c) for c in range(AHEAD)]
        f = None
        for c in range(FF // CHUNK):
            cols = slice(c * CHUNK, (c + 1) * CHUNK)
            if c + AHEAD < FF // CHUNK:
                pend.append(up(c + AHEAD))
            u = pend.pop(0)
            parts = []
            for i in range(0, T, GSTEP):
                g, sl = gelu_pair(u[i : i + GSTEP] + b1[:, cols])
                parts.append(g.astype(BF))
                put(0, c, pl.multiple_of(r * T, T) + i, parts[-1])
                slope[r, pl.ds(i, GSTEP), cols] = sl.astype(BF)
            part = dot(jnp.concatenate(parts, axis=0), wo[cols, :])
            f = part if f is None else f + part
        for i in range(0, T, STEP):
            sub = pl.ds(i, STEP)
            h1 = xh1[r, sub, :] * vec[4:5, :] + vec[5:6, :]
            hat, inv = norm_stats(h1 + (f[i : i + STEP] + vec[3:4, :]))
            xh2[r, sub, :] = hat
            iv2[r, sub, :] = jnp.broadcast_to(inv, (STEP, LANES))
            y = hat * vec[6:7, :] + vec[7:8, :]
            dx_ref[sub, :] = y

    def acc(ref, row, val):
        ref[row : row + 1, :] = ref[row : row + 1, :] + val

    def feed_back(r):
        rows = pl.ds(pl.multiple_of(r * T, T), T)
        sums = [jnp.zeros((8, D), F32) for _ in range(6)]

        def add(k, val):
            sums[k] = sums[k] + jnp.sum(val.reshape(STEP // 8, 8, D), axis=0)

        for i in range(0, T, STEP):
            sub = pl.ds(i, STEP)
            dy = dx_ref[sub, :]
            hat = xh2[r, sub, :]
            add(0, dy * hat)
            add(1, dy)
            dr2 = norm_grad(dy, hat, iv2[r, sub, 0:1], vec[6:7, :])
            dr1[sub, :] = dr2
            d16 = dr2.astype(BF)
            df[pl.ds(pl.multiple_of(r * T, T) + i, STEP), :] = d16
            add(2, d16.astype(F32))
        d16 = df[rows, :]

        def down(c):
            return dot_t(d16, wo[c * CHUNK : (c + 1) * CHUNK, :])

        pend = [down(c) for c in range(AHEAD)]
        dh = None
        for c in range(FF // CHUNK):
            cols = slice(c * CHUNK, (c + 1) * CHUNK)
            if c + AHEAD < FF // CHUNK:
                pend.append(down(c + AHEAD))
            t = pend.pop(0)
            parts = []
            for i in range(0, T, GSTEP):
                g16 = t[i : i + GSTEP].astype(BF) * slope[r, pl.ds(i, GSTEP), cols]
                parts.append(g16)
                put(1, c, pl.multiple_of(r * T, T) + i, g16)
            part = dot_t(jnp.concatenate(parts, axis=0), wi[:, cols])
            dh = part if dh is None else dh + part
        for i in range(0, T, STEP):
            sub = pl.ds(i, STEP)
            hat = xh1[r, sub, :]
            upstream = dr1[sub, :] + dh[i : i + STEP]
            add(3, upstream * hat)
            add(4, upstream)
            d1 = norm_grad(upstream, hat, iv1[r, sub, 0:1], vec[4:5, :])
            dr1[sub, :] = d1
            a16 = d1.astype(BF)
            da[pl.ds(pl.multiple_of(r * T, T) + i, STEP), :] = a16
            add(5, a16.astype(F32))
        for row, k in ((6, 0), (7, 1), (3, 2), (4, 3), (5, 4), (2, 5)):
            acc(gvec, row, colsum(sums[k]))
        c16 = dot_t(da[rows, :], wa[:, 3 * D : 4 * D]).astype(BF)
        for c in range(pairs):
            dc[c] = c16[:, c * LANES : (c + 1) * LANES]

    def attend_back(r):
        rows = pl.ds(pl.multiple_of(r * T, T), T)

        def rise(h):
            return dot_t(dc[h // 2] * lane_mask(h % 2, BF), qkv[r, 2 * pairs + h // 2])

        pend = [rise(h) for h in range(AHEAD)]
        for h in range(HEADS):
            if h + AHEAD < HEADS:
                pend.append(rise(h + AHEAD))
            full = pend.pop(0)
            p, e = h // 2, h % 2
            half = slice(64 * e, 64 * e + 64)
            if e == 0:
                qt = jnp.transpose(qkv[r, p])
                ct = jnp.transpose(dc[p])
                dkt, dvt = [], []
            p16 = ab[r * HEADS + h]
            parts = []
            for i in range(0, T, STEP):
                pf = p16[i : i + STEP].astype(F32)
                t = full[i : i + STEP] * pf
                parts.append((t - pf * jnp.sum(t, axis=-1, keepdims=True)).astype(BF))
            s16 = jnp.concatenate(parts, axis=0)
            part = dot(s16, qkv[r, pairs + p] * lane_mask(e, BF))
            dkt.append(dot(qt[half], s16))
            dvt.append(dot(ct[half], p16))
            if e == 0:
                dq = part
            else:
                dqkv[p, rows, :] = ((dq + part) * scale).astype(BF)
                dqkv[pairs + p, rows, :] = jnp.transpose((jnp.concatenate(dkt, axis=0) * scale).astype(BF))
                dqkv[2 * pairs + p, rows, :] = jnp.transpose(jnp.concatenate(dvt, axis=0).astype(BF))
    def project_back(r):
        rows = pl.ds(pl.multiple_of(r * T, T), T)
        for c in range(pairs):
            cols = slice(c * LANES, (c + 1) * LANES)
            gvec[0:1, cols] = gvec[0:1, cols] + colsum(dqkv[c, rows, :].astype(F32))
            gvec[1:2, cols] = gvec[1:2, cols] + colsum(dqkv[2 * pairs + c, rows, :].astype(F32))
        d3 = jnp.concatenate([dqkv[c, rows, :] for c in range(3 * pairs)], axis=1)
        dx_ref[...] = dr1[...] + dot_t(d3, wa[:, : 3 * D])

    def forward(r, carry):
        def first():
            project(r)
            attend(r)

        phase(first)
        phase(functools.partial(feed, r))
        return carry

    def backward(i, carry):
        r = REC - 1 - i

        def second():
            attend_back(r)
            project_back(r)

        phase(functools.partial(feed_back, r))
        phase(second)
        return carry

    lax.fori_loop(0, REC, forward, 0)
    y_ref[...] = dx_ref[...]
    dx_ref[...] = cot_ref[...].astype(F32)
    lax.fori_loop(0, REC, backward, 0)

    def grad_qkvo():
        xt = jnp.transpose(xb[...])
        for j in range(3):
            d3 = jnp.concatenate([dqkv[j * pairs + c] for c in range(pairs)], axis=1)
            wa[:, j * D : (j + 1) * D] = dot(xt, d3).astype(BF)
        for c in range(pairs):
            wa[c * LANES : (c + 1) * LANES, 3 * D : 4 * D] = t_dot(ctx[c], da[...]).astype(BF)

    def grad_in():
        ht = jnp.concatenate([jnp.transpose(h1b[...]), jnp.ones((16, REC * T), BF)], axis=0)
        for c in range(FF // CHUNK):
            cols = slice(c * CHUNK, (c + 1) * CHUNK)
            grad = dot(ht, get(1, c, 0, REC * T))
            wi[:, cols] = grad[:D].astype(BF)
            gb1[0:1, cols] = grad[D : D + 1]

    def grad_out():
        for c in range(FF // CHUNK):
            cols = slice(c * CHUNK, (c + 1) * CHUNK)
            wo[cols, :] = t_dot(get(0, c, 0, REC * T), df[...]).astype(BF)

    def grads():
        grad_qkvo()
        grad_in()
        grad_out()

    phase(grads)
    pack_weights(flat, wa, wi, wo, D)
    per_out = D // LANES
    rows = [gb1[0:1, c * LANES : (c + 1) * LANES] for c in range(FF // LANES)]
    for r in range(8):
        rows = rows + [gvec[r : r + 1, c * LANES : (c + 1) * LANES] for c in range(per_out)]
    tail = jnp.concatenate(rows, axis=0)
    flat[flat.shape[0] - len(rows) : flat.shape[0], :] = tail.astype(BF)
    if windows:
        store_windows(g_refs, wide, flat, sem, shards, tail[FF // LANES :])
    else:
        cp = pltpu.make_async_copy(flat, g_refs[0], sem.at[0])
        cp.start()
        cp.wait()


def core(x, cot, seg, flats, windows, shards, rows):
    T, D = x.shape
    vm = pltpu.VMEM
    pairs = D // LANES
    scratch = [
        vm((max(2 * FF * REC * T // LANES, rows + TILE + 2 * TILE * shards), LANES), BF),
        vm((D, 4 * D), BF), vm((D, FF), BF), vm((FF, D), BF), vm((1, FF), F32), vm((8, D), F32),
        vm((REC * T, D), BF), vm((REC, 3 * pairs, T, LANES), BF), vm((REC * HEADS, T, T), BF), vm((pairs, REC * T, LANES), BF),
        vm((REC, T, D), F32), vm((REC, T, LANES), F32), vm((REC, T, D), F32), vm((REC, T, LANES), F32),
        vm((REC * T, D), BF), vm((REC, T, FF), BF),
        vm((REC * T, D), BF), vm((REC * T, D), BF), vm((3 * pairs, REC * T, LANES), BF), vm((pairs, T, LANES), BF),
        vm((T, D), F32), vm((T, T), F32),
        vm((1, FF), F32), vm((8, D), F32),
        pltpu.SMEM((1,), jnp.int32), pltpu.SemaphoreType.DMA((8,)),
    ]
    if windows:
        g_shapes = [jax.ShapeDtypeStruct((n, flats[0].shape[0], LANES), BF) for n in (SLOTS, 4, 4, 4, 4)]
    else:
        g_shapes = [jax.ShapeDtypeStruct((rows, LANES), BF)]
    in_vmem = pl.BlockSpec(memory_space=pltpu.VMEM)
    anywhere = pl.BlockSpec(memory_space=pl.ANY)
    return pl.pallas_call(
        functools.partial(core_kernel, width=D, length=T, shards=shards, windows=windows, flat_rows=rows),
        out_shape=tuple([jax.ShapeDtypeStruct((T, D), F32)] * 2 + g_shapes),
        in_specs=[in_vmem] * 3 + [anywhere] * len(flats),
        out_specs=tuple([in_vmem] * 2 + [anywhere] * len(g_shapes)),
        scratch_shapes=scratch,
        compiler_params=pltpu.CompilerParams(vmem_limit_bytes=54 * 1024 * 1024),
        name="layer_core",
    )(x, cot, seg, *flats)


AXES = ("dp", "rep")


def exchange(v, step):
    count = lax.axis_size("dp") * lax.axis_size("rep")
    zero, one = STEPS[step] if step < len(STEPS) else (RC, RC)
    return lax.ppermute(v, AXES, [(j, j ^ (one if j // RC & 1 else zero)) for j in range(count)])


def after(v, earlier):
    return lax.optimization_barrier((v, earlier))[0]


def gather_windows(own):
    next_plane = exchange(own, 3)
    near = [None] * SLOTS
    planes = [own, next_plane, exchange(after(own, next_plane), 2), exchange(next_plane, 2)]
    for m, v in enumerate(planes):
        side = exchange(v, 0)
        near[m], near[8 + m], near[4 + m], near[12 + m] = v, side, exchange(v, 1), exchange(side, 1)
    late = near[8 + 2]
    return near + [exchange(after(v, late) if n % 4 < 2 else v, 4) for n, v in enumerate(near)]


def total(*parts, kind=BF):
    v = parts[0].astype(F32)
    for part in parts[1:]:
        v = v + part.astype(F32)
    return v.astype(kind)


def sum_windows(keep, *sent):
    got = {m: exchange(v, 4) for m, v in zip(PLANES, sent)}
    side, back, last = {}, {}, [None]

    def add(*parts):
        if last[0] is not None:
            parts = (*parts[:-1], after(parts[-1], last[0]))
        last[0] = total(*parts)
        return last[0]

    def single(m):
        far = exchange(add(keep[4 * m + 3], got[m][3]), 0)
        side[m] = (exchange(add(keep[4 * m + 2], got[m][2]), 0), far)

    def pair(m):
        side[m] = exchange(add(keep[4 * m + 2 : 4 * m + 4], got[m][2:]), 0)

    def second(m):
        back[m] = exchange(add(keep[4 * m + 1], got[m][1], side[m][1]), 1)

    def plane(m):
        return (keep[4 * m], got[m][0], side[m][0], back[m])

    single(3)
    single(2)
    second(3)
    second(2)
    pair(1)
    pair(0)
    turn = exchange(add(*plane(3)), 2)
    second(1)
    two = exchange(add(*plane(2)), 2)
    one = exchange(add(*plane(1), turn), 3)
    second(0)
    early = total(*plane(0)[:3], kind=F32)
    return (lax.optimization_barrier(early), back[0], one, two)


def shards_fn(block_input, segment_ids, cotangent, master_weights, momentum, weight_average):
    width = block_input.shape[2]
    length = block_input.shape[1]
    count = lax.axis_size("dp") * lax.axis_size("rep")
    share = master_weights.shape[0]
    rows = share * count // LANES
    tiles = rows // TILE
    args = (block_input[0], cotangent[0], segment_ids)
    if count == 32:
        window = (tiles // count + 2) * TILE
        first = (own_index() * share) % (TILE * LANES)
        padded = jnp.pad(master_weights, (TILE * LANES, window * LANES - share))
        own = lax.dynamic_slice(padded, (TILE * LANES - first,), (window * LANES,)).astype(BF).reshape(window, LANES)
        block_output, input_grad, *sums = core(*args, gather_windows(own), True, count, rows)
        addends = sum_windows(*sums)
        grad = addends[0].astype(F32)
        for addend in addends[1:]:
            grad = grad + addend.astype(F32)
        weight_grad = lax.dynamic_slice(grad.reshape(-1), (first,), (share,))
        vector_grad = grad[window - 1]
    else:
        flat = lax.all_gather(master_weights.astype(BF), AXES, axis=0, tiled=True).reshape(rows, LANES)
        block_output, input_grad, grad = core(*args, [flat], False, count, rows)
        grad = grad.reshape(-1).astype(F32)
        weight_grad = lax.psum_scatter(grad, AXES, scatter_dimension=0, tiled=True)
        vector_grad = lax.psum_scatter(grad[grad.shape[0] - 8 * width :], AXES, scatter_dimension=0, tiled=True)
    token_count = block_input.shape[0] * length * count
    rate = rate_base / math.sqrt(token_count)
    new_momentum = mom_decay * momentum + weight_grad
    new_weights = master_weights - rate * (weight_grad + mom_decay * new_momentum)
    new_average = avg_keep * weight_average + (1.0 - avg_keep) * new_weights
    return (
        block_output[None],
        input_grad[None],
        weight_grad,
        vector_grad,
        new_momentum,
        new_average,
        new_weights,
    )


def solution(mesh):
    three = P(AXES, None, None)
    two = P(AXES, None)
    one = P(AXES)
    return jax.shard_map(
        shards_fn,
        mesh=mesh,
        in_specs=(three, two, three, one, one, one),
        out_specs=(three, three, one, one, one, one, one),
        check_vma=False,
    )
```
